256 devices in a mesh: facet: 32 (over x, z_lo, y), col: 8 (over z_hi, core).
Axes of the slice: x: 4, y: 4, z: 8 (z_hi: 4, z_lo: 2; z = z_hi * 2 + z_lo), core: 2. Of those that a mesh axis runs over, the one named last changes fastest.
Arguments:
- facet_strips: bfloat16 [16384, 2, 1024], P('facet', None, 'col'), may hold values from -6 to 6
- facet_off: int32 [4], replicated, may hold values from 0 to 65535
- strip_off: int32 [8], replicated, may hold values from 0 to 65535
- sub_v: int32 [32], replicated, may hold values from 0 to 65535
- sub_u: int32 [8], replicated, may hold values from 0 to 65535
- screen_phase: float32 [2048, 8192], P('facet', 'col'), may hold values from -3.140625 to 3.140625
- visibilities: bfloat16 [512, 8, 2, 8192], P('facet', None, None, 'col'), may hold values from -6 to 6
- block_band: int32 [512, 8], P('facet', 'col'), may hold values from 0 to 7
- vis_weight: float32 [512, 64], P('facet', 'col'), may hold values from 0.2 to 2
Outputs:
- subgrid_residual: bfloat16 [2048, 2, 8192], P('facet', None, 'col')
- facet_residual: bfloat16 [16384, 2, 1024], P('facet', None, 'col')
The draws below stay inside these ranges and needn't reach their ends.
Inputs may be any that keep to these rules, and one draw needn't show every extreme that they name: `block_band`: each visibility block covers one band of 8 rows of its subgrid's slab.
All inputs are finite; a program needn't handle non-finite values.
Results may differ from the reference program's by a relative error of at most 0.02.
Values may be sent and summed in bfloat16 or wider, within the bound.
A program may use at most 64 MiB of HBM per device.

```python
import math
import jax
import jax.numpy as jnp
from jax import lax

IMG = 65536
SG = 1024
SGR = 64
CR = 64
FW = 128
FH = 4096
PIECES = 8
BR = 8
NB = 16
FACETS = 4
GROUPS = 8
SUBROWS = 32
SUBCOLS = 8
NBANDS = 8


def place_ends(drawn, rng, smallest, largest):
    longest = drawn.shape.index(max(drawn.shape))
    spots = []
    for shift in (0, 1):
        where = [jax.random.randint(jax.random.fold_in(rng, axis), (), 0, length) for axis, length in enumerate(drawn.shape)]
        where[longest] = (where[longest] + shift) % drawn.shape[longest]
        spots.append(tuple(where))
    return drawn.at[spots[0]].set(smallest).at[spots[1]].set(largest)


def level_of(stream_key, shape, split, low, largest):
    def one(dim, blocks):
        draws = jax.random.uniform(jax.random.fold_in(jax.random.fold_in(stream_key, 6), dim), (blocks,), jnp.float32, low / len(split), largest / len(split))
        return jnp.repeat(jnp.exp(draws), shape[dim] // blocks).reshape((-1,) + (1,) * (len(shape) - dim - 1))

    gain = one(*split[0])
    for cut in split[1:]:
        gain = gain * one(*cut)
    return gain


def normal_values(key, dims, scale, limit, cuts=(), held_as=jnp.bfloat16):
    factor_of = level_of(key, dims, cuts, -0.22, 0.18) if cuts else 1.0
    array = jax.random.normal(key, dims, jnp.float32) * scale * factor_of
    return jnp.minimum(jnp.maximum(array, -limit), limit).astype(held_as)


def setup_inputs(seed: int = 0) -> dict:
    arg_keys = jax.random.split(jax.random.key(seed), 10)
    return {
        "facet_strips": normal_values(arg_keys[0], (FACETS * FH, 2, GROUPS * FW), 1.0, 6.0, ((0, 32), (2, 8))),
        "facet_off": place_ends(jax.random.randint(arg_keys[1], (FACETS,), 0, IMG), jax.random.fold_in(arg_keys[1], 1), 0, IMG - 1).astype(jnp.int32),
        "strip_off": place_ends(jax.random.randint(arg_keys[2], (GROUPS,), 0, IMG), jax.random.fold_in(arg_keys[2], 1), 0, IMG - 1).astype(jnp.int32),
        "sub_v": place_ends(jax.random.randint(arg_keys[3], (SUBROWS,), 0, IMG), jax.random.fold_in(arg_keys[3], 1), 0, IMG - 1).astype(jnp.int32),
        "sub_u": place_ends(jax.random.randint(arg_keys[4], (SUBCOLS,), 0, IMG), jax.random.fold_in(arg_keys[4], 1), 0, IMG - 1).astype(jnp.int32),
        "screen_phase": jnp.clip(jax.random.uniform(arg_keys[5], (SUBROWS * SGR, SUBCOLS * SG), jnp.float32, -3.140625, 3.140625), -3.140625, 3.140625),
        "visibilities": normal_values(arg_keys[6], (SUBROWS * NB, BR, 2, SUBCOLS * SG), 1.0, 6.0, ((0, 32), (3, 8))),
        "block_band": place_ends(jax.random.randint(arg_keys[7], (SUBROWS * NB, SUBCOLS), 0, NBANDS), jax.random.fold_in(arg_keys[7], 1), 0, NBANDS - 1).astype(jnp.int32),
        "vis_weight": jnp.clip(jnp.exp(math.log(2.0) - 2.3025851 * jax.random.uniform(arg_keys[8], (SUBROWS * NB, SUBCOLS * BR), jnp.float32) ** level_of(arg_keys[8], (SUBROWS * NB, SUBCOLS * BR), ((0, 32), (1, 8)), -0.2, 0.2)), 0.2, 2.0),
    }


TWO_PI = 2.0 * math.pi

def count_range(total):
    return jnp.arange(total, dtype=jnp.int32)

def modular_product(left, right):
    left = left % IMG
    right = right % IMG
    high = left // 256
    low = left % 256
    return (high * right % IMG * 256 + low * right) % IMG

def phase_pair(left, right, sign):
    angle = modular_product(left, right).astype(jnp.float32) * (TWO_PI / IMG)
    return (jnp.cos(angle), sign * jnp.sin(angle))

def lookup(table, index):
    hits = index[:, None] == count_range(table.shape[0])[None, :]
    return lax.optimization_barrier(jnp.sum(jnp.where(hits, table[None, :], 0), axis=1)).astype(jnp.int32)

def product(left, right):
    return jnp.dot(left, right, preferred_element_type=jnp.float32)

def rounded_table(values):
    narrow = lax.optimization_barrier(values.astype(jnp.bfloat16))
    return narrow.astype(jnp.float32)

def reference(facet_strips, facet_off, strip_off, sub_v, sub_u, screen_phase, visibilities, block_band, vis_weight):
    width_all = GROUPS * FW
    part_rows = FH // PIECES
    strips = facet_strips.reshape(FACETS, FH, 2, width_all)
    rows_iota = count_range(FH)
    strip_scale = 1.0 / math.sqrt(FH)
    gather_scale = 1.0 / math.sqrt(FACETS * CR)
    grid_scale = 1.0 / math.sqrt(GROUPS * FW)
    share_scale = 1.0 / math.sqrt(SUBCOLS * SG)
    return_scale = 1.0 / math.sqrt(SGR)
    facet_scale = 1.0 / math.sqrt(SUBROWS * CR)
    row_step = IMG // FH
    slab_step = IMG // SGR
    grid_step = IMG // SG
    assembly_real_part, assembly_imaginary = phase_pair(count_range(SGR)[None, :, None], (facet_off[:, None] + count_range(CR)[None, :] * slab_step)[:, None, :], 1.0)
    assembly_real_part = assembly_real_part.astype(jnp.bfloat16)
    assembly_imaginary = assembly_imaginary.astype(jnp.bfloat16)

    def facet_tables(offset):
        mod_real, mod_imag = phase_pair(sub_v[:, None], offset + rows_iota[None, :], -1.0)
        table_real, table_imag = phase_pair((count_range(CR) * row_step)[:, None], offset + rows_iota[None, :], -1.0)
        return (mod_real, mod_imag, table_real.astype(jnp.bfloat16), table_imag.astype(jnp.bfloat16))

    def forward_facet(total, inputs):
        strip, offset, own_real, own_imag = inputs
        mod_real, mod_imag, table_real, table_imag = facet_tables(offset)
        strip_real = strip[:, 0].astype(jnp.float32)
        strip_imag = strip[:, 1].astype(jnp.float32)

        def one_row(pair):
            row_real, row_imag = pair
            shifted_real = (row_real[:, None] * strip_real - row_imag[:, None] * strip_imag).astype(jnp.bfloat16)
            shifted_imag = (row_real[:, None] * strip_imag + row_imag[:, None] * strip_real).astype(jnp.bfloat16)
            sum_real = jnp.zeros((SGR, width_all), jnp.float32)
            sum_imag = jnp.zeros((SGR, width_all), jnp.float32)
            for piece in range(PIECES):
                low = piece * part_rows
                high = low + part_rows
                part_real = ((product(table_real[:, low:high], shifted_real[low:high]) - product(table_imag[:, low:high], shifted_imag[low:high])) * strip_scale).astype(jnp.bfloat16)
                part_imag = ((product(table_real[:, low:high], shifted_imag[low:high]) + product(table_imag[:, low:high], shifted_real[low:high])) * strip_scale).astype(jnp.bfloat16)
                sum_real = sum_real + product(own_real, part_real) - product(own_imag, part_imag)
                sum_imag = sum_imag + product(own_real, part_imag) + product(own_imag, part_real)
            return jnp.stack([sum_real, sum_imag], axis=0)
        return (total + lax.map(one_row, (mod_real, mod_imag)), None)
    start = jnp.zeros((SUBROWS, 2, SGR, width_all), jnp.float32)
    total, _ = lax.scan(forward_facet, start, (strips, facet_off, assembly_real_part, assembly_imaginary))
    assembled = (total * gather_scale).astype(jnp.bfloat16)
    assembled_real = assembled[:, 0].astype(jnp.float32)
    assembled_imag = assembled[:, 1].astype(jnp.float32)
    columns = count_range(width_all)
    positions = lookup(strip_off, columns // FW) + columns % FW * grid_step
    phases = screen_phase.reshape(SUBROWS, SGR, SUBCOLS, SG).transpose(2, 0, 1, 3)
    visible = visibilities.reshape(SUBROWS, NB, BR, 2, SUBCOLS, SG).transpose(4, 0, 1, 2, 3, 5)
    bands = block_band.reshape(SUBROWS, NB, SUBCOLS).transpose(2, 0, 1)
    weights = vis_weight.reshape(SUBROWS, NB, SUBCOLS, BR).transpose(2, 0, 1, 3)

    def one_column(inputs):
        offset, phase, vis_column, band_column, weight_column = inputs
        table_real, table_imag = phase_pair((offset + count_range(SG))[:, None], positions[None, :], -1.0)
        table_real = rounded_table(table_real)
        table_imag = rounded_table(table_imag)
        grid_real = (jnp.einsum('ksx,ux->ksu', assembled_real, table_real) - jnp.einsum('ksx,ux->ksu', assembled_imag, table_imag)) * grid_scale
        grid_imag = (jnp.einsum('ksx,ux->ksu', assembled_real, table_imag) + jnp.einsum('ksx,ux->ksu', assembled_imag, table_real)) * grid_scale
        screen_cos = jnp.cos(phase)
        screen_sin = jnp.sin(phase)
        model_real = grid_real * screen_cos - grid_imag * screen_sin
        model_imag = grid_real * screen_sin + grid_imag * screen_cos
        model = jnp.stack([model_real, model_imag], axis=2).reshape(SUBROWS, NBANDS, BR, 2, SG)
        onehot = (band_column[:, :, None] == count_range(NBANDS)[None, None, :]).astype(jnp.float32)
        picked = jnp.einsum('kbn,knrcu->kbrcu', onehot, model, precision=lax.Precision.HIGHEST)
        misfit = weight_column[:, :, :, None, None] * (vis_column.astype(jnp.float32) - picked)
        gridded = jnp.einsum('kbn,kbrcu->knrcu', onehot, misfit, precision=lax.Precision.HIGHEST).reshape(SUBROWS, SGR, 2, SG)
        residual_real = gridded[:, :, 0] * screen_cos + gridded[:, :, 1] * screen_sin
        residual_imag = gridded[:, :, 1] * screen_cos - gridded[:, :, 0] * screen_sin
        return jnp.stack([residual_real, residual_imag], axis=2).astype(jnp.bfloat16)
    residuals = lax.map(one_column, (sub_u, phases, visible, bands, weights))
    subgrid_residual = residuals.transpose(1, 2, 3, 0, 4).reshape(SUBROWS * SGR, 2, SUBCOLS * SG)
    grid_cells = count_range(SUBCOLS * SG)
    frequencies = lookup(sub_u, grid_cells // SG) + grid_cells % SG
    back_real, back_imag = phase_pair(frequencies[:, None], positions[None, :], -1.0)
    back_real = rounded_table(back_real)
    back_imag = rounded_table(back_imag)
    residual_real = subgrid_residual[:, 0].reshape(SUBROWS, SGR, SUBCOLS * SG).astype(jnp.float32)
    residual_imag = subgrid_residual[:, 1].reshape(SUBROWS, SGR, SUBCOLS * SG).astype(jnp.float32)
    share_real = ((jnp.einsum('ksu,ux->ksx', residual_real, back_real) + jnp.einsum('ksu,ux->ksx', residual_imag, back_imag)) * share_scale).astype(jnp.bfloat16)
    share_imag = ((jnp.einsum('ksu,ux->ksx', residual_imag, back_real) - jnp.einsum('ksu,ux->ksx', residual_real, back_imag)) * share_scale).astype(jnp.bfloat16)
    share_real = share_real.astype(jnp.float32)
    share_imag = share_imag.astype(jnp.float32)

    def backward_facet(inputs):
        offset, own_real, own_imag = inputs
        mod_real, mod_imag, table_real, table_imag = facet_tables(offset)
        wide_real = own_real.astype(jnp.float32)
        wide_imag = own_imag.astype(jnp.float32)
        returned_real = ((jnp.einsum('sr,ksx->krx', wide_real, share_real) + jnp.einsum('sr,ksx->krx', wide_imag, share_imag)) * return_scale).astype(jnp.bfloat16)
        returned_imag = ((jnp.einsum('sr,ksx->krx', wide_real, share_imag) - jnp.einsum('sr,ksx->krx', wide_imag, share_real)) * return_scale).astype(jnp.bfloat16)

        def add_row(total, inputs):
            part_real, part_imag, row_real, row_imag = inputs
            prod_real = product(table_real.T, part_real) + product(table_imag.T, part_imag)
            prod_imag = product(table_real.T, part_imag) - product(table_imag.T, part_real)
            out_real = row_real[:, None] * prod_real + row_imag[:, None] * prod_imag
            out_imag = row_real[:, None] * prod_imag - row_imag[:, None] * prod_real
            return (total + jnp.stack([out_real, out_imag], axis=1), None)
        empty = jnp.zeros((FH, 2, width_all), jnp.float32)
        total, _ = lax.scan(add_row, empty, (returned_real, returned_imag, mod_real, mod_imag))
        return (total * facet_scale).astype(jnp.bfloat16)
    facet_parts = lax.map(backward_facet, (facet_off, assembly_real_part, assembly_imaginary))
    facet_residual = facet_parts.reshape(FACETS * FH, 2, width_all)
    return (subgrid_residual, facet_residual)
```

```python
import functools
import math

import jax
import jax.numpy as jnp
from jax import lax
from jax.experimental import pallas as pl
from jax.experimental.pallas import tpu as pltpu
from jax.sharding import PartitionSpec as P

MESH = pl.DeviceIdType.MESH
IMG = 65536
TURN = 2.0 * math.pi / IMG
F32 = jnp.float32
BF16 = jnp.bfloat16

K = 32
C = 8
S = 64
Y = 512
X = 128
U = 1024
PIECES = 8
UB = U // X
BLOCKS = 16


def quarter_turns(q, t):
    t2 = t * t
    sin = t + t * t2 * (-1.6666654611e-1 + t2 * (8.3321608736e-3 + t2 * -1.9515295891e-4))
    cos = 1.0 - 0.5 * t2 + t2 * t2 * (
        4.166664568298827e-2 + t2 * (-1.388731625493765e-3 + t2 * 2.443315711809948e-5)
    )
    odd = (q & 1) == 1
    even_cos = jnp.where(odd, sin, cos)
    even_sin = jnp.where(odd, cos, sin)
    return (
        jnp.where(((q + 1) & 2) != 0, -even_cos, even_cos),
        jnp.where((q & 2) != 0, -even_sin, even_sin),
    )


def unit(k):
    k = k & (IMG - 1)
    q = (k + IMG // 8) >> 14
    return quarter_turns(q, (k - (q << 14)).astype(F32) * TURN)


def cos_sin(angle):
    turns = jnp.floor(angle * (2.0 / math.pi) + 0.5)
    t = (angle - turns * 1.5703125) - turns * 4.837512969970703e-4
    t = t - turns * 7.549789948768648e-8
    return quarter_turns(turns.astype(jnp.int32), t)


def iota(shape, dim):
    return lax.broadcasted_iota(jnp.int32, shape, dim)


def facet_step(me, p):
    x = ((me >> 3) + (p >> 3)) & 3
    z = ((me >> 2) ^ (p >> 2)) & 1
    y = (me + p) & 3
    return (x << 3) | (z << 2) | y


def back_step(p):
    x = (0 - (p >> 3)) & 3
    y = (0 - p) & 3
    return (x << 3) | (p & 4) | y


def col_step(me, q):
    z = ((me >> 1) + (q >> 1)) & 3
    return (z << 1) | ((me ^ q) & 1)


def kernel(
    facet_off,
    strip_off,
    sub_v,
    sub_u,
    strips,
    bands,
    screen_hbm,
    vis_hbm,
    residual,
    image,
    g_tab,
    mod,
    wide,
    m_tab,
    part_out,
    part_in,
    own_part,
    asm,
    w_tab,
    d_tab,
    screen,
    vis,
    base,
    weight,
    share_acc,
    share_out,
    share_in,
    share,
    back,
    back_acc,
    load_sem,
    a_send,
    a_recv,
    c_send,
    c_recv,
    e_send,
    e_recv,
    f_send,
    f_recv,
):
    me = lax.axis_index("facet")
    col = lax.axis_index("col")

    screen_load = pltpu.make_async_copy(screen_hbm, screen, load_sem.at[0])
    vis_load = pltpu.make_async_copy(vis_hbm, vis, load_sem.at[1])
    screen_load.start()
    vis_load.start()

    barrier = pltpu.get_barrier_semaphore()

    def greet_facet(p, carry):
        pl.semaphore_signal(
            barrier, inc=1, device_id=(facet_step(me, p), col), device_id_type=MESH
        )
        return carry

    def greet_col(q, carry):
        pl.semaphore_signal(
            barrier, inc=1, device_id=(me, col_step(col, q)), device_id_type=MESH
        )
        return carry

    lax.fori_loop(1, K, greet_facet, 0)
    lax.fori_loop(1, C, greet_col, 0)

    off = facet_off[me // PIECES]
    first = off + (me % PIECES) * Y

    def g_rows(i, carry):
        row = iota((8, Y), 0) + i * 8
        m = 64 * row - first - iota((8, Y), 1)
        phase_cos, phase_sin = unit(504 * m + row * off)
        top_cos, top_sin = unit(512 * m)
        low_cos, low_sin = unit(8 * m)
        same = (m & 4095) == 0
        ratio = jnp.where(
            same, top_cos * low_cos, top_sin / jnp.where(same, 1.0, 64.0 * low_sin)
        )
        at = pl.ds(pl.multiple_of(i * 8, 8), 8)
        g_tab[at, :Y] = phase_cos * ratio
        g_tab[at, Y:] = phase_sin * ratio
        return carry

    lax.fori_loop(0, S // 8, g_rows, 0)

    def mod_rows(i, carry):
        row = iota((8, Y), 0)
        v = jnp.zeros((8, Y), jnp.int32)
        for r in range(8):
            v = jnp.where(row == r, sub_v[facet_step(me, K - 1 - (i * 8 + r))], v)
        real, imag = unit(0 - v * (first + iota((8, Y), 1)))
        for h in range(2):
            mod[i * 2 + h, :, :Y] = real[h * 4 : h * 4 + 4]
            mod[i * 2 + h, :, Y:] = imag[h * 4 : h * 4 + 4]
        return carry

    lax.fori_loop(0, K // 8, mod_rows, 0)

    wide[:Y, :] = strips[...]
    wide[Y:, :X] = -strips[:, X:]
    wide[Y:, X:] = strips[:, :X]

    def a_copy(t):
        return pltpu.make_async_remote_copy(
            src_ref=part_out.at[t],
            dst_ref=part_in.at[t],
            send_sem=a_send.at[t],
            recv_sem=a_recv.at[t],
            device_id=(facet_step(me, K - 1 - t), col),
            device_id_type=MESH,
        )

    def facet_group(g, carry):
        for i in range(4):
            t = g * 4 + i
            for h in range(4):
                lanes = slice(h * X, (h + 1) * X)
                upper = slice(Y + h * X, Y + (h + 1) * X)
                gr = g_tab[:, lanes]
                gi = g_tab[:, upper]
                mr = mod[g, i : i + 1, lanes]
                mi = mod[g, i : i + 1, upper]
                m_tab[t, :, lanes] = (gr * mr - gi * mi).astype(BF16)
                m_tab[t, :, upper] = (gr * mi + gi * mr).astype(BF16)
        made = jnp.dot(
            m_tab[pl.ds(g * 4, 4)].reshape(4 * S, 2 * Y),
            wide[...],
            preferred_element_type=F32,
        )
        part_out[pl.ds(g * 4, 4)] = made.astype(BF16).reshape(4, S, 2 * X)
        own_part[...] = made[3 * S :, :]

        @pl.when(g == 0)
        def _():
            pl.semaphore_wait(barrier, K - 1 + C - 1)

        for i in range(4):
            t = g * 4 + i

            @pl.when(t < K - 1)
            def _():
                a_copy(t).start()

        return carry

    lax.fori_loop(0, K // 4, facet_group, 0)

    frequency = sub_u[col]

    def w_block(b, carry):
        for h in range(2):
            x = iota((X // 2, X), 0) + h * (X // 2)
            u = iota((X // 2, X), 1) + b * X
            real, imag = unit(0 - 64 * x * (frequency + u))
            top = slice(h * (X // 2), (h + 1) * (X // 2))
            low = slice(X + h * (X // 2), X + (h + 1) * (X // 2))
            w_tab[b, top, :X] = real.astype(BF16)
            w_tab[b, top, X:] = imag.astype(BF16)
            w_tab[b, low, :X] = (-imag).astype(BF16)
            w_tab[b, low, X:] = real.astype(BF16)
        return carry

    lax.fori_loop(0, UB, w_block, 0)

    strip = jnp.zeros((C, X), jnp.int32)
    for c in range(C):
        strip = jnp.where(iota((C, X), 0) == c, strip_off[c], strip)

    def d_block(b, carry):
        real, imag = unit(0 - strip * (frequency + iota((C, X), 1) + b * X))
        d_tab[b, :, :X] = real
        d_tab[b, :, X:] = imag
        return carry

    lax.fori_loop(0, UB, d_block, 0)

    row = iota((S, X), 0)
    lane = iota((S, X), 1)
    covers = (bands[0:1, :] == (row >> 3).astype(F32)) & ((row & 7) == (lane & 7))
    spread = jnp.where(covers, jnp.broadcast_to(bands[1:2, :], (S, X)), 0.0)
    weight[...] = jnp.broadcast_to(jnp.sum(spread, axis=1, keepdims=True), (S, X)) * (1.0 / 32.0)
    high = spread.astype(BF16)
    rest = (spread - high.astype(F32)).astype(BF16)
    both = jnp.concatenate([high, rest], axis=0)
    screen_load.wait()
    vis_load.wait()

    def base_block(b, carry):
        lanes = pl.ds(pl.multiple_of(b * X, X), X)
        upper = pl.ds(pl.multiple_of(U + b * X, X), X)
        real = jnp.dot(both, vis[:, lanes], preferred_element_type=F32)
        imag = jnp.dot(both, vis[:, upper], preferred_element_type=F32)
        real = real[:S] + real[S:]
        imag = imag[:S] + imag[S:]
        cos, sin = cos_sin(screen[:, lanes])
        base[b, :, :X] = real * cos + imag * sin
        base[b, :, X:] = imag * cos - real * sin
        return carry

    lax.fori_loop(0, UB, base_block, 0)

    def a_sum(t, total):
        a_copy(t).wait_recv()
        return total + part_in[t].astype(F32)

    total = lax.fori_loop(0, K - 1, a_sum, own_part[...])
    asm[col] = (total * (1.0 / 16.0)).astype(BF16)

    def c_copy(slot, q):
        return pltpu.make_async_remote_copy(
            src_ref=asm.at[slot],
            dst_ref=asm.at[slot],
            send_sem=c_send.at[q],
            recv_sem=c_recv.at[slot],
            device_id=(me, col_step(col, q)),
            device_id_type=MESH,
        )

    def c_start(q, carry):
        c_copy(col, q).start()
        return carry

    def c_wait(q, carry):
        c_copy(col_step(col, q), q).wait_recv()
        return carry

    lax.fori_loop(1, C, c_start, 0)
    lax.fori_loop(1, C, c_wait, 0)

    share_acc[...] = jnp.zeros_like(share_acc)

    def grid_block(b, carry):
        made = jnp.dot(asm[...].reshape(C * S, 2 * X), w_tab[b], preferred_element_type=F32)
        real = jnp.zeros((S, X), F32)
        imag = jnp.zeros((S, X), F32)
        for c in range(C):
            dr = d_tab[b, c : c + 1, :X]
            di = d_tab[b, c : c + 1, X:]
            pr = made[c * S : (c + 1) * S, :X]
            pi = made[c * S : (c + 1) * S, X:]
            real = real + (pr * dr - pi * di)
            imag = imag + (pr * di + pi * dr)
        real = base[b, :, :X] - weight[...] * real
        imag = base[b, :, X:] - weight[...] * imag
        lanes = pl.ds(pl.multiple_of(b * X, X), X)
        upper = pl.ds(pl.multiple_of(U + b * X, X), X)
        residual[:, lanes] = real.astype(BF16)
        residual[:, upper] = imag.astype(BF16)
        turned = []
        for c in range(C):
            dr = d_tab[b, c : c + 1, :X]
            di = d_tab[b, c : c + 1, X:]
            turned.append(
                jnp.concatenate(
                    [
                        (real * dr + imag * di).astype(BF16),
                        (imag * dr - real * di).astype(BF16),
                    ],
                    axis=1,
                )
            )
        share_acc[...] += lax.dot_general(
            jnp.concatenate(turned, axis=0),
            w_tab[b],
            (((1,), (1,)), ((), ())),
            preferred_element_type=F32,
        )
        return carry

    lax.fori_loop(0, UB, grid_block, 0)
    share_out[...] = share_acc[...].astype(BF16).reshape(C, S, 2 * X)

    def e_copy(slot, q):
        there = col_step(col, q)
        return pltpu.make_async_remote_copy(
            src_ref=share_out.at[there],
            dst_ref=share_in.at[slot],
            send_sem=e_send.at[q],
            recv_sem=e_recv.at[slot],
            device_id=(me, there),
            device_id_type=MESH,
        )

    def e_start(q, carry):
        e_copy(col, q).start()
        return carry

    def e_sum(q, total):
        there = col_step(col, q)
        e_copy(there, q).wait_recv()
        return total + share_in[there].astype(F32)

    lax.fori_loop(1, C, e_start, 0)
    own = share_acc[pl.ds(pl.multiple_of(col * S, S), S), :]
    total = lax.fori_loop(1, C, e_sum, own)
    share[...] = total.astype(BF16)

    def f_copy(t):
        p = K - 1 - t
        slot = K - 1 - back_step(p)
        return pltpu.make_async_remote_copy(
            src_ref=share,
            dst_ref=back.at[slot],
            send_sem=f_send.at[t],
            recv_sem=f_recv.at[slot],
            device_id=(facet_step(me, p), col),
            device_id_type=MESH,
        )

    def f_start(t, carry):
        f_copy(t).start()
        return carry

    lax.fori_loop(0, K - 1, f_start, 0)
    back[K - 1] = share[...]
    back_acc[...] = jnp.zeros_like(back_acc)

    def image_group(g, carry):
        slots = (K - 1 - back_step(K - 1 - g * 4)) // 4
        for i in range(4):
            t = slots * 4 + i

            @pl.when(t < K - 1)
            def _():
                pltpu.make_async_remote_copy(
                    src_ref=share,
                    dst_ref=back.at[t],
                    send_sem=f_send.at[t],
                    recv_sem=f_recv.at[t],
                    device_id=(me, col),
                    device_id_type=MESH,
                ).wait_recv()

        back_acc[...] += lax.dot_general(
            back[pl.ds(slots * 4, 4)].reshape(4 * S, 2 * X),
            m_tab[pl.ds(slots * 4, 4)].reshape(4 * S, 2 * Y),
            (((0,), (0,)), ((), ())),
            preferred_element_type=F32,
        )
        return carry

    lax.fori_loop(0, K // 4, image_group, 0)
    real = back_acc[:X, :Y] + back_acc[X:, Y:]
    imag = back_acc[X:, :Y] - back_acc[:X, Y:]
    image[:, :X] = (real.T * (1.0 / 512.0)).astype(BF16)
    image[:, X:] = (imag.T * (1.0 / 512.0)).astype(BF16)

    def sent(t, carry):
        a_copy(t).wait_send()
        f_copy(t).wait_send()
        return carry

    def sent_col(q, carry):
        c_copy(col, q).wait_send()
        e_copy(col, q).wait_send()
        return carry

    lax.fori_loop(0, K - 1, sent, 0)
    lax.fori_loop(1, C, sent_col, 0)


def shards(
    facet_strips,
    facet_off,
    strip_off,
    sub_v,
    sub_u,
    screen_phase,
    visibilities,
    block_band,
    vis_weight,
):
    bands = jnp.stack(
        [
            jnp.repeat(block_band[:, 0].astype(F32), 8),
            vis_weight.reshape(BLOCKS * 8),
        ]
    )
    smem = pl.BlockSpec(memory_space=pltpu.SMEM)
    vmem = pl.BlockSpec(memory_space=pltpu.VMEM)
    anywhere = pl.BlockSpec(memory_space=pl.ANY)
    dma = pltpu.SemaphoreType.DMA
    residual, image = pl.pallas_call(
        kernel,
        name="imaging_round",
        out_shape=(
            jax.ShapeDtypeStruct((S, 2 * U), BF16),
            jax.ShapeDtypeStruct((Y, 2 * X), BF16),
        ),
        in_specs=[smem] * 4 + [vmem] * 2 + [anywhere] * 2,
        out_specs=(vmem, vmem),
        scratch_shapes=[
            pltpu.VMEM((S, 2 * Y), F32),
            pltpu.VMEM((K // 4, 4, 2 * Y), F32),
            pltpu.VMEM((2 * Y, 2 * X), BF16),
            pltpu.VMEM((K, S, 2 * Y), BF16),
            pltpu.VMEM((K, S, 2 * X), BF16),
            pltpu.VMEM((K, S, 2 * X), BF16),
            pltpu.VMEM((S, 2 * X), F32),
            pltpu.VMEM((C, S, 2 * X), BF16),
            pltpu.VMEM((UB, 2 * X, 2 * X), BF16),
            pltpu.VMEM((UB, C, 2 * X), F32),
            pltpu.VMEM((S, U), F32),
            pltpu.VMEM((BLOCKS * 8, 2 * U), BF16),
            pltpu.VMEM((UB, S, 2 * X), F32),
            pltpu.VMEM((S, X), F32),
            pltpu.VMEM((C * S, 2 * X), F32),
            pltpu.VMEM((C, S, 2 * X), BF16),
            pltpu.VMEM((C, S, 2 * X), BF16),
            pltpu.VMEM((S, 2 * X), BF16),
            pltpu.VMEM((K, S, 2 * X), BF16),
            pltpu.VMEM((2 * X, 2 * Y), F32),
            dma((2,)),
            dma((K,)),
            dma((K,)),
            dma((C,)),
            dma((C,)),
            dma((C,)),
            dma((C,)),
            dma((K,)),
            dma((K,)),
        ],
        compiler_params=pltpu.CompilerParams(
            collective_id=0, has_side_effects=True, vmem_limit_bytes=48 * 1024 * 1024
        ),
    )(
        facet_off,
        strip_off,
        sub_v,
        sub_u,
        facet_strips.reshape(Y, 2 * X),
        bands,
        screen_phase,
        visibilities.reshape(BLOCKS * 8, 2 * U),
    )
    return residual.reshape(S, 2, U), image.reshape(Y, 2, X)


def solution(mesh):
    return jax.shard_map(
        shards,
        mesh=mesh,
        in_specs=(
            P("facet", None, "col"),
            P(),
            P(),
            P(),
            P(),
            P("facet", "col"),
            P("facet", None, None, "col"),
            P("facet", "col"),
            P("facet", "col"),
        ),
        out_specs=(P("facet", None, "col"), P("facet", None, "col")),
        check_vma=False,
    )
```

```python
import math

import jax
import jax.numpy as jnp
from jax import lax
from jax.experimental import pallas as pl
from jax.experimental.pallas import tpu as pltpu
import numpy as np
from jax.sharding import PartitionSpec as P

MESH = pl.DeviceIdType.MESH
IMG = 65536
TURN = 2.0 * math.pi / IMG
F32 = jnp.float32
BF16 = jnp.bfloat16

K = 32
C = 8
S = 64
Y = 512
X = 128
U = 1024
PIECES = 8
UB = U // X
BLOCKS = 16
HALF = 12
TERMS = 2 * HALF
ROWS = 2 * TERMS
PIECE_COLS = PIECES * ROWS


def piece_factors():
    r = np.arange(S) - (S - 1) / 2
    d = np.arange(Y) - (Y - 1) / 2
    angle = 2.0 * np.pi * np.outer(r, d) / (PIECES * Y)
    left = []
    right = []
    for part in (np.cos(angle), np.sin(angle)):
        u, sigma, v = np.linalg.svd(part, full_matrices=False)
        left.append(u[:, :HALF] * sigma[:HALF])
        right.append(v[:HALF])
    q = np.concatenate(left, axis=1) / 1024.0
    b = np.concatenate(right, axis=0)
    return (
        np.tile(q, (1, 2 * PIECES)).astype(np.float32),
        np.repeat(b, 2, axis=1).astype(np.float32),
    )


def quarter_turns(q, t):
    t2 = t * t
    sin = t + t * t2 * (-1.6666654611e-1 + t2 * (8.3321608736e-3 + t2 * -1.9515295891e-4))
    cos = 1.0 - 0.5 * t2 + t2 * t2 * (
        4.166664568298827e-2 + t2 * (-1.388731625493765e-3 + t2 * 2.443315711809948e-5)
    )
    odd = (q & 1) == 1
    even_cos = jnp.where(odd, sin, cos)
    even_sin = jnp.where(odd, cos, sin)
    return (
        jnp.where(((q + 1) & 2) != 0, -even_cos, even_cos),
        jnp.where((q & 2) != 0, -even_sin, even_sin),
    )


def unit(k):
    k = k & (IMG - 1)
    q = (k + IMG // 8) >> 14
    return quarter_turns(q, (k - (q << 14)).astype(F32) * TURN)


def cos_sin(angle):
    turns = jnp.floor(angle * (2.0 / math.pi) + 0.5)
    t = (angle - turns * 1.5703125) - turns * 4.837512969970703e-4
    t = t - turns * 7.549789948768648e-8
    return quarter_turns(turns.astype(jnp.int32), t)


def iota(shape, dim):
    return lax.broadcasted_iota(jnp.int32, shape, dim)


def facet_step(me, p):
    x = ((me >> 3) + (p >> 3)) & 3
    z = ((me >> 2) ^ (p >> 2)) & 1
    y = (me + p) & 3
    return (x << 3) | (z << 2) | y


def back_step(p):
    x = (0 - (p >> 3)) & 3
    y = (0 - p) & 3
    return (x << 3) | (p & 4) | y


def kernel(
    facet_off_hbm,
    strip_off_hbm,
    sub_v_hbm,
    sub_u_hbm,
    strips_hbm,
    b_hbm,
    q_hbm,
    band_hbm,
    weight_hbm,
    screen_hbm,
    vis_hbm,
    residual,
    image,
    facet_off,
    strip_off,
    sub_v,
    sub_u,
    band,
    row_weight,
    strips,
    b_tab,
    q_tab,
    screen,
    vis,
    mod,
    n_tab,
    part_out,
    part_in,
    l_tab,
    lt_tab,
    asm,
    w_tab,
    d_tab,
    base,
    weight,
    rest,
    rest_out,
    share_acc,
    pair_out,
    pair_in,
    share_out,
    share_in,
    back_out,
    back,
    back_acc,
    load_sem,
    vis_sem,
    rest_sem,
    a_send,
    a_recv,
    c_send,
    c_recv,
    pair_send,
    pair_recv,
    e_send,
    e_recv,
    f_send,
    f_recv,
):
    me = lax.axis_index("facet")
    col = lax.axis_index("col")
    z = col >> 1
    core = col & 1
    sibling = 1 - core

    loads = [
        pltpu.make_async_copy(src, dst, load_sem.at[i])
        for i, (src, dst) in enumerate(
            [
                (facet_off_hbm, facet_off),
                (sub_v_hbm, sub_v),
                (b_hbm, b_tab),
                (strips_hbm, strips),
                (strip_off_hbm, strip_off),
                (sub_u_hbm, sub_u),
                (band_hbm, band),
                (weight_hbm, row_weight),
                (q_hbm, q_tab),
                (screen_hbm, screen),
            ]
        )
    ]
    for load in loads:
        load.start()
    barrier = pltpu.get_barrier_semaphore()

    def greet_facet(p, carry):
        pl.semaphore_signal(
            barrier, inc=1, device_id=(facet_step(me, p), col), device_id_type=MESH
        )
        return carry

    lax.fori_loop(1, K, greet_facet, 0)
    for other in [2 * z + sibling] + [2 * ((z + dz) & 3) + core for dz in (1, 2, 3)]:
        pl.semaphore_signal(barrier, inc=1, device_id=(me, other), device_id_type=MESH)

    def vis_load(b):
        lanes = pl.ds(pl.multiple_of(b * X, X), X)
        return pltpu.make_async_copy(vis_hbm.at[:, :, lanes], vis.at[b], vis_sem.at[b])

    def vis_start(b, carry):
        vis_load(b).start()
        return carry

    lax.fori_loop(0, UB, vis_start, 0)

    for load in loads[:4]:
        load.wait()
    first = facet_off[me // PIECES] + (me % PIECES) * Y

    def mod_rows(i, carry):
        row = iota((8, X), 0)
        v = jnp.zeros((8, X), jnp.int32)
        for r in range(8):
            v = jnp.where(row == r, sub_v[i * 8 + r], v)
        for h in range(2 * Y // X):
            lane = iota((8, X), 1) + h * X
            y = lane >> 1
            real, imag = unit(128772 - 504 * y - v * (first + y) + ((lane & 1) << 14))
            for g in range(2):
                mod[i * 2 + g, :, h * X : (h + 1) * X] = real[g * 4 : g * 4 + 4]
                mod[i * 2 + g, :, 2 * Y + h * X : 2 * Y + (h + 1) * X] = imag[g * 4 : g * 4 + 4]
        return carry

    lax.fori_loop(0, K // 8, mod_rows, 0)

    def facet_group(g, carry):
        for h in range(2 * Y // X):
            lanes = slice(h * X, (h + 1) * X)
            upper = slice(2 * Y + h * X, 2 * Y + (h + 1) * X)
            b = b_tab[:, lanes]
            for i in range(4):
                n_tab[g * 4 + i, :, lanes] = jnp.concatenate(
                    [b * mod[g, i : i + 1, lanes], b * mod[g, i : i + 1, upper]], axis=0
                ).astype(BF16)
        made = jnp.dot(
            n_tab[pl.ds(g * 4, 4)].reshape(4 * ROWS, 2 * Y),
            strips[...],
            preferred_element_type=F32,
        )
        part_out[pl.ds(g * 4, 4)] = made.astype(BF16).reshape(4, ROWS, X)
        return carry

    lax.fori_loop(0, K // 4, facet_group, 0)
    pl.semaphore_wait(barrier, K - 1 + 4)

    def a_copy(p):
        there = facet_step(me, p)
        return pltpu.make_async_remote_copy(
            src_ref=part_out.at[there],
            dst_ref=part_in.at[me],
            send_sem=a_send.at[p],
            recv_sem=a_recv.at[me],
            device_id=(there, col),
            device_id_type=MESH,
        )

    def a_arrival(p):
        source = facet_step(me, back_step(p))
        return pltpu.make_async_remote_copy(
            src_ref=part_out.at[source],
            dst_ref=part_in.at[source],
            send_sem=a_send.at[p],
            recv_sem=a_recv.at[source],
            device_id=(source, col),
            device_id_type=MESH,
        )

    def a_start(i, carry):
        a_copy(K - 1 - i).start()
        return carry

    lax.fori_loop(0, K - 1, a_start, 0)
    part_in[me] = part_out[me]

    for load in loads[4:]:
        load.wait()

    l_lane = iota((8, PIECE_COLS), 1)
    piece = jnp.zeros((8, PIECE_COLS), jnp.int32)
    for h in range(1, PIECES):
        piece = piece + (l_lane >= h * ROWS).astype(jnp.int32)
    l_term = l_lane - piece * ROWS
    l_imag = (l_term >= TERMS).astype(jnp.int32)
    l_odd = (l_term - l_imag * TERMS >= HALF).astype(jnp.int32)
    l_quarter = ((l_imag - l_odd) << 14)[0:1]
    l_place = (piece * (16 * Y) + 4088)[0:1]

    def l_facet(f, carry):
        off = facet_off[f]
        r = iota((S, PIECE_COLS), 0)
        real, imag = unit(l_quarter - r * (16 * off + l_place))
        q = q_tab[...]
        right = jnp.concatenate([q * real, q * imag], axis=0)
        row = iota((2 * S, 2 * S), 0)
        lane = iota((2 * S, 2 * S), 1)
        left, _ = unit(
            (row & (S - 1)) * (off + 1024 * (lane & (S - 1))) + (((lane >> 6) - (row >> 6)) << 14)
        )
        made = jnp.dot(left, right, precision=lax.Precision.HIGHEST, preferred_element_type=F32)
        l_tab[:, pl.ds(pl.multiple_of(f * PIECE_COLS, X), PIECE_COLS)] = made.astype(BF16)
        lt_tab[f] = made.T.astype(BF16)
        return carry

    lax.fori_loop(0, 4, l_facet, 0)
    frequency = sub_u[col]

    def w_block(b, carry):
        for h in range(2):
            x = iota((X // 2, X), 0) + h * (X // 2)
            u = iota((X // 2, X), 1) + b * X
            real, imag = unit(0 - 64 * x * (frequency + u))
            top = slice(h * (X // 2), (h + 1) * (X // 2))
            low = slice(X + h * (X // 2), X + (h + 1) * (X // 2))
            w_tab[b, top, :X] = real.astype(BF16)
            w_tab[b, top, X:] = imag.astype(BF16)
            w_tab[b, low, :X] = (-imag).astype(BF16)
            w_tab[b, low, X:] = real.astype(BF16)
        return carry

    lax.fori_loop(0, UB, w_block, 0)

    strip = jnp.zeros((C, X), jnp.int32)
    for c in range(C):
        strip = jnp.where(iota((C, X), 0) == (c & 1) * 4 + (c >> 1), strip_off[c], strip)

    def d_block(b, carry):
        real, imag = unit(0 - strip * (frequency + iota((C, X), 1) + b * X))
        for h in range(2):
            d_tab[h, b, :, :X] = real[h * 4 : h * 4 + 4]
            d_tab[h, b, :, X:] = imag[h * 4 : h * 4 + 4]
        return carry

    lax.fori_loop(0, UB, d_block, 0)

    pair_lane = iota((8, 2 * X), 1) >> 1

    def weight_lane(i, total):
        return jnp.where(pair_lane == i, row_weight[i >> 3, i & 7], total)

    weight_row = lax.fori_loop(0, BLOCKS * 8, weight_lane, jnp.zeros((8, 2 * X), F32))
    band_row = jnp.zeros((8, 2 * X), jnp.int32)
    for b in range(BLOCKS):
        band_row = jnp.where((pair_lane >> 3) == b, band[b, 0], band_row)
    row = iota((2 * S, 2 * X), 0)
    lane = iota((2 * S, 2 * X), 1)
    covers = (
        (band_row[0:1] == ((row & (S - 1)) >> 3))
        & (((lane >> 1) & 7) == (row & 7))
        & ((lane & 1) == (row >> 6))
    )
    spread = jnp.where(covers, jnp.broadcast_to(weight_row[0:1], (2 * S, 2 * X)), 0.0)
    weight[...] = jnp.broadcast_to(jnp.sum(spread[:S], axis=1, keepdims=True), (S, X)) * (
        1.0 / 32.0
    )
    high = spread.astype(BF16)
    both = jnp.concatenate([high, (spread - high.astype(F32)).astype(BF16)], axis=0)

    def base_block(b, carry):
        vis_load(b).wait()
        made = jnp.dot(both, vis.at[b].reshape(2 * X, X)[...], preferred_element_type=F32)
        real = made[:S] + made[2 * S : 3 * S]
        imag = made[S : 2 * S] + made[3 * S :]
        cos, sin = cos_sin(screen[:, pl.ds(pl.multiple_of(b * X, X), X)])
        base[b, :, :X] = real * cos + imag * sin
        base[b, :, X:] = imag * cos - real * sin
        return carry

    lax.fori_loop(0, UB, base_block, 0)

    def a_wait(i, carry):
        a_arrival(K - 1 - i).wait_recv()
        return carry

    lax.fori_loop(0, K - 1, a_wait, 0)
    made = jnp.dot(l_tab[...], part_in[...].reshape(K * ROWS, X), preferred_element_type=F32)
    asm[core * 4 + z] = jnp.concatenate([made[:S], made[S:]], axis=1).astype(BF16)

    def c_copy(slot, send, there):
        return pltpu.make_async_remote_copy(
            src_ref=asm.at[slot],
            dst_ref=asm.at[slot],
            send_sem=c_send.at[send],
            recv_sem=c_recv.at[slot],
            device_id=(me, there),
            device_id_type=MESH,
        )

    c_copies = [
        c_copy(core * 4 + z, dz, 2 * ((z + dz) & 3) + core) for dz in (2, 1, 3)
    ] + [c_copy(core * 4 + z, 0, 2 * z + sibling)]
    for copy in c_copies:
        copy.start()
    for dz in (1, 3, 2):
        slot = core * 4 + ((z - dz) & 3)
        c_copy(slot, dz, 2 * ((z - dz) & 3) + core).wait_recv()
        forward = c_copy(slot, 3 + dz, 2 * z + sibling)
        forward.start()
        c_copies.append(forward)
    for other in range(4):
        c_copy(sibling * 4 + other, 0, 2 * z + sibling).wait_recv()

    row = iota((2 * S, 2 * S), 0)
    lane = iota((2 * S, 2 * S), 1)
    weave = ((row >> 1) == (lane & (S - 1))) & ((row & 1) == (lane >> 6))
    weave = jnp.where(weave, 1.0, 0.0).astype(BF16)

    def rest_store(b):
        lanes = pl.ds(pl.multiple_of(b * X, X), X)
        return pltpu.make_async_copy(rest_out.at[b], residual.at[:, :, lanes], rest_sem.at[b])

    def grid_block(b, carry):
        made = jnp.dot(asm[...].reshape(C * S, 2 * X), w_tab[b], preferred_element_type=F32)
        real = jnp.zeros((S, X), F32)
        imag = jnp.zeros((S, X), F32)
        for c in range(C):
            dr = d_tab[c // 4, b, c % 4 : c % 4 + 1, :X]
            di = d_tab[c // 4, b, c % 4 : c % 4 + 1, X:]
            pr = made[c * S : (c + 1) * S, :X]
            pi = made[c * S : (c + 1) * S, X:]
            real = real + (pr * dr - pi * di)
            imag = imag + (pr * di + pi * dr)
        real = base[b, :, :X] - weight[...] * real
        imag = base[b, :, X:] - weight[...] * imag
        rest[b, :, :X] = real
        rest[b, :, X:] = imag
        woven = jnp.dot(
            weave,
            jnp.concatenate([real, imag], axis=0).astype(BF16),
            preferred_element_type=F32,
        )
        rest_out.at[b].reshape(2 * S, X)[...] = woven.astype(BF16)
        rest_store(b).start()
        return carry

    lax.fori_loop(0, UB, grid_block, 0)

    def share_of(parity):
        share_acc[...] = jnp.zeros_like(share_acc)

        def share_block(b, carry):
            real = rest[b, :, :X]
            imag = rest[b, :, X:]
            turned = []
            for c in range(4):
                dr = d_tab[parity, b, c : c + 1, :X]
                di = d_tab[parity, b, c : c + 1, X:]
                turned.append(
                    jnp.concatenate(
                        [
                            (real * dr + imag * di).astype(BF16),
                            (imag * dr - real * di).astype(BF16),
                        ],
                        axis=1,
                    )
                )
            share_acc[...] += lax.dot_general(
                jnp.concatenate(turned, axis=0),
                w_tab[b],
                (((1,), (1,)), ((), ())),
                preferred_element_type=F32,
            )
            return carry

        lax.fori_loop(0, UB, share_block, 0)

    share_of(sibling)
    pair_out[...] = share_acc[...].astype(BF16).reshape(4, S, 2 * X)
    pair = pltpu.make_async_remote_copy(
        src_ref=pair_out,
        dst_ref=pair_in,
        send_sem=pair_send,
        recv_sem=pair_recv,
        device_id=(me, 2 * z + sibling),
        device_id_type=MESH,
    )
    pair.start()
    share_of(core)
    pair.wait_recv()

    def strip_total(at):
        rows = pl.ds(pl.multiple_of(at * S, S), S)
        return share_acc[rows, :] + pair_in[at].astype(F32)

    def e_copy(there, slot, dz):
        return pltpu.make_async_remote_copy(
            src_ref=share_out.at[there],
            dst_ref=share_in.at[slot],
            send_sem=e_send.at[dz],
            recv_sem=e_recv.at[slot],
            device_id=(me, 2 * there + core),
            device_id_type=MESH,
        )

    for dz in (2, 1, 3):
        there = (z + dz) & 3
        share_out[there] = strip_total(there).astype(BF16)
        e_copy(there, z, dz).start()
    total = strip_total(z)
    for dz in (1, 3, 2):
        there = (z - dz) & 3
        e_copy(there, there, dz).wait_recv()
        total = total + share_in[there].astype(F32)
    share = jnp.concatenate([total[:, :X], total[:, X:]], axis=0).astype(BF16)

    made = jnp.dot(lt_tab[...].reshape(K * ROWS, X), share, preferred_element_type=F32)
    back_out[...] = made.astype(BF16).reshape(K, ROWS, X)

    def f_copy(p):
        there = facet_step(me, p)
        return pltpu.make_async_remote_copy(
            src_ref=back_out.at[there],
            dst_ref=back.at[me],
            send_sem=f_send.at[p],
            recv_sem=f_recv.at[me],
            device_id=(there, col),
            device_id_type=MESH,
        )

    def f_arrival(p):
        source = facet_step(me, back_step(p))
        return pltpu.make_async_remote_copy(
            src_ref=back_out.at[source],
            dst_ref=back.at[source],
            send_sem=f_send.at[p],
            recv_sem=f_recv.at[source],
            device_id=(source, col),
            device_id_type=MESH,
        )

    def f_start(i, carry):
        f_copy(K - 1 - i).start()
        return carry

    lax.fori_loop(0, K - 1, f_start, 0)
    back[me] = back_out[me]
    back_acc[...] = jnp.zeros_like(back_acc)

    def image_group(i, carry):
        dx = 3 - i
        start = (((me >> 3) - dx) & 3) * 8

        def f_wait(j, inner):
            f_arrival(dx * 8 + j).wait_recv()
            return inner

        lax.fori_loop(jnp.where(dx == 0, 1, 0), 8, f_wait, 0)
        back_acc[...] += lax.dot_general(
            back[pl.ds(start, 8)].reshape(8 * ROWS, X),
            n_tab[pl.ds(start, 8)].reshape(8 * ROWS, 2 * Y),
            (((0,), (0,)), ((), ())),
            preferred_element_type=F32,
        )
        return carry

    lax.fori_loop(0, 4, image_group, 0)
    image[...] = (back_acc[...].T * (1.0 / 32.0)).astype(BF16)

    def sent(p, carry):
        a_copy(p).wait_send()
        f_copy(p).wait_send()
        return carry

    lax.fori_loop(1, K, sent, 0)
    for copy in c_copies:
        copy.wait_send()
    pair.wait_send()
    for dz in (2, 1, 3):
        e_copy((z + dz) & 3, z, dz).wait_send()

    def stored(b, carry):
        rest_store(b).wait()
        return carry

    lax.fori_loop(0, UB, stored, 0)


def shards(
    facet_strips,
    facet_off,
    strip_off,
    sub_v,
    sub_u,
    screen_phase,
    visibilities,
    block_band,
    vis_weight,
):
    vmem = pl.BlockSpec(memory_space=pltpu.VMEM)
    anywhere = pl.BlockSpec(memory_space=pl.ANY)
    dma = pltpu.SemaphoreType.DMA
    q, b = piece_factors()
    residual, image = pl.pallas_call(
        kernel,
        name="imaging_round",
        out_shape=(
            jax.ShapeDtypeStruct((S, 2, U), BF16),
            jax.ShapeDtypeStruct((2 * Y, X), BF16),
        ),
        in_specs=[anywhere] * 11,
        out_specs=(anywhere, vmem),
        scratch_shapes=[
            pltpu.SMEM((4,), jnp.int32),
            pltpu.SMEM((C,), jnp.int32),
            pltpu.SMEM((K,), jnp.int32),
            pltpu.SMEM((C,), jnp.int32),
            pltpu.SMEM((BLOCKS, 1), jnp.int32),
            pltpu.SMEM((BLOCKS, 8), F32),
            pltpu.VMEM((2 * Y, X), BF16),
            pltpu.VMEM((TERMS, 2 * Y), F32),
            pltpu.VMEM((S, PIECE_COLS), F32),
            pltpu.VMEM((S, U), F32),
            pltpu.VMEM((UB, BLOCKS * 8, 2, X), BF16),
            pltpu.VMEM((K // 4, 4, 4 * Y), F32),
            pltpu.VMEM((K, ROWS, 2 * Y), BF16),
            pltpu.VMEM((K, ROWS, X), BF16),
            pltpu.VMEM((K, ROWS, X), BF16),
            pltpu.VMEM((2 * S, K * ROWS), BF16),
            pltpu.VMEM((4, PIECE_COLS, 2 * S), BF16),
            pltpu.VMEM((C, S, 2 * X), BF16),
            pltpu.VMEM((UB, 2 * X, 2 * X), BF16),
            pltpu.VMEM((2, UB, 4, 2 * X), F32),
            pltpu.VMEM((UB, S, 2 * X), F32),
            pltpu.VMEM((S, X), F32),
            pltpu.VMEM((UB, S, 2 * X), F32),
            pltpu.VMEM((UB, S, 2, X), BF16),
            pltpu.VMEM((4 * S, 2 * X), F32),
            pltpu.VMEM((4, S, 2 * X), BF16),
            pltpu.VMEM((4, S, 2 * X), BF16),
            pltpu.VMEM((4, S, 2 * X), BF16),
            pltpu.VMEM((4, S, 2 * X), BF16),
            pltpu.VMEM((K, ROWS, X), BF16),
            pltpu.VMEM((K, ROWS, X), BF16),
            pltpu.VMEM((X, 2 * Y), F32),
            dma((10,)),
            dma((UB,)),
            dma((UB,)),
            dma((K,)),
            dma((K,)),
            dma((8,)),
            dma((C,)),
            dma,
            dma,
            dma((4,)),
            dma((4,)),
            dma((K,)),
            dma((K,)),
        ],
        compiler_params=pltpu.CompilerParams(
            collective_id=0, has_side_effects=True, vmem_limit_bytes=48 * 1024 * 1024
        ),
    )(
        facet_off,
        strip_off,
        sub_v,
        sub_u,
        facet_strips.reshape(2 * Y, X),
        jnp.asarray(b),
        jnp.asarray(q),
        block_band,
        vis_weight,
        screen_phase,
        visibilities.reshape(BLOCKS * 8, 2, U),
    )
    return residual, image.reshape(Y, 2, X)


def solution(mesh):
    return jax.shard_map(
        shards,
        mesh=mesh,
        in_specs=(
            P("facet", None, "col"),
            P(),
            P(),
            P(),
            P(),
            P("facet", "col"),
            P("facet", None, None, "col"),
            P("facet", "col"),
            P("facet", "col"),
        ),
        out_specs=(P("facet", None, "col"), P("facet", None, "col")),
        check_vma=False,
    )
```

```python
import math

import jax
import jax.numpy as jnp
from jax import lax
from jax.experimental import pallas as pl
from jax.experimental.pallas import tpu as pltpu
import numpy as np
from jax.sharding import PartitionSpec as P

MESH = pl.DeviceIdType.MESH
IMG = 65536
TURN = 2.0 * math.pi / IMG
F32 = jnp.float32
BF16 = jnp.bfloat16

K = 32
C = 8
S = 64
Y = 512
X = 128
U = 1024
PIECES = 8
UB = U // X
BLOCKS = 16
PLACES = (0, 1, 3, 2)
HALF = 12
TERMS = 2 * HALF
ROWS = 2 * TERMS
PIECE_COLS = PIECES * ROWS


def piece_factors():
    r = np.arange(S) - (S - 1) / 2
    d = np.arange(Y) - (Y - 1) / 2
    angle = 2.0 * np.pi * np.outer(r, d) / (PIECES * Y)
    left = []
    right = []
    for part in (np.cos(angle), np.sin(angle)):
        u, sigma, v = np.linalg.svd(part, full_matrices=False)
        left.append(u[:, :HALF] * sigma[:HALF])
        right.append(v[:HALF])
    q = np.concatenate(left, axis=1) / 1024.0
    b = np.concatenate(right, axis=0)
    return (
        np.tile(q, (1, 2 * PIECES)).astype(np.float32),
        np.repeat(b, 2, axis=1).astype(np.float32),
    )


def quarter_turns(q, t):
    t2 = t * t
    sin = t + t * t2 * (-1.6666654611e-1 + t2 * (8.3321608736e-3 + t2 * -1.9515295891e-4))
    cos = 1.0 - 0.5 * t2 + t2 * t2 * (
        4.166664568298827e-2 + t2 * (-1.388731625493765e-3 + t2 * 2.443315711809948e-5)
    )
    odd = (q & 1) == 1
    even_cos = jnp.where(odd, sin, cos)
    even_sin = jnp.where(odd, cos, sin)
    return (
        jnp.where(((q + 1) & 2) != 0, -even_cos, even_cos),
        jnp.where((q & 2) != 0, -even_sin, even_sin),
    )


def unit(k):
    k = k & (IMG - 1)
    q = (k + IMG // 8) >> 14
    return quarter_turns(q, (k - (q << 14)).astype(F32) * TURN)


def cos_sin(angle):
    turns = jnp.floor(angle * (2.0 / math.pi) + 0.5)
    t = (angle - turns * 1.5703125) - turns * 4.837512969970703e-4
    t = t - turns * 7.549789948768648e-8
    return quarter_turns(turns.astype(jnp.int32), t)


def iota(shape, dim):
    return lax.broadcasted_iota(jnp.int32, shape, dim)


def facet_step(me, p):
    x = ((me >> 3) + (p >> 3)) & 3
    z = ((me >> 2) ^ (p >> 2)) & 1
    y = (me + p) & 3
    return (x << 3) | (z << 2) | y


def back_step(p):
    x = (0 - (p >> 3)) & 3
    y = (0 - p) & 3
    return (x << 3) | (p & 4) | y


def far_first(i):
    a = i >> 3
    b = i & 3
    return ((2 ^ a ^ (a >> 1)) << 3) | (4 - (i & 4)) | (2 ^ b ^ (b >> 1))


def kernel(
    facet_off_hbm,
    strip_off_hbm,
    sub_v_hbm,
    sub_u_hbm,
    strips_hbm,
    b_hbm,
    q_hbm,
    band_hbm,
    weight_hbm,
    screen_hbm,
    vis_hbm,
    residual,
    image,
    facet_off,
    strip_off,
    sub_v,
    sub_u,
    band,
    row_weight,
    strips,
    b_tab,
    q_tab,
    screen,
    vis,
    mod,
    n_tab,
    part_out,
    part_in,
    l_tab,
    lt_tab,
    asm,
    w_tab,
    d_tab,
    base,
    weight,
    rest_out,
    share_acc,
    pair_out,
    pair_in,
    share_out,
    share_in,
    back_out,
    back,
    back_acc,
    load_sem,
    vis_sem,
    rest_sem,
    a_send,
    a_recv,
    c_send,
    c_recv,
    pair_send,
    pair_recv,
    e_send,
    e_recv,
    f_send,
    f_recv,
):
    me = lax.axis_index("facet")
    col = lax.axis_index("col")
    z = col >> 1
    core = col & 1
    sibling = 1 - core

    loads = [
        pltpu.make_async_copy(src, dst, load_sem.at[i])
        for i, (src, dst) in enumerate(
            [
                (facet_off_hbm, facet_off),
                (sub_v_hbm, sub_v),
                (b_hbm, b_tab),
                (strips_hbm, strips),
                (strip_off_hbm, strip_off),
                (sub_u_hbm, sub_u),
                (band_hbm, band),
                (weight_hbm, row_weight),
                (q_hbm, q_tab),
                (screen_hbm, screen),
            ]
        )
    ]
    for load in loads[:4]:
        load.start()
    barrier = pltpu.get_barrier_semaphore()

    def greet_facet(i, carry):
        pl.semaphore_signal(
            barrier, inc=1, device_id=(facet_step(me, far_first(i)), col), device_id_type=MESH
        )
        return carry

    lax.fori_loop(0, K - 1, greet_facet, 0)
    for other in [2 * z + sibling] + [2 * ((z + dz) & 3) + core for dz in (1, 2, 3)]:
        pl.semaphore_signal(barrier, inc=1, device_id=(me, other), device_id_type=MESH)
    for load in loads[4:]:
        load.start()

    def vis_load(b):
        lanes = pl.ds(pl.multiple_of(b * X, X), X)
        return pltpu.make_async_copy(vis_hbm.at[:, :, lanes], vis.at[b], vis_sem.at[b])

    def vis_start(b, carry):
        vis_load(b).start()
        return carry

    lax.fori_loop(0, UB, vis_start, 0)

    for load in loads[:4]:
        load.wait()
    first = facet_off[me // PIECES] + (me % PIECES) * Y

    def mod_rows(i, carry):
        row = iota((8, X), 0)
        v = jnp.zeros((8, X), jnp.int32)
        for r in range(8):
            v = jnp.where(row == r, sub_v[i * 8 + r], v)
        for h in range(2 * Y // X):
            lane = iota((8, X), 1) + h * X
            y = lane >> 1
            real, imag = unit(128772 - 504 * y - v * (first + y) + ((lane & 1) << 14))
            for g in range(2):
                mod[i * 2 + g, :, h * X : (h + 1) * X] = real[g * 4 : g * 4 + 4]
                mod[i * 2 + g, :, 2 * Y + h * X : 2 * Y + (h + 1) * X] = imag[g * 4 : g * 4 + 4]
        return carry

    lax.fori_loop(0, K // 8, mod_rows, 0)

    def facet_group(g, carry):
        for h in range(2 * Y // X):
            lanes = slice(h * X, (h + 1) * X)
            upper = slice(2 * Y + h * X, 2 * Y + (h + 1) * X)
            b = b_tab[:, lanes]
            for i in range(4):
                n_tab[g * 4 + i, :, lanes] = jnp.concatenate(
                    [b * mod[g, i : i + 1, lanes], b * mod[g, i : i + 1, upper]], axis=0
                ).astype(BF16)
        made = jnp.dot(
            n_tab[pl.ds(g * 4, 4)].reshape(4 * ROWS, 2 * Y),
            strips[...],
            preferred_element_type=F32,
        )
        part_out[pl.ds(g * 4, 4)] = made.astype(BF16).reshape(4, ROWS, X)
        return carry

    lax.fori_loop(0, K // 4, facet_group, 0)
    pl.semaphore_wait(barrier, K - 1 + 4)

    def a_copy(p):
        there = facet_step(me, p)
        return pltpu.make_async_remote_copy(
            src_ref=part_out.at[there],
            dst_ref=part_in.at[me],
            send_sem=a_send.at[p],
            recv_sem=a_recv.at[me],
            device_id=(there, col),
            device_id_type=MESH,
        )

    def a_arrival(p):
        source = facet_step(me, back_step(p))
        return pltpu.make_async_remote_copy(
            src_ref=part_out.at[source],
            dst_ref=part_in.at[source],
            send_sem=a_send.at[p],
            recv_sem=a_recv.at[source],
            device_id=(source, col),
            device_id_type=MESH,
        )

    def a_start(i, carry):
        a_copy(far_first(i)).start()
        return carry

    lax.fori_loop(0, K - 1, a_start, 0)
    part_in[me] = part_out[me]

    for load in loads[4:]:
        load.wait()

    l_lane = iota((8, PIECE_COLS), 1)
    piece = jnp.zeros((8, PIECE_COLS), jnp.int32)
    for h in range(1, PIECES):
        piece = piece + (l_lane >= h * ROWS).astype(jnp.int32)
    l_term = l_lane - piece * ROWS
    l_imag = (l_term >= TERMS).astype(jnp.int32)
    l_odd = (l_term - l_imag * TERMS >= HALF).astype(jnp.int32)
    l_quarter = ((l_imag - l_odd) << 14)[0:1]
    l_place = (piece * (16 * Y) + 4088)[0:1]

    def l_facet(f, carry):
        off = facet_off[f]
        r = iota((S, PIECE_COLS), 0)
        real, imag = unit(l_quarter - r * (16 * off + l_place))
        q = q_tab[...]
        right = jnp.concatenate([q * real, q * imag], axis=0)
        row = iota((2 * S, 2 * S), 0)
        lane = iota((2 * S, 2 * S), 1)
        left, _ = unit(
            (row & (S - 1)) * (off + 1024 * (lane & (S - 1))) + (((lane >> 6) - (row >> 6)) << 14)
        )
        made = jnp.dot(left, right, precision=lax.Precision.HIGHEST, preferred_element_type=F32)
        l_tab[:, pl.ds(pl.multiple_of(f * PIECE_COLS, X), PIECE_COLS)] = made.astype(BF16)
        lt_tab[f] = made.T.astype(BF16)
        return carry

    lax.fori_loop(0, 4, l_facet, 0)
    frequency = sub_u[col]

    def w_block(b, carry):
        for h in range(2):
            x = iota((X // 2, X), 0) + h * (X // 2)
            u = iota((X // 2, X), 1) + b * X
            real, imag = unit(0 - 64 * x * (frequency + u))
            top = slice(h * (X // 2), (h + 1) * (X // 2))
            low = slice(X + h * (X // 2), X + (h + 1) * (X // 2))
            w_tab[b, top, :X] = real.astype(BF16)
            w_tab[b, top, X:] = imag.astype(BF16)
            w_tab[b, low, :X] = (-imag).astype(BF16)
            w_tab[b, low, X:] = real.astype(BF16)
        return carry

    lax.fori_loop(0, UB, w_block, 0)

    strip = jnp.zeros((C, X), jnp.int32)
    for at, step in enumerate(PLACES):
        for c in range(2):
            strip = jnp.where(
                iota((C, X), 0) == 2 * at + c, strip_off[2 * ((z + step) & 3) + c], strip
            )

    def d_block(b, carry):
        real, imag = unit(0 - strip * (frequency + iota((C, X), 1) + b * X))
        d_tab[b, :, :X] = real
        d_tab[b, :, X:] = imag
        return carry

    lax.fori_loop(0, UB, d_block, 0)

    pair_lane = iota((8, 2 * X), 1) >> 1

    def weight_lane(i, total):
        return jnp.where(pair_lane == i, row_weight[i & 7, i >> 3], total)

    weight_row = lax.fori_loop(0, BLOCKS * 8, weight_lane, jnp.zeros((8, 2 * X), F32))
    band_row = jnp.zeros((8, 2 * X), jnp.int32)
    for b in range(BLOCKS):
        band_row = jnp.where((pair_lane >> 3) == b, band[0, b], band_row)
    row = iota((2 * S, 2 * X), 0)
    lane = iota((2 * S, 2 * X), 1)
    covers = (
        (band_row[0:1] == ((row & (S - 1)) >> 3))
        & (((lane >> 1) & 7) == (row & 7))
        & ((lane & 1) == (row >> 6))
    )
    spread = jnp.where(covers, jnp.broadcast_to(weight_row[0:1], (2 * S, 2 * X)), 0.0)
    weight[...] = jnp.broadcast_to(jnp.sum(spread[:S], axis=1, keepdims=True), (S, X)) * (
        1.0 / 32.0
    )
    high = spread.astype(BF16)
    both = jnp.concatenate([high, (spread - high.astype(F32)).astype(BF16)], axis=0)

    def base_block(b, carry):
        vis_load(b).wait()
        made = jnp.dot(both, vis.at[b].reshape(2 * X, X)[...], preferred_element_type=F32)
        real = made[:S] + made[2 * S : 3 * S]
        imag = made[S : 2 * S] + made[3 * S :]
        cos, sin = cos_sin(screen[:, pl.ds(pl.multiple_of(b * X, X), X)])
        base[b, :, :X] = real * cos + imag * sin
        base[b, :, X:] = imag * cos - real * sin
        return carry

    lax.fori_loop(0, UB, base_block, 0)

    def a_wait(i, carry):
        a_arrival(far_first(i)).wait_recv()
        return carry

    lax.fori_loop(0, K - 1, a_wait, 0)
    made = jnp.dot(l_tab[...], part_in[...].reshape(K * ROWS, X), preferred_element_type=F32)
    asm[0, core] = jnp.concatenate([made[:S], made[S:]], axis=1).astype(BF16)

    def c_copy(src, dst, half, send, there):
        return pltpu.make_async_remote_copy(
            src_ref=asm.at[src, half],
            dst_ref=asm.at[dst, half],
            send_sem=c_send.at[send],
            recv_sem=c_recv.at[dst, half],
            device_id=(me, there),
            device_id_type=MESH,
        )

    def chip(step):
        return 2 * ((z + step) & 3)

    c_copies = [
        c_copy(0, 3, core, 3, chip(2) + core),
        c_copy(0, 0, core, 0, chip(0) + sibling),
        c_copy(0, 2, core, 2, chip(1) + core),
        c_copy(0, 1, core, 1, chip(3) + core),
    ]
    for copy in c_copies:
        copy.start()

    def hand_on(at):
        c_copy(at, at, core, at, chip(0) + core).wait_recv()
        copy = c_copy(at, at, core, 3 + at, chip(0) + sibling)
        copy.start()
        c_copies.append(copy)

    def grid_part(low, count):
        def grid_block(b, carry):
            made = jnp.dot(
                asm[low : low + count].reshape(count * 2 * S, 2 * X),
                w_tab[b],
                preferred_element_type=F32,
            )
            real = jnp.zeros((S, X), F32)
            imag = jnp.zeros((S, X), F32)
            for c in range(2 * count):
                dr = d_tab[b, 2 * low + c : 2 * low + c + 1, :X]
                di = d_tab[b, 2 * low + c : 2 * low + c + 1, X:]
                pr = made[c * S : (c + 1) * S, :X]
                pi = made[c * S : (c + 1) * S, X:]
                real = real + (pr * dr - pi * di)
                imag = imag + (pr * di + pi * dr)
            base[b, :, :X] -= weight[...] * real
            base[b, :, X:] -= weight[...] * imag
            return carry

        lax.fori_loop(0, UB, grid_block, 0)

    c_copy(0, 0, sibling, 0, chip(0) + sibling).wait_recv()
    grid_part(0, 1)
    hand_on(1)
    hand_on(2)
    c_copy(1, 1, sibling, 1, chip(0) + sibling).wait_recv()
    c_copy(2, 2, sibling, 2, chip(0) + sibling).wait_recv()
    grid_part(1, 2)
    hand_on(3)
    c_copy(3, 3, sibling, 3, chip(0) + sibling).wait_recv()
    grid_part(3, 1)

    def share_part(low, count):
        share_acc[low : low + count] = jnp.zeros((count, 2, S, 2 * X), F32)

        def share_block(b, carry):
            real = base[b, :, :X]
            imag = base[b, :, X:]
            turned = []
            for c in range(2 * low, 2 * (low + count)):
                dr = d_tab[b, c : c + 1, :X]
                di = d_tab[b, c : c + 1, X:]
                turned.append(
                    jnp.concatenate(
                        [
                            (real * dr + imag * di).astype(BF16),
                            (imag * dr - real * di).astype(BF16),
                        ],
                        axis=1,
                    )
                )
            made = lax.dot_general(
                jnp.concatenate(turned, axis=0),
                w_tab[b],
                (((1,), (1,)), ((), ())),
                preferred_element_type=F32,
            )
            share_acc[low : low + count] += made.reshape(count, 2, S, 2 * X)
            return carry

        lax.fori_loop(0, UB, share_block, 0)

    def pair_copy(at):
        return pltpu.make_async_remote_copy(
            src_ref=pair_out.at[at],
            dst_ref=pair_in.at[at],
            send_sem=pair_send.at[at],
            recv_sem=pair_recv.at[at],
            device_id=(me, 2 * z + sibling),
            device_id_type=MESH,
        )

    def pair_start(at):
        pair_out[at] = share_acc[at, sibling].astype(BF16)
        pair_copy(at).start()

    def strip_total(at):
        pair_copy(at).wait_recv()
        return share_acc[at, core] + pair_in[at].astype(F32)

    def e_copy(at):
        return pltpu.make_async_remote_copy(
            src_ref=share_out.at[at],
            dst_ref=share_in.at[PLACES.index((4 - PLACES[at]) % 4)],
            send_sem=e_send.at[at],
            recv_sem=e_recv.at[PLACES.index((4 - PLACES[at]) % 4)],
            device_id=(me, chip(PLACES[at]) + core),
            device_id_type=MESH,
        )

    def e_arrival(at):
        return pltpu.make_async_remote_copy(
            src_ref=share_out.at[at],
            dst_ref=share_in.at[at],
            send_sem=e_send.at[at],
            recv_sem=e_recv.at[at],
            device_id=(me, chip(PLACES[at]) + core),
            device_id_type=MESH,
        )

    def e_start(at):
        share_out[at] = strip_total(at).astype(BF16)
        e_copy(at).start()

    share_part(3, 1)
    pair_start(3)
    share_part(0, 3)
    e_start(3)
    for at in (1, 2, 0):
        pair_start(at)
    e_start(1)
    e_start(2)
    total = strip_total(0)

    row = iota((2 * S, 2 * S), 0)
    lane = iota((2 * S, 2 * S), 1)
    weave = ((row >> 1) == (lane & (S - 1))) & ((row & 1) == (lane >> 6))
    weave = jnp.where(weave, 1.0, 0.0).astype(BF16)

    def rest_store(b):
        lanes = pl.ds(pl.multiple_of(b * X, X), X)
        return pltpu.make_async_copy(rest_out.at[b], residual.at[:, :, lanes], rest_sem.at[b])

    def rest_block(b, carry):
        woven = jnp.dot(
            weave,
            jnp.concatenate([base[b, :, :X], base[b, :, X:]], axis=0).astype(BF16),
            preferred_element_type=F32,
        )
        rest_out.at[b].reshape(2 * S, X)[...] = woven.astype(BF16)
        rest_store(b).start()
        return carry

    lax.fori_loop(0, UB, rest_block, 0)
    for at in (1, 2, 3):
        e_arrival(at).wait_recv()
        total = total + share_in[at].astype(F32)
    share = jnp.concatenate([total[:, :X], total[:, X:]], axis=0).astype(BF16)

    def f_copy(p):
        there = facet_step(me, p)
        return pltpu.make_async_remote_copy(
            src_ref=back_out.at[there],
            dst_ref=back.at[me],
            send_sem=f_send.at[p],
            recv_sem=f_recv.at[me],
            device_id=(there, col),
            device_id_type=MESH,
        )

    def f_arrival(p):
        source = facet_step(me, back_step(p))
        return pltpu.make_async_remote_copy(
            src_ref=back_out.at[source],
            dst_ref=back.at[source],
            send_sem=f_send.at[p],
            recv_sem=f_recv.at[source],
            device_id=(source, col),
            device_id_type=MESH,
        )

    def back_group(a, carry):
        facet = ((me >> 3) + (far_first(a * 8) >> 3)) & 3
        made = jnp.dot(lt_tab[facet], share, preferred_element_type=F32)
        back_out[pl.ds(facet * 8, 8)] = made.astype(BF16).reshape(8, ROWS, X)

        def f_start(i, inner):
            f_copy(far_first(a * 8 + i)).start()
            return inner

        lax.fori_loop(0, jnp.where(a == 3, 7, 8), f_start, 0)
        return carry

    lax.fori_loop(0, 4, back_group, 0)
    back[me] = back_out[me]
    back_acc[...] = jnp.zeros_like(back_acc)

    def image_group(i, carry):
        start = (((me >> 3) - (far_first(i * 8) >> 3)) & 3) * 8

        def f_wait(j, inner):
            f_arrival(far_first(i * 8 + j)).wait_recv()
            return inner

        lax.fori_loop(0, jnp.where(i == 3, 7, 8), f_wait, 0)
        back_acc[...] += lax.dot_general(
            back[pl.ds(start, 8)].reshape(8 * ROWS, X),
            n_tab[pl.ds(start, 8)].reshape(8 * ROWS, 2 * Y),
            (((0,), (0,)), ((), ())),
            preferred_element_type=F32,
        )
        return carry

    lax.fori_loop(0, 4, image_group, 0)
    image[...] = (back_acc[...].T * (1.0 / 32.0)).astype(BF16)

    def sent(p, carry):
        a_copy(p).wait_send()
        f_copy(p).wait_send()
        return carry

    lax.fori_loop(1, K, sent, 0)
    for copy in c_copies:
        copy.wait_send()
    for at in range(4):
        pair_copy(at).wait_send()
    for at in (1, 2, 3):
        e_copy(at).wait_send()

    def stored(b, carry):
        rest_store(b).wait()
        return carry

    lax.fori_loop(0, UB, stored, 0)


def shards(
    facet_strips,
    facet_off,
    strip_off,
    sub_v,
    sub_u,
    screen_phase,
    visibilities,
    block_band,
    vis_weight,
):
    vmem = pl.BlockSpec(memory_space=pltpu.VMEM)
    anywhere = pl.BlockSpec(memory_space=pl.ANY)
    dma = pltpu.SemaphoreType.DMA
    q, b = piece_factors()
    residual, image = pl.pallas_call(
        kernel,
        name="imaging_round",
        out_shape=(
            jax.ShapeDtypeStruct((S, 2, U), BF16),
            jax.ShapeDtypeStruct((2 * Y, X), BF16),
        ),
        in_specs=[pl.BlockSpec(memory_space=pltpu.HBM)] * 11,
        out_specs=(anywhere, vmem),
        scratch_shapes=[
            pltpu.SMEM((4,), jnp.int32),
            pltpu.SMEM((C,), jnp.int32),
            pltpu.SMEM((K,), jnp.int32),
            pltpu.SMEM((C,), jnp.int32),
            pltpu.SMEM((1, BLOCKS), jnp.int32),
            pltpu.SMEM((8, BLOCKS), F32),
            pltpu.VMEM((2 * Y, X), BF16),
            pltpu.VMEM((TERMS, 2 * Y), F32),
            pltpu.VMEM((S, PIECE_COLS), F32),
            pltpu.VMEM((S, U), F32),
            pltpu.VMEM((UB, BLOCKS * 8, 2, X), BF16),
            pltpu.VMEM((K // 4, 4, 4 * Y), F32),
            pltpu.VMEM((K, ROWS, 2 * Y), BF16),
            pltpu.VMEM((K, ROWS, X), BF16),
            pltpu.VMEM((K, ROWS, X), BF16),
            pltpu.VMEM((2 * S, K * ROWS), BF16),
            pltpu.VMEM((4, PIECE_COLS, 2 * S), BF16),
            pltpu.VMEM((4, 2, S, 2 * X), BF16),
            pltpu.VMEM((UB, 2 * X, 2 * X), BF16),
            pltpu.VMEM((UB, C, 2 * X), F32),
            pltpu.VMEM((UB, S, 2 * X), F32),
            pltpu.VMEM((S, X), F32),
            pltpu.VMEM((UB, S, 2, X), BF16),
            pltpu.VMEM((4, 2, S, 2 * X), F32),
            pltpu.VMEM((4, S, 2 * X), BF16),
            pltpu.VMEM((4, S, 2 * X), BF16),
            pltpu.VMEM((4, S, 2 * X), BF16),
            pltpu.VMEM((4, S, 2 * X), BF16),
            pltpu.VMEM((K, ROWS, X), BF16),
            pltpu.VMEM((K, ROWS, X), BF16),
            pltpu.VMEM((X, 2 * Y), F32),
            dma((10,)),
            dma((UB,)),
            dma((UB,)),
            dma((K,)),
            dma((K,)),
            dma((7,)),
            dma((4, 2)),
            dma((4,)),
            dma((4,)),
            dma((4,)),
            dma((4,)),
            dma((K,)),
            dma((K,)),
        ],
        compiler_params=pltpu.CompilerParams(
            collective_id=0, has_side_effects=True, vmem_limit_bytes=60 * 1024 * 1024
        ),
    )(
        facet_off,
        strip_off,
        sub_v,
        sub_u,
        facet_strips.reshape(2 * Y, X),
        jnp.asarray(b),
        jnp.asarray(q),
        block_band.T,
        vis_weight.T,
        screen_phase,
        visibilities.reshape(BLOCKS * 8, 2, U),
    )
    return residual, image.reshape(Y, 2, X)


def solution(mesh):
    return jax.shard_map(
        shards,
        mesh=mesh,
        in_specs=(
            P("facet", None, "col"),
            P(),
            P(),
            P(),
            P(),
            P("facet", "col"),
            P("facet", None, None, "col"),
            P("facet", "col"),
            P("facet", "col"),
        ),
        out_specs=(P("facet", None, "col"), P("facet", None, "col")),
        check_vma=False,
    )
```

```python
import math

import jax
import jax.numpy as jnp
from jax import lax
from jax.experimental import pallas as pl
from jax.experimental.pallas import tpu as pltpu
import numpy as np
from jax.sharding import PartitionSpec as P

MESH = pl.DeviceIdType.MESH
IMG = 65536
TURN = 2.0 * math.pi / IMG
F32 = jnp.float32
BF16 = jnp.bfloat16

K = 32
C = 8
S = 64
Y = 512
X = 128
U = 1024
PIECES = 8
UB = U // X
BLOCKS = 16
PLACES = (0, 1, 3, 2)
HALF = 10
TERMS = 2 * HALF
SENT = 2 * TERMS
ROWS = 48
PIECE_COLS = PIECES * ROWS


def piece_factors():
    r = np.arange(S) - (S - 1) / 2
    d = np.arange(Y) - (Y - 1) / 2
    angle = 2.0 * np.pi * np.outer(r, d) / (PIECES * Y)
    left = []
    right = []
    for part in (np.cos(angle), np.sin(angle)):
        u, sigma, v = np.linalg.svd(part, full_matrices=False)
        left.append(u[:, :HALF] * sigma[:HALF])
        right.append(v[:HALF])
    q = np.concatenate(left, axis=1) / 1024.0
    b = np.concatenate(right, axis=0)
    q = np.pad(np.tile(q, (1, 2)), ((0, 0), (0, ROWS - SENT)))
    b = np.tile(np.repeat(b, 2, axis=1), (2, 1))
    return np.tile(q, (1, PIECES)).astype(np.float32), b.astype(np.float32)


def quarter_turns(q, t):
    t2 = t * t
    sin = t + t * t2 * (-1.6666654611e-1 + t2 * (8.3321608736e-3 + t2 * -1.9515295891e-4))
    cos = 1.0 - 0.5 * t2 + t2 * t2 * (
        4.166664568298827e-2 + t2 * (-1.388731625493765e-3 + t2 * 2.443315711809948e-5)
    )
    odd = (q & 1) == 1
    even_cos = jnp.where(odd, sin, cos)
    even_sin = jnp.where(odd, cos, sin)
    return (
        jnp.where(((q + 1) & 2) != 0, -even_cos, even_cos),
        jnp.where((q & 2) != 0, -even_sin, even_sin),
    )


def unit(k):
    k = k & (IMG - 1)
    q = (k + IMG // 8) >> 14
    return quarter_turns(q, (k - (q << 14)).astype(F32) * TURN)


def cos_sin(angle):
    turns = jnp.floor(angle * (2.0 / math.pi) + 0.5)
    t = (angle - turns * 1.5703125) - turns * 4.837512969970703e-4
    t = t - turns * 7.549789948768648e-8
    return quarter_turns(turns.astype(jnp.int32), t)


def iota(shape, dim):
    return lax.broadcasted_iota(jnp.int32, shape, dim)


def facet_step(me, p):
    x = ((me >> 3) + (p >> 3)) & 3
    z = ((me >> 2) ^ (p >> 2)) & 1
    y = (me + p) & 3
    return (x << 3) | (z << 2) | y


def back_step(p):
    x = (0 - (p >> 3)) & 3
    y = (0 - p) & 3
    return (x << 3) | (p & 4) | y


def far_first(i):
    a = i >> 3
    b = i & 3
    return ((2 ^ a ^ (a >> 1)) << 3) | (4 - (i & 4)) | (2 ^ b ^ (b >> 1))


def kernel(
    facet_off_hbm,
    strip_off_hbm,
    sub_v_hbm,
    sub_u_hbm,
    strips_hbm,
    b_hbm,
    q_hbm,
    band_hbm,
    weight_hbm,
    screen_hbm,
    vis_hbm,
    residual,
    image,
    facet_off,
    strip_off,
    sub_v,
    sub_u,
    band,
    row_weight,
    strips,
    b_tab,
    q_tab,
    screen,
    vis,
    mod,
    n_tab,
    part_out,
    part_in,
    l_tab,
    lt_tab,
    asm,
    w_tab,
    d_tab,
    base,
    weight,
    rest_out,
    share_acc,
    pair_out,
    pair_in,
    share_out,
    share_in,
    back_out,
    back,
    back_acc,
    load_sem,
    vis_sem,
    rest_sem,
    a_send,
    a_recv,
    c_send,
    c_recv,
    pair_send,
    pair_recv,
    e_send,
    e_recv,
    f_send,
    f_recv,
):
    me = lax.axis_index("facet")
    col = lax.axis_index("col")
    z = col >> 1
    core = col & 1
    sibling = 1 - core

    loads = [
        pltpu.make_async_copy(src, dst, load_sem.at[i])
        for i, (src, dst) in enumerate(
            [
                (facet_off_hbm, facet_off),
                (sub_v_hbm, sub_v),
                (b_hbm, b_tab),
                (strips_hbm, strips),
                (strip_off_hbm, strip_off),
                (sub_u_hbm, sub_u),
                (band_hbm, band),
                (weight_hbm, row_weight),
                (q_hbm, q_tab),
                (screen_hbm, screen),
            ]
        )
    ]
    for load in loads[:4]:
        load.start()
    pad = slice(32, ROWS)
    part_in[:, pad] = jnp.zeros((K, ROWS - 32, X), BF16)
    back[:, pad] = jnp.zeros((K, ROWS - 32, X), BF16)
    barrier = pltpu.get_barrier_semaphore()

    def greet_facet(i, carry):
        pl.semaphore_signal(
            barrier, inc=1, device_id=(facet_step(me, far_first(i)), col), device_id_type=MESH
        )
        return carry

    lax.fori_loop(0, K - 1, greet_facet, 0)
    for step in (2, 1, 3, 0):
        for half in (0, 1)[step == 0 :]:
            pl.semaphore_signal(
                barrier,
                inc=1,
                device_id=(me, 2 * ((z + step) & 3) + (core ^ half)),
                device_id_type=MESH,
            )
    for load in loads[4:]:
        load.start()

    def vis_load(b):
        lanes = pl.ds(pl.multiple_of(b * X, X), X)
        return pltpu.make_async_copy(vis_hbm.at[:, :, lanes], vis.at[b], vis_sem.at[b])

    def vis_start(b, carry):
        vis_load(b).start()
        return carry

    lax.fori_loop(0, UB, vis_start, 0)

    for load in loads[:4]:
        load.wait()
    first = facet_off[me // PIECES] + (me % PIECES) * Y

    def mod_rows(i, carry):
        row = iota((8, X), 0)
        v = jnp.zeros((8, X), jnp.int32)
        for r in range(8):
            v = jnp.where(row == r, sub_v[i * 8 + r], v)
        for h in range(2 * Y // X):
            lane = iota((8, X), 1) + h * X
            y = lane >> 1
            real, imag = unit(128772 - 504 * y - v * (first + y) + ((lane & 1) << 14))
            for g in range(2):
                mod[i * 2 + g, :, h * X : (h + 1) * X] = real[g * 4 : g * 4 + 4]
                mod[i * 2 + g, :, 2 * Y + h * X : 2 * Y + (h + 1) * X] = imag[g * 4 : g * 4 + 4]
        return carry

    lax.fori_loop(0, K // 8, mod_rows, 0)

    is_real = iota((SENT, X), 0) < TERMS
    padding = jnp.zeros((ROWS - SENT, X), F32)

    def facet_group(g, carry):
        for h in range(2 * Y // X):
            lanes = slice(h * X, (h + 1) * X)
            upper = slice(2 * Y + h * X, 2 * Y + (h + 1) * X)
            b = b_tab[:, lanes]
            for i in range(4):
                turn = jnp.where(is_real, mod[g, i : i + 1, lanes], mod[g, i : i + 1, upper])
                n_tab[g * 4 + i, :, lanes] = jnp.concatenate([b * turn, padding], axis=0).astype(BF16)
        made = jnp.dot(
            n_tab[pl.ds(g * 4, 4)].reshape(4 * ROWS, 2 * Y),
            strips[...],
            preferred_element_type=F32,
        )
        part_out[pl.ds(g * 4, 4)] = made.astype(BF16).reshape(4, ROWS, X)
        return carry

    lax.fori_loop(0, K // 4, facet_group, 0, unroll=2)
    pl.semaphore_wait(barrier, K - 1 + C - 1)

    def a_copy(p):
        there = facet_step(me, p)
        return pltpu.make_async_remote_copy(
            src_ref=part_out.at[there, :SENT],
            dst_ref=part_in.at[me, :SENT],
            send_sem=a_send.at[p],
            recv_sem=a_recv.at[me],
            device_id=(there, col),
            device_id_type=MESH,
        )

    def a_arrival(p):
        source = facet_step(me, back_step(p))
        return pltpu.make_async_remote_copy(
            src_ref=part_out.at[source, :SENT],
            dst_ref=part_in.at[source, :SENT],
            send_sem=a_send.at[p],
            recv_sem=a_recv.at[source],
            device_id=(source, col),
            device_id_type=MESH,
        )

    def a_start(i, carry):
        a_copy(far_first(i)).start()
        return carry

    lax.fori_loop(0, K - 1, a_start, 0)
    part_in[me] = part_out[me]

    for load in loads[8:]:
        load.wait()

    l_lane = iota((8, PIECE_COLS), 1)
    piece = jnp.zeros((8, PIECE_COLS), jnp.int32)
    for h in range(1, PIECES):
        piece = piece + (l_lane >= h * ROWS).astype(jnp.int32)
    l_term = l_lane - piece * ROWS
    l_imag = (l_term >= TERMS).astype(jnp.int32)
    l_odd = (l_term - l_imag * TERMS >= HALF).astype(jnp.int32)
    l_quarter = ((l_imag - l_odd) << 14)[0:1]
    l_place = (piece * (16 * Y) + 4088)[0:1]

    def l_facet(f, carry):
        off = facet_off[f]
        r = iota((S, PIECE_COLS), 0)
        real, imag = unit(l_quarter - r * (16 * off + l_place))
        q = q_tab[...]
        right = jnp.concatenate([q * real, q * imag], axis=0)
        row = iota((2 * S, 2 * S), 0)
        lane = iota((2 * S, 2 * S), 1)
        left, _ = unit(
            (row & (S - 1)) * (off + 1024 * (lane & (S - 1))) + (((lane >> 6) - (row >> 6)) << 14)
        )
        made = jnp.dot(left, right, precision=lax.Precision.HIGHEST, preferred_element_type=F32)
        l_tab[:, pl.ds(pl.multiple_of(f * PIECE_COLS, X), PIECE_COLS)] = made.astype(BF16)
        return carry

    lax.fori_loop(0, 4, l_facet, 0)
    def a_wait(i, carry):
        a_arrival(far_first(i)).wait_recv()
        return carry

    lax.fori_loop(0, K - 1, a_wait, 0)
    made = jnp.dot(l_tab[...], part_in[...].reshape(K * ROWS, X), preferred_element_type=F32)
    asm[0, 0] = jnp.concatenate([made[:S], made[S:]], axis=1).astype(BF16)

    def c_copy(src, dst, half, send, there):
        return pltpu.make_async_remote_copy(
            src_ref=asm.at[src, 0],
            dst_ref=asm.at[dst, half],
            send_sem=c_send.at[send],
            recv_sem=c_recv.at[dst, half],
            device_id=(me, there),
            device_id_type=MESH,
        )

    def chip(step):
        return 2 * ((z + step) & 3)

    c_copies = [
        c_copy(0, 3, 0, 6, chip(2) + core),
        c_copy(0, 3, 1, 7, chip(2) + sibling),
        c_copy(0, 0, 1, 0, chip(0) + sibling),
        c_copy(0, 2, 0, 2, chip(1) + core),
        c_copy(0, 1, 0, 3, chip(3) + core),
        c_copy(0, 2, 1, 4, chip(1) + sibling),
        c_copy(0, 1, 1, 5, chip(3) + sibling),
    ]
    for copy in c_copies:
        copy.start()

    for load in loads[4:8]:
        load.wait()
    frequency = sub_u[col]

    def w_block(b, carry):
        for h in range(2):
            x = iota((X // 2, X), 0) + h * (X // 2)
            u = iota((X // 2, X), 1) + b * X
            real, imag = unit(0 - 64 * x * (frequency + u))
            top = slice(h * (X // 2), (h + 1) * (X // 2))
            low = slice(X + h * (X // 2), X + (h + 1) * (X // 2))
            w_tab[b, top, :X] = real.astype(BF16)
            w_tab[b, top, X:] = imag.astype(BF16)
            w_tab[b, low, :X] = (-imag).astype(BF16)
            w_tab[b, low, X:] = real.astype(BF16)
        return carry

    lax.fori_loop(0, UB, w_block, 0)

    strip = jnp.zeros((C, X), jnp.int32)
    for at, step in enumerate(PLACES):
        for c in range(2):
            strip = jnp.where(
                iota((C, X), 0) == 2 * at + c, strip_off[2 * ((z + step) & 3) + (core ^ c)], strip
            )

    def d_block(b, carry):
        real, imag = unit(0 - strip * (frequency + iota((C, X), 1) + b * X))
        d_tab[b, :, :X] = real
        d_tab[b, :, X:] = imag
        return carry

    lax.fori_loop(0, UB, d_block, 0)

    pair_lane = iota((8, 2 * X), 1) >> 1

    def weight_lane(i, total):
        return jnp.where(pair_lane == i, row_weight[i & 7, i >> 3], total)

    weight_row = lax.fori_loop(0, BLOCKS * 8, weight_lane, jnp.zeros((8, 2 * X), F32))
    band_row = jnp.zeros((8, 2 * X), jnp.int32)
    for b in range(BLOCKS):
        band_row = jnp.where((pair_lane >> 3) == b, band[0, b], band_row)
    row = iota((2 * S, 2 * X), 0)
    lane = iota((2 * S, 2 * X), 1)
    covers = (
        (band_row[0:1] == ((row & (S - 1)) >> 3))
        & (((lane >> 1) & 7) == (row & 7))
        & ((lane & 1) == (row >> 6))
    )
    spread = jnp.where(covers, jnp.broadcast_to(weight_row[0:1], (2 * S, 2 * X)), 0.0)
    weight[...] = jnp.broadcast_to(jnp.sum(spread[:S], axis=1, keepdims=True), (S, X)) * (
        1.0 / 32.0
    )
    high = spread.astype(BF16)
    both = jnp.concatenate([high, (spread - high.astype(F32)).astype(BF16)], axis=0)

    def base_block(b, carry):
        vis_load(b).wait()
        made = jnp.dot(both, vis.at[b].reshape(2 * X, X)[...], preferred_element_type=F32)
        real = made[:S] + made[2 * S : 3 * S]
        imag = made[S : 2 * S] + made[3 * S :]
        cos, sin = cos_sin(screen[:, pl.ds(pl.multiple_of(b * X, X), X)])
        base[b, :, :X] = real * cos + imag * sin
        base[b, :, X:] = imag * cos - real * sin
        return carry

    lax.fori_loop(0, UB, base_block, 0)

    def c_wait(at, half):
        c_copy(at, at, half, 0, chip(0) + sibling).wait_recv()

    def grid_part(low, count):
        def grid_block(b, carry):
            made = jnp.dot(
                asm[low : low + count].reshape(count * 2 * S, 2 * X),
                w_tab[b],
                preferred_element_type=F32,
            )
            real = jnp.zeros((S, X), F32)
            imag = jnp.zeros((S, X), F32)
            for c in range(2 * count):
                dr = d_tab[b, 2 * low + c : 2 * low + c + 1, :X]
                di = d_tab[b, 2 * low + c : 2 * low + c + 1, X:]
                pr = made[c * S : (c + 1) * S, :X]
                pi = made[c * S : (c + 1) * S, X:]
                real = real + (pr * dr - pi * di)
                imag = imag + (pr * di + pi * dr)
            base[b, :, :X] -= weight[...] * real
            base[b, :, X:] -= weight[...] * imag
            return carry

        lax.fori_loop(0, UB, grid_block, 0, unroll=4)

    for at in range(4):
        if at:
            c_wait(at, 0)
        c_wait(at, 1)
    grid_part(0, 4)

    def share_part(low, high):
        rows = slice(low * S, high * S)
        share_acc[rows, :] = jnp.zeros(((high - low) * S, 2 * X), F32)

        def share_block(b, carry):
            real = base[b, :, :X]
            imag = base[b, :, X:]
            turned = []
            for c in range(low, high):
                dr = d_tab[b, c : c + 1, :X]
                di = d_tab[b, c : c + 1, X:]
                turned.append(
                    jnp.concatenate(
                        [
                            (real * dr + imag * di).astype(BF16),
                            (imag * dr - real * di).astype(BF16),
                        ],
                        axis=1,
                    )
                )
            share_acc[rows, :] += lax.dot_general(
                jnp.concatenate(turned, axis=0),
                w_tab[b],
                (((1,), (1,)), ((), ())),
                preferred_element_type=F32,
            )
            return carry

        lax.fori_loop(0, UB, share_block, 0, unroll=4)

    def pair_copy(at):
        return pltpu.make_async_remote_copy(
            src_ref=pair_out.at[at],
            dst_ref=pair_in.at[at],
            send_sem=pair_send.at[at],
            recv_sem=pair_recv.at[at],
            device_id=(me, 2 * z + sibling),
            device_id_type=MESH,
        )

    def pair_start(at):
        pair_out[at] = share_acc[(2 * at + 1) * S : (2 * at + 2) * S, :].astype(BF16)
        pair_copy(at).start()

    def strip_total(at):
        pair_copy(at).wait_recv()
        return share_acc[2 * at * S : (2 * at + 1) * S, :] + pair_in[at].astype(F32)

    def e_copy(at):
        return pltpu.make_async_remote_copy(
            src_ref=share_out.at[at],
            dst_ref=share_in.at[PLACES.index((4 - PLACES[at]) % 4)],
            send_sem=e_send.at[at],
            recv_sem=e_recv.at[PLACES.index((4 - PLACES[at]) % 4)],
            device_id=(me, chip(PLACES[at]) + core),
            device_id_type=MESH,
        )

    def e_arrival(at):
        return pltpu.make_async_remote_copy(
            src_ref=share_out.at[at],
            dst_ref=share_in.at[at],
            send_sem=e_send.at[at],
            recv_sem=e_recv.at[at],
            device_id=(me, chip(PLACES[at]) + core),
            device_id_type=MESH,
        )

    def e_start(at):
        share_out[at] = strip_total(at).astype(BF16)
        e_copy(at).start()

    share_part(7, 8)
    pair_start(3)
    share_part(2, 7)
    pair_start(1)
    pair_start(2)
    e_start(3)
    share_part(0, 2)
    pair_start(0)
    e_start(1)
    e_start(2)
    total = strip_total(0)

    row = iota((2 * S, 2 * S), 0)
    lane = iota((2 * S, 2 * S), 1)
    weave = ((row >> 1) == (lane & (S - 1))) & ((row & 1) == (lane >> 6))
    weave = jnp.where(weave, 1.0, 0.0).astype(BF16)

    def rest_store(b):
        lanes = pl.ds(pl.multiple_of(b * X, X), X)
        return pltpu.make_async_copy(rest_out.at[b], residual.at[:, :, lanes], rest_sem.at[b])

    def rest_block(b, carry):
        woven = jnp.dot(
            weave,
            jnp.concatenate([base[b, :, :X], base[b, :, X:]], axis=0).astype(BF16),
            preferred_element_type=F32,
        )
        rest_out.at[b].reshape(2 * S, X)[...] = woven.astype(BF16)
        rest_store(b).start()
        return carry

    lax.fori_loop(0, UB, rest_block, 0, unroll=4)

    def turn_table(f, carry):
        lt_tab[f] = l_tab[:, pl.ds(pl.multiple_of(f * PIECE_COLS, X), PIECE_COLS)].T
        return carry

    lax.fori_loop(0, 4, turn_table, 0)
    for at in (1, 2, 3):
        e_arrival(at).wait_recv()
        total = total + share_in[at].astype(F32)
    share = jnp.concatenate([total[:, :X], total[:, X:]], axis=0).astype(BF16)

    def f_copy(p):
        there = facet_step(me, p)
        return pltpu.make_async_remote_copy(
            src_ref=back_out.at[there, :SENT],
            dst_ref=back.at[me, :SENT],
            send_sem=f_send.at[p],
            recv_sem=f_recv.at[me],
            device_id=(there, col),
            device_id_type=MESH,
        )

    def f_arrival(p):
        source = facet_step(me, back_step(p))
        return pltpu.make_async_remote_copy(
            src_ref=back_out.at[source, :SENT],
            dst_ref=back.at[source, :SENT],
            send_sem=f_send.at[p],
            recv_sem=f_recv.at[source],
            device_id=(source, col),
            device_id_type=MESH,
        )

    def back_group(a, carry):
        facet = ((me >> 3) + (far_first(a * 8) >> 3)) & 3
        made = jnp.dot(lt_tab[facet], share, preferred_element_type=F32)
        back_out[pl.ds(facet * 8, 8)] = made.astype(BF16).reshape(8, ROWS, X)

        def f_start(i, inner):
            f_copy(far_first(a * 8 + i)).start()
            return inner

        lax.fori_loop(0, jnp.where(a == 3, 7, 8), f_start, 0)
        return carry

    lax.fori_loop(0, 4, back_group, 0)
    back[me] = back_out[me]
    back_acc[...] = jnp.zeros_like(back_acc)

    def image_group(i, carry):
        start = (((me >> 3) - (far_first(i * 8) >> 3)) & 3) * 8

        def f_wait(j, inner):
            f_arrival(far_first(i * 8 + j)).wait_recv()
            return inner

        lax.fori_loop(0, jnp.where(i == 3, 7, 8), f_wait, 0)
        back_acc[...] += lax.dot_general(
            back[pl.ds(start, 8)].reshape(8 * ROWS, X),
            n_tab[pl.ds(start, 8)].reshape(8 * ROWS, 2 * Y),
            (((0,), (0,)), ((), ())),
            preferred_element_type=F32,
        )
        return carry

    lax.fori_loop(0, 4, image_group, 0)
    image[...] = (back_acc[...].T * (1.0 / 32.0)).astype(BF16)

    def sent(p, carry):
        a_copy(p).wait_send()
        f_copy(p).wait_send()
        return carry

    lax.fori_loop(1, K, sent, 0)
    for copy in c_copies:
        copy.wait_send()
    for at in range(4):
        pair_copy(at).wait_send()
    for at in (1, 2, 3):
        e_copy(at).wait_send()

    def stored(b, carry):
        rest_store(b).wait()
        return carry

    lax.fori_loop(0, UB, stored, 0)


def store(residual, image, residual_out, image_out, sem):
    copies = [
        pltpu.make_async_copy(residual, residual_out, sem.at[0]),
        pltpu.make_async_copy(image, image_out, sem.at[1]),
    ]
    for copy in copies:
        copy.start()
    for copy in copies:
        copy.wait()


def shards(
    facet_strips,
    facet_off,
    strip_off,
    sub_v,
    sub_u,
    screen_phase,
    visibilities,
    block_band,
    vis_weight,
):
    vmem = pl.BlockSpec(memory_space=pltpu.VMEM)
    anywhere = pl.BlockSpec(memory_space=pl.ANY)
    dma = pltpu.SemaphoreType.DMA
    q, b = piece_factors()
    residual, image = pl.pallas_call(
        kernel,
        name="imaging_round",
        out_shape=(
            jax.ShapeDtypeStruct((S, 2, U), BF16),
            jax.ShapeDtypeStruct((2 * Y, X), BF16),
        ),
        in_specs=[pl.BlockSpec(memory_space=pltpu.HBM)] * 11,
        out_specs=(anywhere, vmem),
        scratch_shapes=[
            pltpu.SMEM((4,), jnp.int32),
            pltpu.SMEM((C,), jnp.int32),
            pltpu.SMEM((K,), jnp.int32),
            pltpu.SMEM((C,), jnp.int32),
            pltpu.SMEM((1, BLOCKS), jnp.int32),
            pltpu.SMEM((8, BLOCKS), F32),
            pltpu.VMEM((2 * Y, X), BF16),
            pltpu.VMEM((SENT, 2 * Y), F32),
            pltpu.VMEM((S, PIECE_COLS), F32),
            pltpu.VMEM((S, U), F32),
            pltpu.VMEM((UB, BLOCKS * 8, 2, X), BF16),
            pltpu.VMEM((K // 4, 4, 4 * Y), F32),
            pltpu.VMEM((K, ROWS, 2 * Y), BF16),
            pltpu.VMEM((K, ROWS, X), BF16),
            pltpu.VMEM((K, ROWS, X), BF16),
            pltpu.VMEM((2 * S, K * ROWS), BF16),
            pltpu.VMEM((4, PIECE_COLS, 2 * S), BF16),
            pltpu.VMEM((4, 2, S, 2 * X), BF16),
            pltpu.VMEM((UB, 2 * X, 2 * X), BF16),
            pltpu.VMEM((UB, C, 2 * X), F32),
            pltpu.VMEM((UB, S, 2 * X), F32),
            pltpu.VMEM((S, X), F32),
            pltpu.VMEM((UB, S, 2, X), BF16),
            pltpu.VMEM((C * S, 2 * X), F32),
            pltpu.VMEM((4, S, 2 * X), BF16),
            pltpu.VMEM((4, S, 2 * X), BF16),
            pltpu.VMEM((4, S, 2 * X), BF16),
            pltpu.VMEM((4, S, 2 * X), BF16),
            pltpu.VMEM((K, ROWS, X), BF16),
            pltpu.VMEM((K, ROWS, X), BF16),
            pltpu.VMEM((X, 2 * Y), F32),
            dma((10,)),
            dma((UB,)),
            dma((UB,)),
            dma((K,)),
            dma((K,)),
            dma((8,)),
            dma((4, 2)),
            dma((4,)),
            dma((4,)),
            dma((4,)),
            dma((4,)),
            dma((K,)),
            dma((K,)),
        ],
        compiler_params=pltpu.CompilerParams(
            collective_id=0, has_side_effects=True, vmem_limit_bytes=48 * 1024 * 1024
        ),
    )(
        *(
            pltpu.with_memory_space_constraint(array, pltpu.HBM)
            for array in (
                facet_off,
                strip_off,
                sub_v,
                sub_u,
                facet_strips.reshape(2 * Y, X),
                jnp.asarray(b),
                jnp.asarray(q),
                block_band.T,
                vis_weight.T,
                screen_phase,
                visibilities.reshape(BLOCKS * 8, 2, U),
            )
        )
    )
    hbm = pl.BlockSpec(memory_space=pltpu.HBM)
    residual, image = pl.pallas_call(
        store,
        name="store",
        out_shape=(
            jax.ShapeDtypeStruct((S, 2, U), BF16),
            jax.ShapeDtypeStruct((2 * Y, X), BF16),
        ),
        in_specs=[anywhere, anywhere],
        out_specs=(hbm, hbm),
        scratch_shapes=[dma((2,))],
    )(
        pltpu.with_memory_space_constraint(residual, pltpu.VMEM),
        pltpu.with_memory_space_constraint(image, pltpu.VMEM),
    )
    return residual, image.reshape(Y, 2, X)


def solution(mesh):
    return jax.shard_map(
        shards,
        mesh=mesh,
        in_specs=(
            P("facet", None, "col"),
            P(),
            P(),
            P(),
            P(),
            P("facet", "col"),
            P("facet", None, None, "col"),
            P("facet", "col"),
            P("facet", "col"),
        ),
        out_specs=(P("facet", None, "col"), P("facet", None, "col")),
        check_vma=False,
    )
```

```python
import math

import jax
import jax.numpy as jnp
from jax import lax
from jax.experimental import pallas as pl
from jax.experimental.pallas import tpu as pltpu
import numpy as np
from jax.sharding import PartitionSpec as P

MESH = pl.DeviceIdType.MESH
IMG = 65536
TURN = 2.0 * math.pi / IMG
F32 = jnp.float32
BF16 = jnp.bfloat16

K = 32
C = 8
S = 64
Y = 512
X = 128
U = 1024
PIECES = 8
UB = U // X
BLOCKS = 16
PLACES = (0, 1, 3, 2)
HALF = 10
TERMS = 2 * HALF
SENT = 2 * TERMS
ROWS = 48
PIECE_COLS = PIECES * ROWS


def piece_factors():
    r = np.arange(S) - (S - 1) / 2
    d = np.arange(Y) - (Y - 1) / 2
    angle = 2.0 * np.pi * np.outer(r, d) / (PIECES * Y)
    left = []
    right = []
    for part in (np.cos(angle), np.sin(angle)):
        u, sigma, v = np.linalg.svd(part, full_matrices=False)
        left.append(u[:, :HALF] * sigma[:HALF])
        right.append(v[:HALF])
    q = np.concatenate(left, axis=1) / 1024.0
    b = np.concatenate(right, axis=0)
    q = np.pad(np.tile(q, (1, 2)), ((0, 0), (0, ROWS - SENT)))
    b = np.tile(np.repeat(b, 2, axis=1), (2, 1))
    return np.tile(q, (1, PIECES)).astype(np.float32), b.astype(np.float32)


def quarter_turns(q, t):
    t2 = t * t
    sin = t + t * t2 * (-1.6666654611e-1 + t2 * (8.3321608736e-3 + t2 * -1.9515295891e-4))
    cos = 1.0 - 0.5 * t2 + t2 * t2 * (
        4.166664568298827e-2 + t2 * (-1.388731625493765e-3 + t2 * 2.443315711809948e-5)
    )
    odd = (q & 1) == 1
    even_cos = jnp.where(odd, sin, cos)
    even_sin = jnp.where(odd, cos, sin)
    return (
        jnp.where(((q + 1) & 2) != 0, -even_cos, even_cos),
        jnp.where((q & 2) != 0, -even_sin, even_sin),
    )


def unit(k):
    k = k & (IMG - 1)
    q = (k + IMG // 8) >> 14
    return quarter_turns(q, (k - (q << 14)).astype(F32) * TURN)


def cos_sin(angle):
    turns = jnp.floor(angle * (2.0 / math.pi) + 0.5)
    t = (angle - turns * 1.5703125) - turns * 4.837512969970703e-4
    t = t - turns * 7.549789948768648e-8
    return quarter_turns(turns.astype(jnp.int32), t)


def iota(shape, dim):
    return lax.broadcasted_iota(jnp.int32, shape, dim)


def facet_step(me, p):
    x = ((me >> 3) + (p >> 3)) & 3
    z = ((me >> 2) ^ (p >> 2)) & 1
    y = (me + p) & 3
    return (x << 3) | (z << 2) | y


def back_step(p):
    x = (0 - (p >> 3)) & 3
    y = (0 - p) & 3
    return (x << 3) | (p & 4) | y


def far_first(i):
    a = i >> 3
    b = i & 3
    return ((2 ^ a ^ (a >> 1)) << 3) | (4 - (i & 4)) | (2 ^ b ^ (b >> 1))


def kernel(
    facet_off_hbm,
    strip_off_hbm,
    sub_v_hbm,
    sub_u_hbm,
    strips_hbm,
    b_hbm,
    q_hbm,
    band_hbm,
    weight_hbm,
    screen_hbm,
    vis_hbm,
    residual,
    image,
    facet_off,
    strip_off,
    sub_v,
    sub_u,
    band,
    row_weight,
    strips,
    b_tab,
    q_tab,
    screen,
    vis,
    mod,
    n_tab,
    part_out,
    part_in,
    l_tab,
    lt_tab,
    asm,
    w_tab,
    d_tab,
    base,
    weight,
    rest_out,
    share_acc,
    pair_out,
    pair_in,
    share_out,
    share_in,
    back_out,
    back,
    back_acc,
    load_sem,
    vis_sem,
    rest_sem,
    a_send,
    a_recv,
    c_send,
    c_recv,
    pair_send,
    pair_recv,
    e_send,
    e_recv,
    f_send,
    f_recv,
):
    me = lax.axis_index("facet")
    col = lax.axis_index("col")
    z = col >> 1
    core = col & 1
    sibling = 1 - core

    loads = [
        pltpu.make_async_copy(src, dst, load_sem.at[i])
        for i, (src, dst) in enumerate(
            [
                (facet_off_hbm, facet_off),
                (sub_v_hbm, sub_v),
                (b_hbm, b_tab),
                (strips_hbm, strips),
                (strip_off_hbm, strip_off),
                (sub_u_hbm, sub_u),
                (band_hbm, band),
                (weight_hbm, row_weight),
                (q_hbm, q_tab),
                (screen_hbm, screen),
            ]
        )
    ]
    for load in loads[:4]:
        load.start()
    pad = slice(32, ROWS)
    part_in[:, pad] = jnp.zeros((K, ROWS - 32, X), BF16)
    back[:, pad] = jnp.zeros((K, ROWS - 32, X), BF16)
    barrier = pltpu.get_barrier_semaphore()

    def greet_facet(i, carry):
        pl.semaphore_signal(
            barrier, inc=1, device_id=(facet_step(me, far_first(i)), col), device_id_type=MESH
        )
        return carry

    lax.fori_loop(0, K - 1, greet_facet, 0)
    for step in (2, 1, 3, 0):
        for half in (0, 1)[step == 0 :]:
            pl.semaphore_signal(
                barrier,
                inc=1,
                device_id=(me, 2 * ((z + step) & 3) + (core ^ half)),
                device_id_type=MESH,
            )
    for load in loads[4:]:
        load.start()

    def vis_load(b):
        lanes = pl.ds(pl.multiple_of(b * X, X), X)
        return pltpu.make_async_copy(vis_hbm.at[:, :, lanes], vis.at[b], vis_sem.at[b])

    def vis_start(b, carry):
        vis_load(b).start()
        return carry

    lax.fori_loop(0, UB, vis_start, 0)

    for load in loads[:4]:
        load.wait()
    first = facet_off[me // PIECES] + (me % PIECES) * Y

    def mod_rows(i, carry):
        row = iota((8, X), 0)
        v = jnp.zeros((8, X), jnp.int32)
        for r in range(8):
            v = jnp.where(row == r, sub_v[i * 8 + r], v)
        for h in range(2 * Y // X):
            lane = iota((8, X), 1) + h * X
            y = lane >> 1
            real, imag = unit(128772 - 504 * y - v * (first + y) + ((lane & 1) << 14))
            for g in range(2):
                mod[i * 2 + g, :, h * X : (h + 1) * X] = real[g * 4 : g * 4 + 4]
                mod[i * 2 + g, :, 2 * Y + h * X : 2 * Y + (h + 1) * X] = imag[g * 4 : g * 4 + 4]
        return carry

    lax.fori_loop(0, K // 8, mod_rows, 0, unroll=2)

    is_real = iota((SENT, X), 0) < TERMS
    padding = jnp.zeros((ROWS - SENT, X), F32)

    def facet_group(g, carry):
        for h in range(2 * Y // X):
            lanes = slice(h * X, (h + 1) * X)
            upper = slice(2 * Y + h * X, 2 * Y + (h + 1) * X)
            b = b_tab[:, lanes]
            for i in range(4):
                turn = jnp.where(is_real, mod[g, i : i + 1, lanes], mod[g, i : i + 1, upper])
                n_tab[g * 4 + i, :, lanes] = jnp.concatenate([b * turn, padding], axis=0).astype(BF16)
        made = jnp.dot(
            n_tab[pl.ds(g * 4, 4)].reshape(4 * ROWS, 2 * Y),
            strips[...],
            preferred_element_type=F32,
        )
        part_out[pl.ds(g * 4, 4)] = made.astype(BF16).reshape(4, ROWS, X)
        return carry

    lax.fori_loop(0, K // 4, facet_group, 0, unroll=4)
    pl.semaphore_wait(barrier, K - 1 + C - 1)

    def a_copy(p):
        there = facet_step(me, p)
        return pltpu.make_async_remote_copy(
            src_ref=part_out.at[there, :SENT],
            dst_ref=part_in.at[me, :SENT],
            send_sem=a_send.at[p],
            recv_sem=a_recv.at[me],
            device_id=(there, col),
            device_id_type=MESH,
        )

    def a_arrival(p):
        source = facet_step(me, back_step(p))
        return pltpu.make_async_remote_copy(
            src_ref=part_out.at[source, :SENT],
            dst_ref=part_in.at[source, :SENT],
            send_sem=a_send.at[p],
            recv_sem=a_recv.at[source],
            device_id=(source, col),
            device_id_type=MESH,
        )

    def a_start(i, carry):
        a_copy(far_first(i)).start()
        return carry

    lax.fori_loop(0, K - 1, a_start, 0)
    part_in[me] = part_out[me]

    for load in loads[8:]:
        load.wait()

    l_lane = iota((8, PIECE_COLS), 1)
    piece = jnp.zeros((8, PIECE_COLS), jnp.int32)
    for h in range(1, PIECES):
        piece = piece + (l_lane >= h * ROWS).astype(jnp.int32)
    l_term = l_lane - piece * ROWS
    l_imag = (l_term >= TERMS).astype(jnp.int32)
    l_odd = (l_term - l_imag * TERMS >= HALF).astype(jnp.int32)
    l_quarter = ((l_imag - l_odd) << 14)[0:1]
    l_place = (piece * (16 * Y) + 4088)[0:1]

    def l_facet(f, carry):
        off = facet_off[f]
        r = iota((S, PIECE_COLS), 0)
        real, imag = unit(l_quarter - r * (16 * off + l_place))
        q = q_tab[...]
        right = jnp.concatenate([q * real, q * imag], axis=0)
        row = iota((2 * S, 2 * S), 0)
        lane = iota((2 * S, 2 * S), 1)
        left, _ = unit(
            (row & (S - 1)) * (off + 1024 * (lane & (S - 1))) + (((lane >> 6) - (row >> 6)) << 14)
        )
        made = jnp.dot(left, right, precision=lax.Precision.HIGHEST, preferred_element_type=F32)
        l_tab[:, pl.ds(pl.multiple_of(f * PIECE_COLS, X), PIECE_COLS)] = made.astype(BF16)
        return carry

    lax.fori_loop(0, 4, l_facet, 0)
    def a_wait(i, carry):
        a_arrival(far_first(i)).wait_recv()
        return carry

    lax.fori_loop(0, K - 1, a_wait, 0)
    made = jnp.dot(l_tab[...], part_in[...].reshape(K * ROWS, X), preferred_element_type=F32)
    asm[0, 0] = jnp.concatenate([made[:S], made[S:]], axis=1).astype(BF16)

    def c_copy(src, dst, half, send, there):
        return pltpu.make_async_remote_copy(
            src_ref=asm.at[src, 0],
            dst_ref=asm.at[dst, half],
            send_sem=c_send.at[send],
            recv_sem=c_recv.at[dst, half],
            device_id=(me, there),
            device_id_type=MESH,
        )

    def chip(step):
        return 2 * ((z + step) & 3)

    c_copies = [
        c_copy(0, 3, 0, 6, chip(2) + core),
        c_copy(0, 3, 1, 7, chip(2) + sibling),
        c_copy(0, 0, 1, 0, chip(0) + sibling),
        c_copy(0, 2, 0, 2, chip(1) + core),
        c_copy(0, 1, 0, 3, chip(3) + core),
    ]
    for copy in c_copies:
        copy.start()

    for load in loads[4:8]:
        load.wait()
    frequency = sub_u[col]

    def w_block(b, carry):
        for h in range(2):
            x = iota((X // 2, X), 0) + h * (X // 2)
            u = iota((X // 2, X), 1) + b * X
            real, imag = unit(0 - 64 * x * (frequency + u))
            top = slice(h * (X // 2), (h + 1) * (X // 2))
            low = slice(X + h * (X // 2), X + (h + 1) * (X // 2))
            w_tab[b, top, :X] = real.astype(BF16)
            w_tab[b, top, X:] = imag.astype(BF16)
            w_tab[b, low, :X] = (-imag).astype(BF16)
            w_tab[b, low, X:] = real.astype(BF16)
        return carry

    lax.fori_loop(0, UB, w_block, 0)

    strip = jnp.zeros((C, X), jnp.int32)
    for at, step in enumerate(PLACES):
        for c in range(2):
            strip = jnp.where(
                iota((C, X), 0) == 2 * at + c, strip_off[2 * ((z + step) & 3) + (core ^ c)], strip
            )

    def d_block(b, carry):
        real, imag = unit(0 - strip * (frequency + iota((C, X), 1) + b * X))
        d_tab[b, :, :X] = real
        d_tab[b, :, X:] = imag
        return carry

    lax.fori_loop(0, UB, d_block, 0)

    pair_lane = iota((8, 2 * X), 1) >> 1

    def weight_lane(i, total):
        return jnp.where(pair_lane == i, row_weight[i & 7, i >> 3], total)

    weight_row = lax.fori_loop(0, BLOCKS * 8, weight_lane, jnp.zeros((8, 2 * X), F32))
    band_row = jnp.zeros((8, 2 * X), jnp.int32)
    for b in range(BLOCKS):
        band_row = jnp.where((pair_lane >> 3) == b, band[0, b], band_row)
    row = iota((2 * S, 2 * X), 0)
    lane = iota((2 * S, 2 * X), 1)
    covers = (
        (band_row[0:1] == ((row & (S - 1)) >> 3))
        & (((lane >> 1) & 7) == (row & 7))
        & ((lane & 1) == (row >> 6))
    )
    spread = jnp.where(covers, jnp.broadcast_to(weight_row[0:1], (2 * S, 2 * X)), 0.0)
    weight[...] = jnp.broadcast_to(jnp.sum(spread[:S], axis=1, keepdims=True), (S, X)) * (
        1.0 / 32.0
    )
    high = spread.astype(BF16)
    both = jnp.concatenate([high, (spread - high.astype(F32)).astype(BF16)], axis=0)

    def base_block(b, carry):
        vis_load(b).wait()
        made = jnp.dot(both, vis.at[b].reshape(2 * X, X)[...], preferred_element_type=F32)
        real = made[:S] + made[2 * S : 3 * S]
        imag = made[S : 2 * S] + made[3 * S :]
        cos, sin = cos_sin(screen[:, pl.ds(pl.multiple_of(b * X, X), X)])
        base[b, :, :X] = real * cos + imag * sin
        base[b, :, X:] = imag * cos - real * sin
        return carry

    lax.fori_loop(0, UB, base_block, 0)

    def c_wait(at, half):
        c_copy(at, at, half, 0, chip(0) + sibling).wait_recv()

    def grid_part(low, count):
        def grid_block(b, carry):
            made = jnp.dot(
                asm[low : low + count].reshape(count * 2 * S, 2 * X),
                w_tab[b],
                preferred_element_type=F32,
            )
            real = jnp.zeros((S, X), F32)
            imag = jnp.zeros((S, X), F32)
            for c in range(2 * count):
                dr = d_tab[b, 2 * low + c : 2 * low + c + 1, :X]
                di = d_tab[b, 2 * low + c : 2 * low + c + 1, X:]
                pr = made[c * S : (c + 1) * S, :X]
                pi = made[c * S : (c + 1) * S, X:]
                real = real + (pr * dr - pi * di)
                imag = imag + (pr * di + pi * dr)
            base[b, :, :X] -= weight[...] * real
            base[b, :, X:] -= weight[...] * imag
            return carry

        lax.fori_loop(0, UB, grid_block, 0, unroll=4)

    c_wait(0, 1)
    grid_part(0, 1)
    for at in (1, 2):
        c_wait(at, 0)
        forward = c_copy(at, at, 1, 3 + at, chip(0) + sibling)
        forward.start()
        c_copies.append(forward)
    c_wait(1, 1)
    c_wait(2, 1)
    grid_part(1, 2)
    c_wait(3, 0)
    c_wait(3, 1)
    grid_part(3, 1)

    def share_part(low, high):
        rows = slice(low * S, high * S)
        share_acc[rows, :] = jnp.zeros(((high - low) * S, 2 * X), F32)

        def share_block(b, carry):
            real = base[b, :, :X]
            imag = base[b, :, X:]
            turned = []
            for c in range(low, high):
                dr = d_tab[b, c : c + 1, :X]
                di = d_tab[b, c : c + 1, X:]
                turned.append(
                    jnp.concatenate(
                        [
                            (real * dr + imag * di).astype(BF16),
                            (imag * dr - real * di).astype(BF16),
                        ],
                        axis=1,
                    )
                )
            share_acc[rows, :] += lax.dot_general(
                jnp.concatenate(turned, axis=0),
                w_tab[b],
                (((1,), (1,)), ((), ())),
                preferred_element_type=F32,
            )
            return carry

        lax.fori_loop(0, UB, share_block, 0, unroll=4)

    def pair_copy(at):
        return pltpu.make_async_remote_copy(
            src_ref=pair_out.at[at],
            dst_ref=pair_in.at[at],
            send_sem=pair_send.at[at],
            recv_sem=pair_recv.at[at],
            device_id=(me, 2 * z + sibling),
            device_id_type=MESH,
        )

    def pair_start(at):
        pair_out[at] = share_acc[(2 * at + 1) * S : (2 * at + 2) * S, :].astype(BF16)
        pair_copy(at).start()

    def strip_total(at):
        pair_copy(at).wait_recv()
        return share_acc[2 * at * S : (2 * at + 1) * S, :] + pair_in[at].astype(F32)

    def e_copy(at):
        return pltpu.make_async_remote_copy(
            src_ref=share_out.at[at],
            dst_ref=share_in.at[PLACES.index((4 - PLACES[at]) % 4)],
            send_sem=e_send.at[at],
            recv_sem=e_recv.at[PLACES.index((4 - PLACES[at]) % 4)],
            device_id=(me, chip(PLACES[at]) + core),
            device_id_type=MESH,
        )

    def e_arrival(at):
        return pltpu.make_async_remote_copy(
            src_ref=share_out.at[at],
            dst_ref=share_in.at[at],
            send_sem=e_send.at[at],
            recv_sem=e_recv.at[at],
            device_id=(me, chip(PLACES[at]) + core),
            device_id_type=MESH,
        )

    def e_start(at):
        share_out[at] = strip_total(at).astype(BF16)
        e_copy(at).start()

    share_part(7, 8)
    pair_start(3)
    share_part(2, 7)
    pair_start(1)
    pair_start(2)
    e_start(3)
    share_part(0, 2)
    pair_start(0)
    e_start(1)
    e_start(2)
    total = strip_total(0)

    row = iota((2 * S, 2 * S), 0)
    lane = iota((2 * S, 2 * S), 1)
    weave = ((row >> 1) == (lane & (S - 1))) & ((row & 1) == (lane >> 6))
    weave = jnp.where(weave, 1.0, 0.0).astype(BF16)

    def rest_store(b):
        lanes = pl.ds(pl.multiple_of(b * X, X), X)
        return pltpu.make_async_copy(rest_out.at[b], residual.at[:, :, lanes], rest_sem.at[b])

    def rest_block(b, carry):
        woven = jnp.dot(
            weave,
            jnp.concatenate([base[b, :, :X], base[b, :, X:]], axis=0).astype(BF16),
            preferred_element_type=F32,
        )
        rest_out.at[b].reshape(2 * S, X)[...] = woven.astype(BF16)
        rest_store(b).start()
        return carry

    lax.fori_loop(0, UB, rest_block, 0, unroll=4)

    def turn_table(f, carry):
        lt_tab[f] = l_tab[:, pl.ds(pl.multiple_of(f * PIECE_COLS, X), PIECE_COLS)].T
        return carry

    lax.fori_loop(0, 4, turn_table, 0)
    for at in (1, 2, 3):
        e_arrival(at).wait_recv()
        total = total + share_in[at].astype(F32)
    share = jnp.concatenate([total[:, :X], total[:, X:]], axis=0).astype(BF16)

    def f_copy(p):
        there = facet_step(me, p)
        return pltpu.make_async_remote_copy(
            src_ref=back_out.at[there, :SENT],
            dst_ref=back.at[me, :SENT],
            send_sem=f_send.at[p],
            recv_sem=f_recv.at[me],
            device_id=(there, col),
            device_id_type=MESH,
        )

    def f_arrival(p):
        source = facet_step(me, back_step(p))
        return pltpu.make_async_remote_copy(
            src_ref=back_out.at[source, :SENT],
            dst_ref=back.at[source, :SENT],
            send_sem=f_send.at[p],
            recv_sem=f_recv.at[source],
            device_id=(source, col),
            device_id_type=MESH,
        )

    def back_group(a, carry):
        facet = ((me >> 3) + (far_first(a * 8) >> 3)) & 3
        made = jnp.dot(lt_tab[facet], share, preferred_element_type=F32)
        back_out[pl.ds(facet * 8, 8)] = made.astype(BF16).reshape(8, ROWS, X)

        def f_start(i, inner):
            f_copy(far_first(a * 8 + i)).start()
            return inner

        lax.fori_loop(0, 7 if a == 3 else 8, f_start, 0)
        return carry

    for a in range(4):
        back_group(a, 0)
    back[me] = back_out[me]

    def image_group(i, carry):
        start = (((me >> 3) - (far_first(i * 8) >> 3)) & 3) * 8

        def f_wait(j, inner):
            f_arrival(far_first(i * 8 + j)).wait_recv()
            return inner

        lax.fori_loop(0, 7 if i == 3 else 8, f_wait, 0)
        made = lax.dot_general(
            back[pl.ds(start, 8)].reshape(8 * ROWS, X),
            n_tab[pl.ds(start, 8)].reshape(8 * ROWS, 2 * Y),
            (((0,), (0,)), ((), ())),
            preferred_element_type=F32,
        )
        back_acc[...] = made if i == 0 else back_acc[...] + made
        return carry

    for i in range(4):
        image_group(i, 0)
    image[...] = (back_acc[...].T * (1.0 / 32.0)).astype(BF16)

    def sent(p, carry):
        a_copy(p).wait_send()
        f_copy(p).wait_send()
        return carry

    lax.fori_loop(1, K, sent, 0)
    for copy in c_copies:
        copy.wait_send()
    for at in range(4):
        pair_copy(at).wait_send()
    for at in (1, 2, 3):
        e_copy(at).wait_send()

    def stored(b, carry):
        rest_store(b).wait()
        return carry

    lax.fori_loop(0, UB, stored, 0)


def store(residual, image, residual_out, image_out, sem):
    copies = [
        pltpu.make_async_copy(residual, residual_out, sem.at[0]),
        pltpu.make_async_copy(image, image_out, sem.at[1]),
    ]
    for copy in copies:
        copy.start()
    for copy in copies:
        copy.wait()


def shards(
    facet_strips,
    facet_off,
    strip_off,
    sub_v,
    sub_u,
    screen_phase,
    visibilities,
    block_band,
    vis_weight,
):
    vmem = pl.BlockSpec(memory_space=pltpu.VMEM)
    anywhere = pl.BlockSpec(memory_space=pl.ANY)
    dma = pltpu.SemaphoreType.DMA
    q, b = piece_factors()
    residual, image = pl.pallas_call(
        kernel,
        name="imaging_round",
        out_shape=(
            jax.ShapeDtypeStruct((S, 2, U), BF16),
            jax.ShapeDtypeStruct((2 * Y, X), BF16),
        ),
        in_specs=[pl.BlockSpec(memory_space=pltpu.HBM)] * 11,
        out_specs=(anywhere, vmem),
        scratch_shapes=[
            pltpu.SMEM((4,), jnp.int32),
            pltpu.SMEM((C,), jnp.int32),
            pltpu.SMEM((K,), jnp.int32),
            pltpu.SMEM((C,), jnp.int32),
            pltpu.SMEM((1, BLOCKS), jnp.int32),
            pltpu.SMEM((8, BLOCKS), F32),
            pltpu.VMEM((2 * Y, X), BF16),
            pltpu.VMEM((SENT, 2 * Y), F32),
            pltpu.VMEM((S, PIECE_COLS), F32),
            pltpu.VMEM((S, U), F32),
            pltpu.VMEM((UB, BLOCKS * 8, 2, X), BF16),
            pltpu.VMEM((K // 4, 4, 4 * Y), F32),
            pltpu.VMEM((K, ROWS, 2 * Y), BF16),
            pltpu.VMEM((K, ROWS, X), BF16),
            pltpu.VMEM((K, ROWS, X), BF16),
            pltpu.VMEM((2 * S, K * ROWS), BF16),
            pltpu.VMEM((4, PIECE_COLS, 2 * S), BF16),
            pltpu.VMEM((4, 2, S, 2 * X), BF16),
            pltpu.VMEM((UB, 2 * X, 2 * X), BF16),
            pltpu.VMEM((UB, C, 2 * X), F32),
            pltpu.VMEM((UB, S, 2 * X), F32),
            pltpu.VMEM((S, X), F32),
            pltpu.VMEM((UB, S, 2, X), BF16),
            pltpu.VMEM((C * S, 2 * X), F32),
            pltpu.VMEM((4, S, 2 * X), BF16),
            pltpu.VMEM((4, S, 2 * X), BF16),
            pltpu.VMEM((4, S, 2 * X), BF16),
            pltpu.VMEM((4, S, 2 * X), BF16),
            pltpu.VMEM((K, ROWS, X), BF16),
            pltpu.VMEM((K, ROWS, X), BF16),
            pltpu.VMEM((X, 2 * Y), F32),
            dma((10,)),
            dma((UB,)),
            dma((UB,)),
            dma((K,)),
            dma((K,)),
            dma((8,)),
            dma((4, 2)),
            dma((4,)),
            dma((4,)),
            dma((4,)),
            dma((4,)),
            dma((K,)),
            dma((K,)),
        ],
        compiler_params=pltpu.CompilerParams(
            collective_id=0, has_side_effects=True, vmem_limit_bytes=48 * 1024 * 1024
        ),
    )(
        *(
            pltpu.with_memory_space_constraint(array, pltpu.HBM)
            for array in (
                facet_off,
                strip_off,
                sub_v,
                sub_u,
                facet_strips.reshape(2 * Y, X),
                jnp.asarray(b),
                jnp.asarray(q),
                block_band.T,
                vis_weight.T,
                screen_phase,
                visibilities.reshape(BLOCKS * 8, 2, U),
            )
        )
    )
    hbm = pl.BlockSpec(memory_space=pltpu.HBM)
    residual, image = pl.pallas_call(
        store,
        name="store",
        out_shape=(
            jax.ShapeDtypeStruct((S, 2, U), BF16),
            jax.ShapeDtypeStruct((2 * Y, X), BF16),
        ),
        in_specs=[anywhere, anywhere],
        out_specs=(hbm, hbm),
        scratch_shapes=[dma((2,))],
    )(
        pltpu.with_memory_space_constraint(residual, pltpu.VMEM),
        pltpu.with_memory_space_constraint(image, pltpu.VMEM),
    )
    return residual, image.reshape(Y, 2, X)


def solution(mesh):
    return jax.shard_map(
        shards,
        mesh=mesh,
        in_specs=(
            P("facet", None, "col"),
            P(),
            P(),
            P(),
            P(),
            P("facet", "col"),
            P("facet", None, None, "col"),
            P("facet", "col"),
            P("facet", "col"),
        ),
        out_specs=(P("facet", None, "col"), P("facet", None, "col")),
        check_vma=False,
    )
```

```python
import math

import jax
import jax.numpy as jnp
from jax import lax
from jax.experimental import pallas as pl
from jax.experimental.pallas import tpu as pltpu
import numpy as np
from jax.sharding import PartitionSpec as P

MESH = pl.DeviceIdType.MESH
IMG = 65536
TURN = 2.0 * math.pi / IMG
F32 = jnp.float32
BF16 = jnp.bfloat16

K = 32
C = 8
S = 64
Y = 512
X = 128
U = 1024
PIECES = 8
UB = U // X
BLOCKS = 16
PLACES = (0, 1, 3, 2)
HALF = 10
TERMS = 2 * HALF
SENT = 2 * TERMS
ROWS = 48
PIECE_COLS = PIECES * ROWS


def piece_factors():
    r = np.arange(S) - (S - 1) / 2
    d = np.arange(Y) - (Y - 1) / 2
    angle = 2.0 * np.pi * np.outer(r, d) / (PIECES * Y)
    left = []
    right = []
    for part in (np.cos(angle), np.sin(angle)):
        u, sigma, v = np.linalg.svd(part, full_matrices=False)
        left.append(u[:, :HALF] * sigma[:HALF])
        right.append(v[:HALF])
    q = np.concatenate(left, axis=1) / 1024.0
    b = np.concatenate(right, axis=0)
    q = np.pad(np.tile(q, (1, 2)), ((0, 0), (0, ROWS - SENT)))
    b = np.tile(np.repeat(b, 2, axis=1), (2, 1))
    return np.tile(q, (1, PIECES)).astype(np.float32), b.astype(np.float32)


def quarter_turns(q, t):
    t2 = t * t
    sin = t + t * t2 * (-1.6666654611e-1 + t2 * (8.3321608736e-3 + t2 * -1.9515295891e-4))
    cos = 1.0 - 0.5 * t2 + t2 * t2 * (
        4.166664568298827e-2 + t2 * (-1.388731625493765e-3 + t2 * 2.443315711809948e-5)
    )
    odd = (q & 1) == 1
    even_cos = jnp.where(odd, sin, cos)
    even_sin = jnp.where(odd, cos, sin)
    return (
        jnp.where(((q + 1) & 2) != 0, -even_cos, even_cos),
        jnp.where((q & 2) != 0, -even_sin, even_sin),
    )


def unit(k):
    k = k & (IMG - 1)
    q = (k + IMG // 8) >> 14
    return quarter_turns(q, (k - (q << 14)).astype(F32) * TURN)


def cos_sin(angle):
    turns = jnp.floor(angle * (2.0 / math.pi) + 0.5)
    t = (angle - turns * 1.5703125) - turns * 4.837512969970703e-4
    t = t - turns * 7.549789948768648e-8
    return quarter_turns(turns.astype(jnp.int32), t)


def iota(shape, dim):
    return lax.broadcasted_iota(jnp.int32, shape, dim)


def facet_step(me, p):
    x = ((me >> 3) + (p >> 3)) & 3
    z = ((me >> 2) ^ (p >> 2)) & 1
    y = (me + p) & 3
    return (x << 3) | (z << 2) | y


def back_step(p):
    x = (0 - (p >> 3)) & 3
    y = (0 - p) & 3
    return (x << 3) | (p & 4) | y


def far_first(i):
    a = i >> 3
    b = i & 3
    return ((2 ^ a ^ (a >> 1)) << 3) | (4 - (i & 4)) | (2 ^ b ^ (b >> 1))


def kernel(
    facet_off_hbm,
    strip_off_hbm,
    sub_v_hbm,
    sub_u_hbm,
    strips_hbm,
    b_hbm,
    q_hbm,
    band_hbm,
    weight_hbm,
    screen_hbm,
    vis_hbm,
    residual,
    image,
    facet_off,
    strip_off,
    sub_v,
    sub_u,
    band,
    row_weight,
    strips,
    b_tab,
    q_tab,
    screen,
    vis,
    mod,
    n_tab,
    part_out,
    part_in,
    l_tab,
    lt_tab,
    asm,
    w_tab,
    d_tab,
    base,
    weight,
    rest_out,
    share_acc,
    pair_out,
    pair_in,
    share_out,
    share_in,
    back_out,
    back,
    back_acc,
    load_sem,
    vis_sem,
    rest_sem,
    a_send,
    a_recv,
    c_send,
    c_recv,
    pair_send,
    pair_recv,
    e_send,
    e_recv,
    f_send,
    f_recv,
):
    me = lax.axis_index("facet")
    col = lax.axis_index("col")
    z = col >> 1
    core = col & 1
    sibling = 1 - core

    loads = [
        pltpu.make_async_copy(src, dst, load_sem.at[i])
        for i, (src, dst) in enumerate(
            [
                (facet_off_hbm, facet_off),
                (sub_v_hbm, sub_v),
                (b_hbm, b_tab),
                (strips_hbm, strips),
                (strip_off_hbm, strip_off),
                (sub_u_hbm, sub_u),
                (band_hbm, band),
                (weight_hbm, row_weight),
                (q_hbm, q_tab),
                (screen_hbm, screen),
            ]
        )
    ]
    for load in loads[:4]:
        load.start()
    pad = slice(32, ROWS)
    part_in[:, pad] = jnp.zeros((K, ROWS - 32, X), BF16)
    back[:, pad] = jnp.zeros((K, ROWS - 32, X), BF16)
    barrier = pltpu.get_barrier_semaphore()

    def greet_facet(i, carry):
        pl.semaphore_signal(
            barrier, inc=1, device_id=(facet_step(me, far_first(i)), col), device_id_type=MESH
        )
        return carry

    lax.fori_loop(0, K - 1, greet_facet, 0)
    for step in (2, 1, 3, 0):
        for half in (0, 1)[step == 0 :]:
            pl.semaphore_signal(
                barrier,
                inc=1,
                device_id=(me, 2 * ((z + step) & 3) + (core ^ half)),
                device_id_type=MESH,
            )
    for load in loads[4:]:
        load.start()

    def vis_load(b):
        lanes = pl.ds(pl.multiple_of(b * X, X), X)
        return pltpu.make_async_copy(vis_hbm.at[:, :, lanes], vis.at[b], vis_sem.at[b])

    def vis_start(b, carry):
        vis_load(b).start()
        return carry

    lax.fori_loop(0, UB, vis_start, 0)

    for load in loads[:4]:
        load.wait()
    first = facet_off[me // PIECES] + (me % PIECES) * Y

    def mod_rows(i, carry):
        row = iota((8, X), 0)
        v = jnp.zeros((8, X), jnp.int32)
        for r in range(8):
            v = jnp.where(row == r, sub_v[i * 8 + r], v)
        for h in range(2 * Y // X):
            lane = iota((8, X), 1) + h * X
            y = lane >> 1
            real, imag = unit(128772 - 504 * y - v * (first + y) + ((lane & 1) << 14))
            for g in range(2):
                mod[i * 2 + g, :, h * X : (h + 1) * X] = real[g * 4 : g * 4 + 4]
                mod[i * 2 + g, :, 2 * Y + h * X : 2 * Y + (h + 1) * X] = imag[g * 4 : g * 4 + 4]
        return carry

    lax.fori_loop(0, K // 8, mod_rows, 0, unroll=2)

    is_real = iota((SENT, X), 0) < TERMS
    padding = jnp.zeros((ROWS - SENT, X), F32)

    def facet_group(g, carry):
        for h in range(2 * Y // X):
            lanes = slice(h * X, (h + 1) * X)
            upper = slice(2 * Y + h * X, 2 * Y + (h + 1) * X)
            b = b_tab[:, lanes]
            for i in range(4):
                turn = jnp.where(is_real, mod[g, i : i + 1, lanes], mod[g, i : i + 1, upper])
                n_tab[g * 4 + i, :, lanes] = jnp.concatenate([b * turn, padding], axis=0).astype(BF16)
        made = jnp.dot(
            n_tab[pl.ds(g * 4, 4)].reshape(4 * ROWS, 2 * Y),
            strips[...],
            preferred_element_type=F32,
        )
        part_out[pl.ds(g * 4, 4)] = made.astype(BF16).reshape(4, ROWS, X)
        return carry

    lax.fori_loop(0, K // 4, facet_group, 0, unroll=4)
    pl.semaphore_wait(barrier, K - 1 + C - 1)

    def a_copy(p):
        there = facet_step(me, p)
        return pltpu.make_async_remote_copy(
            src_ref=part_out.at[there, :SENT],
            dst_ref=part_in.at[me, :SENT],
            send_sem=a_send.at[p],
            recv_sem=a_recv.at[me],
            device_id=(there, col),
            device_id_type=MESH,
        )

    def a_arrival(p):
        source = facet_step(me, back_step(p))
        return pltpu.make_async_remote_copy(
            src_ref=part_out.at[source, :SENT],
            dst_ref=part_in.at[source, :SENT],
            send_sem=a_send.at[p],
            recv_sem=a_recv.at[source],
            device_id=(source, col),
            device_id_type=MESH,
        )

    def a_start(i, carry):
        a_copy(far_first(i)).start()
        return carry

    lax.fori_loop(0, K - 1, a_start, 0)
    part_in[me] = part_out[me]

    for load in loads[8:]:
        load.wait()

    l_lane = iota((8, PIECE_COLS), 1)
    piece = jnp.zeros((8, PIECE_COLS), jnp.int32)
    for h in range(1, PIECES):
        piece = piece + (l_lane >= h * ROWS).astype(jnp.int32)
    l_term = l_lane - piece * ROWS
    l_imag = (l_term >= TERMS).astype(jnp.int32)
    l_odd = (l_term - l_imag * TERMS >= HALF).astype(jnp.int32)
    l_quarter = ((l_imag - l_odd) << 14)[0:1]
    l_place = (piece * (16 * Y) + 4088)[0:1]

    def l_facet(f, carry):
        off = facet_off[f]
        r = iota((S, PIECE_COLS), 0)
        real, imag = unit(l_quarter - r * (16 * off + l_place))
        q = q_tab[...]
        right = jnp.concatenate([q * real, q * imag], axis=0)
        row = iota((2 * S, 2 * S), 0)
        lane = iota((2 * S, 2 * S), 1)
        left, _ = unit(
            (row & (S - 1)) * (off + 1024 * (lane & (S - 1))) + (((lane >> 6) - (row >> 6)) << 14)
        )
        made = jnp.dot(left, right, precision=lax.Precision.HIGHEST, preferred_element_type=F32)
        l_tab[:, pl.ds(pl.multiple_of(f * PIECE_COLS, X), PIECE_COLS)] = made.astype(BF16)
        return carry

    lax.fori_loop(0, 4, l_facet, 0)
    def a_wait(i, carry):
        a_arrival(far_first(i)).wait_recv()
        return carry

    lax.fori_loop(0, K - 1, a_wait, 0)
    made = jnp.dot(l_tab[...], part_in[...].reshape(K * ROWS, X), preferred_element_type=F32)
    asm[0, 0] = jnp.concatenate([made[:S], made[S:]], axis=1).astype(BF16)

    def c_copy(src, dst, half, send, there):
        return pltpu.make_async_remote_copy(
            src_ref=asm.at[src, 0],
            dst_ref=asm.at[dst, half],
            send_sem=c_send.at[send],
            recv_sem=c_recv.at[dst, half],
            device_id=(me, there),
            device_id_type=MESH,
        )

    def chip(step):
        return 2 * ((z + step) & 3)

    c_copies = [
        c_copy(0, 3, 0, 6, chip(2) + core),
        c_copy(0, 3, 1, 7, chip(2) + sibling),
        c_copy(0, 0, 1, 0, chip(0) + sibling),
        c_copy(0, 2, 0, 2, chip(1) + core),
        c_copy(0, 1, 0, 3, chip(3) + core),
    ]
    for copy in c_copies:
        copy.start()

    for load in loads[4:8]:
        load.wait()
    frequency = sub_u[col]

    def w_block(b, carry):
        for h in range(2):
            x = iota((X // 2, X), 0) + h * (X // 2)
            u = iota((X // 2, X), 1) + b * X
            real, imag = unit(0 - 64 * x * (frequency + u))
            top = slice(h * (X // 2), (h + 1) * (X // 2))
            low = slice(X + h * (X // 2), X + (h + 1) * (X // 2))
            w_tab[b, top, :X] = real.astype(BF16)
            w_tab[b, top, X:] = imag.astype(BF16)
            w_tab[b, low, :X] = (-imag).astype(BF16)
            w_tab[b, low, X:] = real.astype(BF16)
        return carry

    lax.fori_loop(0, UB, w_block, 0)

    strip = jnp.zeros((C, X), jnp.int32)
    for at, step in enumerate(PLACES):
        for c in range(2):
            strip = jnp.where(
                iota((C, X), 0) == 2 * at + c, strip_off[2 * ((z + step) & 3) + (core ^ c)], strip
            )

    def d_block(b, carry):
        real, imag = unit(0 - strip * (frequency + iota((C, X), 1) + b * X))
        d_tab[b, :, :X] = real
        d_tab[b, :, X:] = imag
        return carry

    lax.fori_loop(0, UB, d_block, 0)

    pair_lane = iota((8, 2 * X), 1) >> 1

    def weight_lane(i, total):
        return jnp.where(pair_lane == i, row_weight[i & 7, i >> 3], total)

    weight_row = lax.fori_loop(0, BLOCKS * 8, weight_lane, jnp.zeros((8, 2 * X), F32))
    band_row = jnp.zeros((8, 2 * X), jnp.int32)
    for b in range(BLOCKS):
        band_row = jnp.where((pair_lane >> 3) == b, band[0, b], band_row)
    row = iota((2 * S, 2 * X), 0)
    lane = iota((2 * S, 2 * X), 1)
    covers = (
        (band_row[0:1] == ((row & (S - 1)) >> 3))
        & (((lane >> 1) & 7) == (row & 7))
        & ((lane & 1) == (row >> 6))
    )
    spread = jnp.where(covers, jnp.broadcast_to(weight_row[0:1], (2 * S, 2 * X)), 0.0)
    weight[...] = jnp.broadcast_to(jnp.sum(spread[:S], axis=1, keepdims=True), (S, X)) * (
        1.0 / 32.0
    )
    high = spread.astype(BF16)
    both = jnp.concatenate([high, (spread - high.astype(F32)).astype(BF16)], axis=0)

    def base_block(b, carry):
        vis_load(b).wait()
        made = jnp.dot(both, vis.at[b].reshape(2 * X, X)[...], preferred_element_type=F32)
        real = made[:S] + made[2 * S : 3 * S]
        imag = made[S : 2 * S] + made[3 * S :]
        cos, sin = cos_sin(screen[:, pl.ds(pl.multiple_of(b * X, X), X)])
        base[b, :, :X] = real * cos + imag * sin
        base[b, :, X:] = imag * cos - real * sin
        return carry

    lax.fori_loop(0, UB, base_block, 0)

    def turn_table(f, carry):
        lt_tab[f] = l_tab[:, pl.ds(pl.multiple_of(f * PIECE_COLS, X), PIECE_COLS)].T
        return carry

    lax.fori_loop(0, 4, turn_table, 0)

    def c_wait(at, half):
        c_copy(at, at, half, 0, chip(0) + sibling).wait_recv()

    def grid_part(low, count):
        def grid_block(b, carry):
            made = jnp.dot(
                asm[low : low + count].reshape(count * 2 * S, 2 * X),
                w_tab[b],
                preferred_element_type=F32,
            )
            real = jnp.zeros((S, X), F32)
            imag = jnp.zeros((S, X), F32)
            for c in range(2 * count):
                dr = d_tab[b, 2 * low + c : 2 * low + c + 1, :X]
                di = d_tab[b, 2 * low + c : 2 * low + c + 1, X:]
                pr = made[c * S : (c + 1) * S, :X]
                pi = made[c * S : (c + 1) * S, X:]
                real = real + (pr * dr - pi * di)
                imag = imag + (pr * di + pi * dr)
            base[b, :, :X] -= weight[...] * real
            base[b, :, X:] -= weight[...] * imag
            return carry

        lax.fori_loop(0, UB, grid_block, 0, unroll=4)

    c_wait(0, 1)
    grid_part(0, 1)
    for at in (1, 2):
        c_wait(at, 0)
        forward = c_copy(at, at, 1, 3 + at, chip(0) + sibling)
        forward.start()
        c_copies.append(forward)
    c_wait(1, 1)
    c_wait(2, 1)
    grid_part(1, 2)
    c_wait(3, 0)
    c_wait(3, 1)
    grid_part(3, 1)

    def share_part(low, high):
        rows = slice(low * S, high * S)
        share_acc[rows, :] = jnp.zeros(((high - low) * S, 2 * X), F32)

        def share_block(b, carry):
            real = base[b, :, :X]
            imag = base[b, :, X:]
            turned = []
            for c in range(low, high):
                dr = d_tab[b, c : c + 1, :X]
                di = d_tab[b, c : c + 1, X:]
                turned.append(
                    jnp.concatenate(
                        [
                            (real * dr + imag * di).astype(BF16),
                            (imag * dr - real * di).astype(BF16),
                        ],
                        axis=1,
                    )
                )
            share_acc[rows, :] += lax.dot_general(
                jnp.concatenate(turned, axis=0),
                w_tab[b],
                (((1,), (1,)), ((), ())),
                preferred_element_type=F32,
            )
            return carry

        lax.fori_loop(0, UB, share_block, 0, unroll=4)

    def pair_copy(at):
        return pltpu.make_async_remote_copy(
            src_ref=pair_out.at[at],
            dst_ref=pair_in.at[at],
            send_sem=pair_send.at[at],
            recv_sem=pair_recv.at[at],
            device_id=(me, 2 * z + sibling),
            device_id_type=MESH,
        )

    def pair_start(at):
        pair_out[at] = share_acc[(2 * at + 1) * S : (2 * at + 2) * S, :].astype(BF16)
        pair_copy(at).start()

    def strip_total(at):
        pair_copy(at).wait_recv()
        return share_acc[2 * at * S : (2 * at + 1) * S, :] + pair_in[at].astype(F32)

    def e_copy(at):
        return pltpu.make_async_remote_copy(
            src_ref=share_out.at[at],
            dst_ref=share_in.at[PLACES.index((4 - PLACES[at]) % 4)],
            send_sem=e_send.at[at],
            recv_sem=e_recv.at[PLACES.index((4 - PLACES[at]) % 4)],
            device_id=(me, chip(PLACES[at]) + core),
            device_id_type=MESH,
        )

    def e_arrival(at):
        return pltpu.make_async_remote_copy(
            src_ref=share_out.at[at],
            dst_ref=share_in.at[at],
            send_sem=e_send.at[at],
            recv_sem=e_recv.at[at],
            device_id=(me, chip(PLACES[at]) + core),
            device_id_type=MESH,
        )

    def e_start(at):
        share_out[at] = strip_total(at).astype(BF16)
        e_copy(at).start()

    share_part(7, 8)
    pair_start(3)
    share_part(2, 7)
    pair_start(1)
    pair_start(2)
    e_start(3)
    share_part(0, 2)
    pair_start(0)
    e_start(1)
    e_start(2)
    total = strip_total(0)

    row = iota((2 * S, 2 * S), 0)
    lane = iota((2 * S, 2 * S), 1)
    weave = ((row >> 1) == (lane & (S - 1))) & ((row & 1) == (lane >> 6))
    weave = jnp.where(weave, 1.0, 0.0).astype(BF16)

    def rest_store(b):
        lanes = pl.ds(pl.multiple_of(b * X, X), X)
        return pltpu.make_async_copy(rest_out.at[b], residual.at[:, :, lanes], rest_sem.at[b])

    def rest_block(b, carry):
        woven = jnp.dot(
            weave,
            jnp.concatenate([base[b, :, :X], base[b, :, X:]], axis=0).astype(BF16),
            preferred_element_type=F32,
        )
        rest_out.at[b].reshape(2 * S, X)[...] = woven.astype(BF16)
        rest_store(b).start()
        return carry

    lax.fori_loop(0, UB, rest_block, 0, unroll=4)

    for at in (1, 2, 3):
        e_arrival(at).wait_recv()
        total = total + share_in[at].astype(F32)
    share = jnp.concatenate([total[:, :X], total[:, X:]], axis=0).astype(BF16)

    def f_copy(p):
        there = facet_step(me, p)
        return pltpu.make_async_remote_copy(
            src_ref=back_out.at[there, :SENT],
            dst_ref=back.at[me, :SENT],
            send_sem=f_send.at[p],
            recv_sem=f_recv.at[me],
            device_id=(there, col),
            device_id_type=MESH,
        )

    def f_arrival(p):
        source = facet_step(me, back_step(p))
        return pltpu.make_async_remote_copy(
            src_ref=back_out.at[source, :SENT],
            dst_ref=back.at[source, :SENT],
            send_sem=f_send.at[p],
            recv_sem=f_recv.at[source],
            device_id=(source, col),
            device_id_type=MESH,
        )

    def back_group(a, carry):
        facet = ((me >> 3) + (far_first(a * 8) >> 3)) & 3
        made = jnp.dot(lt_tab[facet], share, preferred_element_type=F32)
        back_out[pl.ds(facet * 8, 8)] = made.astype(BF16).reshape(8, ROWS, X)

        def f_start(i, inner):
            f_copy(far_first(a * 8 + i)).start()
            return inner

        lax.fori_loop(0, 7 if a == 3 else 8, f_start, 0)
        return carry

    for a in range(4):
        back_group(a, 0)
    back[me] = back_out[me]

    def image_group(i, carry):
        start = (((me >> 3) - (far_first(i * 8) >> 3)) & 3) * 8

        def f_wait(j, inner):
            f_arrival(far_first(i * 8 + j)).wait_recv()
            return inner

        lax.fori_loop(0, 7 if i == 3 else 8, f_wait, 0)
        made = lax.dot_general(
            back[pl.ds(start, 8)].reshape(8 * ROWS, X),
            n_tab[pl.ds(start, 8)].reshape(8 * ROWS, 2 * Y),
            (((0,), (0,)), ((), ())),
            preferred_element_type=F32,
        )
        back_acc[...] = made if i == 0 else back_acc[...] + made
        return carry

    for i in range(4):
        image_group(i, 0)
    image[...] = (back_acc[...].T * (1.0 / 32.0)).astype(BF16)

    def sent(p, carry):
        a_copy(p).wait_send()
        f_copy(p).wait_send()
        return carry

    lax.fori_loop(1, K, sent, 0)
    for copy in c_copies:
        copy.wait_send()
    for at in range(4):
        pair_copy(at).wait_send()
    for at in (1, 2, 3):
        e_copy(at).wait_send()

    def stored(b, carry):
        rest_store(b).wait()
        return carry

    lax.fori_loop(0, UB, stored, 0)


def store(residual, image, residual_out, image_out, sem):
    copies = [
        pltpu.make_async_copy(residual, residual_out, sem.at[0]),
        pltpu.make_async_copy(image, image_out, sem.at[1]),
    ]
    for copy in copies:
        copy.start()
    for copy in copies:
        copy.wait()


def shards(
    facet_strips,
    facet_off,
    strip_off,
    sub_v,
    sub_u,
    screen_phase,
    visibilities,
    block_band,
    vis_weight,
):
    vmem = pl.BlockSpec(memory_space=pltpu.VMEM)
    anywhere = pl.BlockSpec(memory_space=pl.ANY)
    dma = pltpu.SemaphoreType.DMA
    q, b = piece_factors()
    residual, image = pl.pallas_call(
        kernel,
        name="imaging_round",
        out_shape=(
            jax.ShapeDtypeStruct((S, 2, U), BF16),
            jax.ShapeDtypeStruct((2 * Y, X), BF16),
        ),
        in_specs=[pl.BlockSpec(memory_space=pltpu.HBM)] * 11,
        out_specs=(anywhere, vmem),
        scratch_shapes=[
            pltpu.SMEM((4,), jnp.int32),
            pltpu.SMEM((C,), jnp.int32),
            pltpu.SMEM((K,), jnp.int32),
            pltpu.SMEM((C,), jnp.int32),
            pltpu.SMEM((1, BLOCKS), jnp.int32),
            pltpu.SMEM((8, BLOCKS), F32),
            pltpu.VMEM((2 * Y, X), BF16),
            pltpu.VMEM((SENT, 2 * Y), F32),
            pltpu.VMEM((S, PIECE_COLS), F32),
            pltpu.VMEM((S, U), F32),
            pltpu.VMEM((UB, BLOCKS * 8, 2, X), BF16),
            pltpu.VMEM((K // 4, 4, 4 * Y), F32),
            pltpu.VMEM((K, ROWS, 2 * Y), BF16),
            pltpu.VMEM((K, ROWS, X), BF16),
            pltpu.VMEM((K, ROWS, X), BF16),
            pltpu.VMEM((2 * S, K * ROWS), BF16),
            pltpu.VMEM((4, PIECE_COLS, 2 * S), BF16),
            pltpu.VMEM((4, 2, S, 2 * X), BF16),
            pltpu.VMEM((UB, 2 * X, 2 * X), BF16),
            pltpu.VMEM((UB, C, 2 * X), F32),
            pltpu.VMEM((UB, S, 2 * X), F32),
            pltpu.VMEM((S, X), F32),
            pltpu.VMEM((UB, S, 2, X), BF16),
            pltpu.VMEM((C * S, 2 * X), F32),
            pltpu.VMEM((4, S, 2 * X), BF16),
            pltpu.VMEM((4, S, 2 * X), BF16),
            pltpu.VMEM((4, S, 2 * X), BF16),
            pltpu.VMEM((4, S, 2 * X), BF16),
            pltpu.VMEM((K, ROWS, X), BF16),
            pltpu.VMEM((K, ROWS, X), BF16),
            pltpu.VMEM((X, 2 * Y), F32),
            dma((10,)),
            dma((UB,)),
            dma((UB,)),
            dma((K,)),
            dma((K,)),
            dma((8,)),
            dma((4, 2)),
            dma((4,)),
            dma((4,)),
            dma((4,)),
            dma((4,)),
            dma((K,)),
            dma((K,)),
        ],
        compiler_params=pltpu.CompilerParams(
            collective_id=0, has_side_effects=True, vmem_limit_bytes=48 * 1024 * 1024
        ),
    )(
        *(
            pltpu.with_memory_space_constraint(array, pltpu.HBM)
            for array in (
                facet_off,
                strip_off,
                sub_v,
                sub_u,
                facet_strips.reshape(2 * Y, X),
                jnp.asarray(b),
                jnp.asarray(q),
                block_band.T,
                vis_weight.T,
                screen_phase,
                visibilities.reshape(BLOCKS * 8, 2, U),
            )
        )
    )
    hbm = pl.BlockSpec(memory_space=pltpu.HBM)
    residual, image = pl.pallas_call(
        store,
        name="store",
        out_shape=(
            jax.ShapeDtypeStruct((S, 2, U), BF16),
            jax.ShapeDtypeStruct((2 * Y, X), BF16),
        ),
        in_specs=[anywhere, anywhere],
        out_specs=(hbm, hbm),
        scratch_shapes=[dma((2,))],
    )(
        pltpu.with_memory_space_constraint(residual, pltpu.VMEM),
        pltpu.with_memory_space_constraint(image, pltpu.VMEM),
    )
    return residual, image.reshape(Y, 2, X)


def solution(mesh):
    return jax.shard_map(
        shards,
        mesh=mesh,
        in_specs=(
            P("facet", None, "col"),
            P(),
            P(),
            P(),
            P(),
            P("facet", "col"),
            P("facet", None, None, "col"),
            P("facet", "col"),
            P("facet", "col"),
        ),
        out_specs=(P("facet", None, "col"), P("facet", None, "col")),
        check_vma=False,
    )
```

```python
import math

import jax
import jax.numpy as jnp
from jax import lax
from jax.experimental import pallas as pl
from jax.experimental.pallas import tpu as pltpu
import numpy as np
from jax.sharding import PartitionSpec as P

MESH = pl.DeviceIdType.MESH
IMG = 65536
TURN = 2.0 * math.pi / IMG
F32 = jnp.float32
BF16 = jnp.bfloat16

K = 32
C = 8
S = 64
Y = 512
X = 128
U = 1024
PIECES = 8
UB = U // X
BLOCKS = 16
PLACES = (0, 1, 3, 2)
HALF = 10
TERMS = 2 * HALF
SENT = 2 * TERMS
ROWS = 48
PIECE_COLS = PIECES * ROWS


def piece_factors():
    r = np.arange(S) - (S - 1) / 2
    d = np.arange(Y) - (Y - 1) / 2
    angle = 2.0 * np.pi * np.outer(r, d) / (PIECES * Y)
    left = []
    right = []
    for part in (np.cos(angle), np.sin(angle)):
        u, sigma, v = np.linalg.svd(part, full_matrices=False)
        left.append(u[:, :HALF] * sigma[:HALF])
        right.append(v[:HALF])
    q = np.concatenate(left, axis=1) / 1024.0
    b = np.concatenate(right, axis=0)
    q = np.pad(np.tile(q, (1, 2)), ((0, 0), (0, ROWS - SENT)))
    b = np.tile(np.repeat(b, 2, axis=1), (2, 1))
    return np.tile(q, (1, PIECES)).astype(np.float32), b.astype(np.float32)


def quarter_turns(q, t):
    t2 = t * t
    sin = t + t * t2 * (-1.6666654611e-1 + t2 * (8.3321608736e-3 + t2 * -1.9515295891e-4))
    cos = 1.0 - 0.5 * t2 + t2 * t2 * (
        4.166664568298827e-2 + t2 * (-1.388731625493765e-3 + t2 * 2.443315711809948e-5)
    )
    odd = (q & 1) == 1
    even_cos = jnp.where(odd, sin, cos)
    even_sin = jnp.where(odd, cos, sin)
    return (
        jnp.where(((q + 1) & 2) != 0, -even_cos, even_cos),
        jnp.where((q & 2) != 0, -even_sin, even_sin),
    )


def unit(k):
    k = k & (IMG - 1)
    q = (k + IMG // 8) >> 14
    return quarter_turns(q, (k - (q << 14)).astype(F32) * TURN)


def cos_sin(angle):
    turns = jnp.floor(angle * (2.0 / math.pi) + 0.5)
    t = (angle - turns * 1.5703125) - turns * 4.837512969970703e-4
    t = t - turns * 7.549789948768648e-8
    return quarter_turns(turns.astype(jnp.int32), t)


def iota(shape, dim):
    return lax.broadcasted_iota(jnp.int32, shape, dim)


def facet_step(me, p):
    x = ((me >> 3) + (p >> 3)) & 3
    z = ((me >> 2) ^ (p >> 2)) & 1
    y = (me + p) & 3
    return (x << 3) | (z << 2) | y


def back_step(p):
    x = (0 - (p >> 3)) & 3
    y = (0 - p) & 3
    return (x << 3) | (p & 4) | y


def far_first(i):
    a = i >> 3
    b = i & 3
    return ((2 ^ a ^ (a >> 1)) << 3) | (4 - (i & 4)) | (2 ^ b ^ (b >> 1))


def kernel(
    facet_off_hbm,
    strip_off_hbm,
    sub_v_hbm,
    sub_u_hbm,
    strips_hbm,
    b_hbm,
    q_hbm,
    band_hbm,
    weight_hbm,
    screen_hbm,
    vis_hbm,
    residual,
    image,
    facet_off,
    strip_off,
    sub_v,
    sub_u,
    band,
    row_weight,
    strips,
    b_tab,
    q_tab,
    screen,
    vis,
    mod,
    n_tab,
    part_out,
    part_in,
    l_tab,
    lt_tab,
    asm,
    w_tab,
    d_tab,
    base,
    weight,
    rest_out,
    share_acc,
    pair_out,
    pair_in,
    share_out,
    share_in,
    back_out,
    back,
    back_acc,
    load_sem,
    vis_sem,
    rest_sem,
    a_send,
    a_recv,
    c_send,
    c_recv,
    pair_send,
    pair_recv,
    e_send,
    e_recv,
    f_send,
    f_recv,
):
    me = lax.axis_index("facet")
    col = lax.axis_index("col")
    z = col >> 1
    core = col & 1
    sibling = 1 - core

    loads = [
        pltpu.make_async_copy(src, dst, load_sem.at[i])
        for i, (src, dst) in enumerate(
            [
                (facet_off_hbm, facet_off),
                (sub_v_hbm, sub_v),
                (b_hbm, b_tab),
                (strips_hbm, strips),
                (strip_off_hbm, strip_off),
                (sub_u_hbm, sub_u),
                (band_hbm, band),
                (weight_hbm, row_weight),
                (q_hbm, q_tab),
                (screen_hbm, screen),
            ]
        )
    ]
    for load in loads[:4]:
        load.start()
    pad = slice(32, ROWS)
    part_in[:, pad] = jnp.zeros((K, ROWS - 32, X), BF16)
    back[:, pad] = jnp.zeros((K, ROWS - 32, X), BF16)
    barrier = pltpu.get_barrier_semaphore()

    def greet_facet(i, carry):
        pl.semaphore_signal(
            barrier, inc=1, device_id=(facet_step(me, far_first(i)), col), device_id_type=MESH
        )
        return carry

    lax.fori_loop(0, K - 1, greet_facet, 0)
    for step in (2, 1, 3, 0):
        for half in (0, 1)[step == 0 :]:
            pl.semaphore_signal(
                barrier,
                inc=1,
                device_id=(me, 2 * ((z + step) & 3) + (core ^ half)),
                device_id_type=MESH,
            )
    for load in loads[4:]:
        load.start()

    def vis_load(b):
        lanes = pl.ds(pl.multiple_of(b * X, X), X)
        return pltpu.make_async_copy(vis_hbm.at[:, :, lanes], vis.at[b], vis_sem.at[b])

    def vis_start(b, carry):
        vis_load(b).start()
        return carry

    lax.fori_loop(0, UB, vis_start, 0)

    for load in loads[:4]:
        load.wait()
    first = facet_off[me // PIECES] + (me % PIECES) * Y

    def mod_rows(i, carry):
        row = iota((8, X), 0)
        v = jnp.zeros((8, X), jnp.int32)
        for r in range(8):
            v = jnp.where(row == r, sub_v[i * 8 + r], v)
        for h in range(2 * Y // X):
            lane = iota((8, X), 1) + h * X
            y = lane >> 1
            real, imag = unit(128772 - 504 * y - v * (first + y) + ((lane & 1) << 14))
            for g in range(2):
                mod[i * 2 + g, :, h * X : (h + 1) * X] = real[g * 4 : g * 4 + 4]
                mod[i * 2 + g, :, 2 * Y + h * X : 2 * Y + (h + 1) * X] = imag[g * 4 : g * 4 + 4]
        return carry

    lax.fori_loop(0, K // 8, mod_rows, 0, unroll=2)

    is_real = iota((SENT, X), 0) < TERMS
    padding = jnp.zeros((ROWS - SENT, X), F32)

    def facet_group(g, carry):
        for h in range(2 * Y // X):
            lanes = slice(h * X, (h + 1) * X)
            upper = slice(2 * Y + h * X, 2 * Y + (h + 1) * X)
            b = b_tab[:, lanes]
            for i in range(4):
                turn = jnp.where(is_real, mod[g, i : i + 1, lanes], mod[g, i : i + 1, upper])
                n_tab[g * 4 + i, :, lanes] = jnp.concatenate([b * turn, padding], axis=0).astype(BF16)
        made = jnp.dot(
            n_tab[pl.ds(g * 4, 4)].reshape(4 * ROWS, 2 * Y),
            strips[...],
            preferred_element_type=F32,
        )
        part_out[pl.ds(g * 4, 4)] = made.astype(BF16).reshape(4, ROWS, X)
        return carry

    lax.fori_loop(0, K // 4, facet_group, 0, unroll=4)
    pl.semaphore_wait(barrier, K - 1 + C - 1)

    def a_copy(p):
        there = facet_step(me, p)
        return pltpu.make_async_remote_copy(
            src_ref=part_out.at[there, :SENT],
            dst_ref=part_in.at[me, :SENT],
            send_sem=a_send.at[p],
            recv_sem=a_recv.at[me],
            device_id=(there, col),
            device_id_type=MESH,
        )

    def a_arrival(p):
        source = facet_step(me, back_step(p))
        return pltpu.make_async_remote_copy(
            src_ref=part_out.at[source, :SENT],
            dst_ref=part_in.at[source, :SENT],
            send_sem=a_send.at[p],
            recv_sem=a_recv.at[source],
            device_id=(source, col),
            device_id_type=MESH,
        )

    def a_start(i, carry):
        a_copy(far_first(i)).start()
        return carry

    lax.fori_loop(0, K - 1, a_start, 0)
    part_in[me] = part_out[me]

    for load in loads[8:]:
        load.wait()

    l_lane = iota((8, PIECE_COLS), 1)
    piece = jnp.zeros((8, PIECE_COLS), jnp.int32)
    for h in range(1, PIECES):
        piece = piece + (l_lane >= h * ROWS).astype(jnp.int32)
    l_term = l_lane - piece * ROWS
    l_imag = (l_term >= TERMS).astype(jnp.int32)
    l_odd = (l_term - l_imag * TERMS >= HALF).astype(jnp.int32)
    l_quarter = ((l_imag - l_odd) << 14)[0:1]
    l_place = (piece * (16 * Y) + 4088)[0:1]

    def l_facet(f, carry):
        off = facet_off[f]
        r = iota((S, PIECE_COLS), 0)
        real, imag = unit(l_quarter - r * (16 * off + l_place))
        q = q_tab[...]
        right = jnp.concatenate([q * real, q * imag], axis=0)
        row = iota((2 * S, 2 * S), 0)
        lane = iota((2 * S, 2 * S), 1)
        left, _ = unit(
            (row & (S - 1)) * (off + 1024 * (lane & (S - 1))) + (((lane >> 6) - (row >> 6)) << 14)
        )
        made = jnp.dot(left, right, precision=lax.Precision.HIGHEST, preferred_element_type=F32)
        l_tab[:, pl.ds(pl.multiple_of(f * PIECE_COLS, X), PIECE_COLS)] = made.astype(BF16)
        return carry

    lax.fori_loop(0, 4, l_facet, 0)
    def a_wait(i, carry):
        a_arrival(far_first(i)).wait_recv()
        return carry

    lax.fori_loop(0, K - 1, a_wait, 0)
    made = jnp.dot(l_tab[...], part_in[...].reshape(K * ROWS, X), preferred_element_type=F32)
    asm[0, 0] = jnp.concatenate([made[:S], made[S:]], axis=1).astype(BF16)

    def c_copy(src, dst, half, send, there):
        return pltpu.make_async_remote_copy(
            src_ref=asm.at[src, 0],
            dst_ref=asm.at[dst, half],
            send_sem=c_send.at[send],
            recv_sem=c_recv.at[dst, half],
            device_id=(me, there),
            device_id_type=MESH,
        )

    def chip(step):
        return 2 * ((z + step) & 3)

    c_copies = [
        c_copy(0, 3, 0, 6, chip(2) + core),
        c_copy(0, 3, 1, 7, chip(2) + sibling),
        c_copy(0, 0, 1, 0, chip(0) + sibling),
        c_copy(0, 2, 0, 2, chip(1) + core),
        c_copy(0, 1, 0, 3, chip(3) + core),
    ]
    for copy in c_copies:
        copy.start()

    for load in loads[4:8]:
        load.wait()
    frequency = sub_u[col]

    def w_block(b, carry):
        for h in range(2):
            x = iota((X // 2, X), 0) + h * (X // 2)
            u = iota((X // 2, X), 1) + b * X
            real, imag = unit(0 - 64 * x * (frequency + u))
            top = slice(h * (X // 2), (h + 1) * (X // 2))
            low = slice(X + h * (X // 2), X + (h + 1) * (X // 2))
            w_tab[b, top, :X] = real.astype(BF16)
            w_tab[b, top, X:] = imag.astype(BF16)
            w_tab[b, low, :X] = (-imag).astype(BF16)
            w_tab[b, low, X:] = real.astype(BF16)
        return carry

    lax.fori_loop(0, UB, w_block, 0)

    strip = jnp.zeros((C, X), jnp.int32)
    for at, step in enumerate(PLACES):
        for c in range(2):
            strip = jnp.where(
                iota((C, X), 0) == 2 * at + c, strip_off[2 * ((z + step) & 3) + (core ^ c)], strip
            )

    def d_block(b, carry):
        real, imag = unit(0 - strip * (frequency + iota((C, X), 1) + b * X))
        d_tab[b, :, :X] = real
        d_tab[b, :, X:] = imag
        return carry

    lax.fori_loop(0, UB, d_block, 0)

    pair_lane = iota((8, 2 * X), 1) >> 1

    def weight_lane(i, total):
        return jnp.where(pair_lane == i, row_weight[i & 7, i >> 3], total)

    weight_row = lax.fori_loop(0, BLOCKS * 8, weight_lane, jnp.zeros((8, 2 * X), F32))
    band_row = jnp.zeros((8, 2 * X), jnp.int32)
    for b in range(BLOCKS):
        band_row = jnp.where((pair_lane >> 3) == b, band[0, b], band_row)
    row = iota((2 * S, 2 * X), 0)
    lane = iota((2 * S, 2 * X), 1)
    covers = (
        (band_row[0:1] == ((row & (S - 1)) >> 3))
        & (((lane >> 1) & 7) == (row & 7))
        & ((lane & 1) == (row >> 6))
    )
    spread = jnp.where(covers, jnp.broadcast_to(weight_row[0:1], (2 * S, 2 * X)), 0.0)
    weight[...] = jnp.broadcast_to(jnp.sum(spread[:S], axis=1, keepdims=True), (S, X)) * (
        1.0 / 32.0
    )
    high = spread.astype(BF16)
    both = jnp.concatenate([high, (spread - high.astype(F32)).astype(BF16)], axis=0)

    def base_block(b, carry):
        vis_load(b).wait()
        made = jnp.dot(both, vis.at[b].reshape(2 * X, X)[...], preferred_element_type=F32)
        real = made[:S] + made[2 * S : 3 * S]
        imag = made[S : 2 * S] + made[3 * S :]
        cos, sin = cos_sin(screen[:, pl.ds(pl.multiple_of(b * X, X), X)])
        base[b, :, :X] = real * cos + imag * sin
        base[b, :, X:] = imag * cos - real * sin
        return carry

    lax.fori_loop(0, UB, base_block, 0)

    def turn_table(f, carry):
        lt_tab[f] = l_tab[:, pl.ds(pl.multiple_of(f * PIECE_COLS, X), PIECE_COLS)].T
        return carry

    lax.fori_loop(0, 4, turn_table, 0)

    def c_wait(at, half):
        c_copy(at, at, half, 0, chip(0) + sibling).wait_recv()

    def grid_part(low, count):
        def grid_block(b, carry):
            made = jnp.dot(
                asm[low : low + count].reshape(count * 2 * S, 2 * X),
                w_tab[b],
                preferred_element_type=F32,
            )
            real = jnp.zeros((S, X), F32)
            imag = jnp.zeros((S, X), F32)
            for c in range(2 * count):
                dr = d_tab[b, 2 * low + c : 2 * low + c + 1, :X]
                di = d_tab[b, 2 * low + c : 2 * low + c + 1, X:]
                pr = made[c * S : (c + 1) * S, :X]
                pi = made[c * S : (c + 1) * S, X:]
                real = real + (pr * dr - pi * di)
                imag = imag + (pr * di + pi * dr)
            base[b, :, :X] -= weight[...] * real
            base[b, :, X:] -= weight[...] * imag
            return carry

        lax.fori_loop(0, UB, grid_block, 0, unroll=4)

    c_wait(0, 1)
    grid_part(0, 1)
    for at in (1, 2):
        c_wait(at, 0)
        forward = c_copy(at, at, 1, 3 + at, chip(0) + sibling)
        forward.start()
        c_copies.append(forward)
    c_wait(1, 1)
    c_wait(2, 1)
    grid_part(1, 2)
    c_wait(3, 0)
    c_wait(3, 1)
    grid_part(3, 1)

    def share_part(low, high):
        rows = slice(low * S, high * S)
        share_acc[rows, :] = jnp.zeros(((high - low) * S, 2 * X), F32)

        def share_block(b, carry):
            real = base[b, :, :X]
            imag = base[b, :, X:]
            turned = []
            for c in range(low, high):
                dr = d_tab[b, c : c + 1, :X]
                di = d_tab[b, c : c + 1, X:]
                turned.append(
                    jnp.concatenate(
                        [
                            (real * dr + imag * di).astype(BF16),
                            (imag * dr - real * di).astype(BF16),
                        ],
                        axis=1,
                    )
                )
            share_acc[rows, :] += lax.dot_general(
                jnp.concatenate(turned, axis=0),
                w_tab[b],
                (((1,), (1,)), ((), ())),
                preferred_element_type=F32,
            )
            return carry

        lax.fori_loop(0, UB, share_block, 0, unroll=8 if high - low < 3 else 4)

    def pair_copy(at):
        return pltpu.make_async_remote_copy(
            src_ref=pair_out.at[at],
            dst_ref=pair_in.at[at],
            send_sem=pair_send.at[at],
            recv_sem=pair_recv.at[at],
            device_id=(me, 2 * z + sibling),
            device_id_type=MESH,
        )

    def pair_start(at):
        pair_out[at] = share_acc[(2 * at + 1) * S : (2 * at + 2) * S, :].astype(BF16)
        pair_copy(at).start()

    def strip_total(at):
        pair_copy(at).wait_recv()
        return share_acc[2 * at * S : (2 * at + 1) * S, :] + pair_in[at].astype(F32)

    def e_copy(at):
        return pltpu.make_async_remote_copy(
            src_ref=share_out.at[at],
            dst_ref=share_in.at[PLACES.index((4 - PLACES[at]) % 4)],
            send_sem=e_send.at[at],
            recv_sem=e_recv.at[PLACES.index((4 - PLACES[at]) % 4)],
            device_id=(me, chip(PLACES[at]) + core),
            device_id_type=MESH,
        )

    def e_arrival(at):
        return pltpu.make_async_remote_copy(
            src_ref=share_out.at[at],
            dst_ref=share_in.at[at],
            send_sem=e_send.at[at],
            recv_sem=e_recv.at[at],
            device_id=(me, chip(PLACES[at]) + core),
            device_id_type=MESH,
        )

    def e_start(at):
        share_out[at] = strip_total(at).astype(BF16)
        e_copy(at).start()

    share_part(7, 8)
    pair_start(3)
    share_part(2, 7)
    pair_start(1)
    pair_start(2)
    e_start(3)
    share_part(0, 2)
    pair_start(0)
    e_start(1)
    e_start(2)
    total = strip_total(0)

    row = iota((2 * S, 2 * S), 0)
    lane = iota((2 * S, 2 * S), 1)
    weave = ((row >> 1) == (lane & (S - 1))) & ((row & 1) == (lane >> 6))
    weave = jnp.where(weave, 1.0, 0.0).astype(BF16)

    def rest_store(b):
        lanes = pl.ds(pl.multiple_of(b * X, X), X)
        return pltpu.make_async_copy(rest_out.at[b], residual.at[:, :, lanes], rest_sem.at[b])

    def rest_block(b, carry):
        woven = jnp.dot(
            weave,
            jnp.concatenate([base[b, :, :X], base[b, :, X:]], axis=0).astype(BF16),
            preferred_element_type=F32,
        )
        rest_out.at[b].reshape(2 * S, X)[...] = woven.astype(BF16)
        rest_store(b).start()
        return carry

    lax.fori_loop(0, UB, rest_block, 0, unroll=4)

    for at in (1, 2, 3):
        e_arrival(at).wait_recv()
        total = total + share_in[at].astype(F32)
    share = jnp.concatenate([total[:, :X], total[:, X:]], axis=0).astype(BF16)

    def f_copy(p):
        there = facet_step(me, p)
        return pltpu.make_async_remote_copy(
            src_ref=back_out.at[there, :SENT],
            dst_ref=back.at[me, :SENT],
            send_sem=f_send.at[p],
            recv_sem=f_recv.at[me],
            device_id=(there, col),
            device_id_type=MESH,
        )

    def f_arrival(p):
        source = facet_step(me, back_step(p))
        return pltpu.make_async_remote_copy(
            src_ref=back_out.at[source, :SENT],
            dst_ref=back.at[source, :SENT],
            send_sem=f_send.at[p],
            recv_sem=f_recv.at[source],
            device_id=(source, col),
            device_id_type=MESH,
        )

    def back_group(a, carry):
        facet = ((me >> 3) + (far_first(a * 8) >> 3)) & 3
        made = jnp.dot(lt_tab[facet], share, preferred_element_type=F32)
        back_out[pl.ds(facet * 8, 8)] = made.astype(BF16).reshape(8, ROWS, X)

        def f_start(i, inner):
            f_copy(far_first(a * 8 + i)).start()
            return inner

        lax.fori_loop(0, 7 if a == 3 else 8, f_start, 0)
        return carry

    for a in range(4):
        back_group(a, 0)
    back[me] = back_out[me]

    def image_group(i, carry):
        start = (((me >> 3) - (far_first(i * 8) >> 3)) & 3) * 8

        def f_wait(j, inner):
            f_arrival(far_first(i * 8 + j)).wait_recv()
            return inner

        lax.fori_loop(0, 7 if i == 3 else 8, f_wait, 0)
        made = lax.dot_general(
            back[pl.ds(start, 8)].reshape(8 * ROWS, X),
            n_tab[pl.ds(start, 8)].reshape(8 * ROWS, 2 * Y),
            (((0,), (0,)), ((), ())),
            preferred_element_type=F32,
        )
        back_acc[...] = made if i == 0 else back_acc[...] + made
        return carry

    for i in range(4):
        image_group(i, 0)
    image[...] = (back_acc[...].T * (1.0 / 32.0)).astype(BF16)

    def sent(p, carry):
        a_copy(p).wait_send()
        f_copy(p).wait_send()
        return carry

    lax.fori_loop(1, K, sent, 0)
    for copy in c_copies:
        copy.wait_send()
    for at in range(4):
        pair_copy(at).wait_send()
    for at in (1, 2, 3):
        e_copy(at).wait_send()

    def stored(b, carry):
        rest_store(b).wait()
        return carry

    lax.fori_loop(0, UB, stored, 0)


def store(residual, image, residual_out, image_out, sem):
    copies = [
        pltpu.make_async_copy(residual, residual_out, sem.at[0]),
        pltpu.make_async_copy(image, image_out, sem.at[1]),
    ]
    for copy in copies:
        copy.start()
    for copy in copies:
        copy.wait()


def shards(
    facet_strips,
    facet_off,
    strip_off,
    sub_v,
    sub_u,
    screen_phase,
    visibilities,
    block_band,
    vis_weight,
):
    vmem = pl.BlockSpec(memory_space=pltpu.VMEM)
    anywhere = pl.BlockSpec(memory_space=pl.ANY)
    dma = pltpu.SemaphoreType.DMA
    q, b = piece_factors()
    residual, image = pl.pallas_call(
        kernel,
        name="imaging_round",
        out_shape=(
            jax.ShapeDtypeStruct((S, 2, U), BF16),
            jax.ShapeDtypeStruct((2 * Y, X), BF16),
        ),
        in_specs=[pl.BlockSpec(memory_space=pltpu.HBM)] * 11,
        out_specs=(anywhere, vmem),
        scratch_shapes=[
            pltpu.SMEM((4,), jnp.int32),
            pltpu.SMEM((C,), jnp.int32),
            pltpu.SMEM((K,), jnp.int32),
            pltpu.SMEM((C,), jnp.int32),
            pltpu.SMEM((1, BLOCKS), jnp.int32),
            pltpu.SMEM((8, BLOCKS), F32),
            pltpu.VMEM((2 * Y, X), BF16),
            pltpu.VMEM((SENT, 2 * Y), F32),
            pltpu.VMEM((S, PIECE_COLS), F32),
            pltpu.VMEM((S, U), F32),
            pltpu.VMEM((UB, BLOCKS * 8, 2, X), BF16),
            pltpu.VMEM((K // 4, 4, 4 * Y), F32),
            pltpu.VMEM((K, ROWS, 2 * Y), BF16),
            pltpu.VMEM((K, ROWS, X), BF16),
            pltpu.VMEM((K, ROWS, X), BF16),
            pltpu.VMEM((2 * S, K * ROWS), BF16),
            pltpu.VMEM((4, PIECE_COLS, 2 * S), BF16),
            pltpu.VMEM((4, 2, S, 2 * X), BF16),
            pltpu.VMEM((UB, 2 * X, 2 * X), BF16),
            pltpu.VMEM((UB, C, 2 * X), F32),
            pltpu.VMEM((UB, S, 2 * X), F32),
            pltpu.VMEM((S, X), F32),
            pltpu.VMEM((UB, S, 2, X), BF16),
            pltpu.VMEM((C * S, 2 * X), F32),
            pltpu.VMEM((4, S, 2 * X), BF16),
            pltpu.VMEM((4, S, 2 * X), BF16),
            pltpu.VMEM((4, S, 2 * X), BF16),
            pltpu.VMEM((4, S, 2 * X), BF16),
            pltpu.VMEM((K, ROWS, X), BF16),
            pltpu.VMEM((K, ROWS, X), BF16),
            pltpu.VMEM((X, 2 * Y), F32),
            dma((10,)),
            dma((UB,)),
            dma((UB,)),
            dma((K,)),
            dma((K,)),
            dma((8,)),
            dma((4, 2)),
            dma((4,)),
            dma((4,)),
            dma((4,)),
            dma((4,)),
            dma((K,)),
            dma((K,)),
        ],
        compiler_params=pltpu.CompilerParams(
            collective_id=0, has_side_effects=True, vmem_limit_bytes=48 * 1024 * 1024
        ),
    )(
        *(
            pltpu.with_memory_space_constraint(array, pltpu.HBM)
            for array in (
                facet_off,
                strip_off,
                sub_v,
                sub_u,
                facet_strips.reshape(2 * Y, X),
                jnp.asarray(b),
                jnp.asarray(q),
                block_band.T,
                vis_weight.T,
                screen_phase,
                visibilities.reshape(BLOCKS * 8, 2, U),
            )
        )
    )
    hbm = pl.BlockSpec(memory_space=pltpu.HBM)
    residual, image = pl.pallas_call(
        store,
        name="store",
        out_shape=(
            jax.ShapeDtypeStruct((S, 2, U), BF16),
            jax.ShapeDtypeStruct((2 * Y, X), BF16),
        ),
        in_specs=[anywhere, anywhere],
        out_specs=(hbm, hbm),
        scratch_shapes=[dma((2,))],
    )(
        pltpu.with_memory_space_constraint(residual, pltpu.VMEM),
        pltpu.with_memory_space_constraint(image, pltpu.VMEM),
    )
    return residual, image.reshape(Y, 2, X)


def solution(mesh):
    return jax.shard_map(
        shards,
        mesh=mesh,
        in_specs=(
            P("facet", None, "col"),
            P(),
            P(),
            P(),
            P(),
            P("facet", "col"),
            P("facet", None, None, "col"),
            P("facet", "col"),
            P("facet", "col"),
        ),
        out_specs=(P("facet", None, "col"), P("facet", None, "col")),
        check_vma=False,
    )
```

```python
import math

import jax
import jax.numpy as jnp
from jax import lax
from jax.experimental import pallas as pl
from jax.experimental.pallas import tpu as pltpu
import numpy as np
from jax.sharding import PartitionSpec as P

MESH = pl.DeviceIdType.MESH
IMG = 65536
TURN = 2.0 * math.pi / IMG
F32 = jnp.float32
BF16 = jnp.bfloat16

K = 32
C = 8
S = 64
Y = 512
X = 128
U = 1024
PIECES = 8
UB = U // X
BLOCKS = 16
PLACES = (0, 1, 3, 2)
HALF = 10
TERMS = 2 * HALF
SENT = 2 * TERMS
ROWS = 48
PIECE_COLS = PIECES * ROWS


def piece_factors():
    r = np.arange(S) - (S - 1) / 2
    d = np.arange(Y) - (Y - 1) / 2
    angle = 2.0 * np.pi * np.outer(r, d) / (PIECES * Y)
    left = []
    right = []
    for part in (np.cos(angle), np.sin(angle)):
        u, sigma, v = np.linalg.svd(part, full_matrices=False)
        left.append(u[:, :HALF] * sigma[:HALF])
        right.append(v[:HALF])
    q = np.concatenate(left, axis=1) / 1024.0
    b = np.concatenate(right, axis=0)
    q = np.pad(np.tile(q, (1, 2)), ((0, 0), (0, ROWS - SENT)))
    b = np.tile(np.repeat(b, 2, axis=1), (2, 1))
    return np.tile(q, (1, PIECES)).astype(np.float32), b.astype(np.float32)


def quarter_turns(q, t):
    t2 = t * t
    sin = t + t * t2 * (-1.6666654611e-1 + t2 * (8.3321608736e-3 + t2 * -1.9515295891e-4))
    cos = 1.0 - 0.5 * t2 + t2 * t2 * (
        4.166664568298827e-2 + t2 * (-1.388731625493765e-3 + t2 * 2.443315711809948e-5)
    )
    odd = (q & 1) == 1
    even_cos = jnp.where(odd, sin, cos)
    even_sin = jnp.where(odd, cos, sin)
    return (
        jnp.where(((q + 1) & 2) != 0, -even_cos, even_cos),
        jnp.where((q & 2) != 0, -even_sin, even_sin),
    )


def unit(k):
    k = k & (IMG - 1)
    q = (k + IMG // 8) >> 14
    return quarter_turns(q, (k - (q << 14)).astype(F32) * TURN)


def cos_sin(angle):
    turns = jnp.floor(angle * (2.0 / math.pi) + 0.5)
    t = (angle - turns * 1.5703125) - turns * 4.837512969970703e-4
    t = t - turns * 7.549789948768648e-8
    return quarter_turns(turns.astype(jnp.int32), t)


def iota(shape, dim):
    return lax.broadcasted_iota(jnp.int32, shape, dim)


def facet_step(me, p):
    x = ((me >> 3) + (p >> 3)) & 3
    z = ((me >> 2) ^ (p >> 2)) & 1
    y = (me + p) & 3
    return (x << 3) | (z << 2) | y


def back_step(p):
    x = (0 - (p >> 3)) & 3
    y = (0 - p) & 3
    return (x << 3) | (p & 4) | y


def far_first(i):
    a = i >> 3
    b = i & 3
    return ((2 ^ a ^ (a >> 1)) << 3) | (4 - (i & 4)) | (2 ^ b ^ (b >> 1))


def kernel(
    facet_off_hbm,
    strip_off_hbm,
    sub_v_hbm,
    sub_u_hbm,
    strips_hbm,
    b_hbm,
    q_hbm,
    band_hbm,
    weight_hbm,
    screen_hbm,
    vis_hbm,
    residual,
    image,
    facet_off,
    strip_off,
    sub_v,
    sub_u,
    band,
    row_weight,
    strips,
    b_tab,
    q_tab,
    screen,
    vis,
    mod,
    n_tab,
    part_out,
    part_in,
    l_tab,
    lt_tab,
    asm,
    w_tab,
    d_tab,
    base,
    weight,
    rest_out,
    share_acc,
    pair_out,
    pair_in,
    share_out,
    share_in,
    back_out,
    back,
    back_acc,
    load_sem,
    vis_sem,
    rest_sem,
    a_send,
    a_recv,
    c_send,
    c_recv,
    pair_send,
    pair_recv,
    e_send,
    e_recv,
    f_send,
    f_recv,
):
    me = lax.axis_index("facet")
    col = lax.axis_index("col")
    z = col >> 1
    core = col & 1
    sibling = 1 - core

    loads = [
        pltpu.make_async_copy(src, dst, load_sem.at[i])
        for i, (src, dst) in enumerate(
            [
                (facet_off_hbm, facet_off),
                (sub_v_hbm, sub_v),
                (b_hbm, b_tab),
                (strips_hbm, strips),
                (strip_off_hbm, strip_off),
                (sub_u_hbm, sub_u),
                (band_hbm, band),
                (weight_hbm, row_weight),
                (q_hbm, q_tab),
                (screen_hbm, screen),
            ]
        )
    ]
    for load in loads[:4]:
        load.start()
    pad = slice(32, ROWS)
    part_in[:, pad] = jnp.zeros((K, ROWS - 32, X), BF16)
    back[:, pad] = jnp.zeros((K, ROWS - 32, X), BF16)
    barrier = pltpu.get_barrier_semaphore()

    def greet_facet(i, carry):
        pl.semaphore_signal(
            barrier, inc=1, device_id=(facet_step(me, far_first(i)), col), device_id_type=MESH
        )
        return carry

    lax.fori_loop(0, K - 1, greet_facet, 0)
    for step in (2, 1, 3, 0):
        for half in (0, 1)[step == 0 :]:
            pl.semaphore_signal(
                barrier,
                inc=1,
                device_id=(me, 2 * ((z + step) & 3) + (core ^ half)),
                device_id_type=MESH,
            )
    for load in loads[4:]:
        load.start()

    def vis_load(b):
        lanes = pl.ds(pl.multiple_of(b * X, X), X)
        return pltpu.make_async_copy(vis_hbm.at[:, :, lanes], vis.at[b], vis_sem.at[b])

    def vis_start(b, carry):
        vis_load(b).start()
        return carry

    lax.fori_loop(0, UB, vis_start, 0)

    for load in loads[:4]:
        load.wait()
    first = facet_off[me // PIECES] + (me % PIECES) * Y

    def mod_rows(i, carry):
        row = iota((8, X), 0)
        v = jnp.zeros((8, X), jnp.int32)
        for r in range(8):
            v = jnp.where(row == r, sub_v[i * 8 + r], v)
        for h in range(2 * Y // X):
            lane = iota((8, X), 1) + h * X
            y = lane >> 1
            real, imag = unit(128772 - 504 * y - v * (first + y) + ((lane & 1) << 14))
            for g in range(2):
                mod[i * 2 + g, :, h * X : (h + 1) * X] = real[g * 4 : g * 4 + 4]
                mod[i * 2 + g, :, 2 * Y + h * X : 2 * Y + (h + 1) * X] = imag[g * 4 : g * 4 + 4]
        return carry

    lax.fori_loop(0, K // 8, mod_rows, 0, unroll=2)

    is_real = iota((SENT, X), 0) < TERMS
    padding = jnp.zeros((ROWS - SENT, X), F32)

    def facet_group(g, carry):
        for h in range(2 * Y // X):
            lanes = slice(h * X, (h + 1) * X)
            upper = slice(2 * Y + h * X, 2 * Y + (h + 1) * X)
            b = b_tab[:, lanes]
            for i in range(4):
                turn = jnp.where(is_real, mod[g, i : i + 1, lanes], mod[g, i : i + 1, upper])
                n_tab[g * 4 + i, :, lanes] = jnp.concatenate([b * turn, padding], axis=0).astype(BF16)
        made = jnp.dot(
            n_tab[pl.ds(g * 4, 4)].reshape(4 * ROWS, 2 * Y),
            strips[...],
            preferred_element_type=F32,
        )
        part_out[pl.ds(g * 4, 4)] = made.astype(BF16).reshape(4, ROWS, X)
        return carry

    lax.fori_loop(0, K // 4, facet_group, 0, unroll=4)
    pl.semaphore_wait(barrier, K - 1 + C - 1)

    def a_copy(p):
        there = facet_step(me, p)
        return pltpu.make_async_remote_copy(
            src_ref=part_out.at[there, :SENT],
            dst_ref=part_in.at[me, :SENT],
            send_sem=a_send.at[p],
            recv_sem=a_recv.at[me],
            device_id=(there, col),
            device_id_type=MESH,
        )

    def a_arrival(p):
        source = facet_step(me, back_step(p))
        return pltpu.make_async_remote_copy(
            src_ref=part_out.at[source, :SENT],
            dst_ref=part_in.at[source, :SENT],
            send_sem=a_send.at[p],
            recv_sem=a_recv.at[source],
            device_id=(source, col),
            device_id_type=MESH,
        )

    def a_start(i, carry):
        a_copy(far_first(i)).start()
        return carry

    lax.fori_loop(0, K - 1, a_start, 0)
    part_in[me] = part_out[me]

    for load in loads[8:]:
        load.wait()

    l_lane = iota((8, PIECE_COLS), 1)
    piece = jnp.zeros((8, PIECE_COLS), jnp.int32)
    for h in range(1, PIECES):
        piece = piece + (l_lane >= h * ROWS).astype(jnp.int32)
    l_term = l_lane - piece * ROWS
    l_imag = (l_term >= TERMS).astype(jnp.int32)
    l_odd = (l_term - l_imag * TERMS >= HALF).astype(jnp.int32)
    l_quarter = ((l_imag - l_odd) << 14)[0:1]
    l_place = (piece * (16 * Y) + 4088)[0:1]

    def l_facet(f, carry):
        off = facet_off[f]
        r = iota((S, PIECE_COLS), 0)
        real, imag = unit(l_quarter - r * (16 * off + l_place))
        q = q_tab[...]
        right = jnp.concatenate([q * real, q * imag], axis=0)
        row = iota((2 * S, 2 * S), 0)
        lane = iota((2 * S, 2 * S), 1)
        left, _ = unit(
            (row & (S - 1)) * (off + 1024 * (lane & (S - 1))) + (((lane >> 6) - (row >> 6)) << 14)
        )
        made = jnp.dot(left, right, precision=lax.Precision.HIGHEST, preferred_element_type=F32)
        l_tab[:, pl.ds(pl.multiple_of(f * PIECE_COLS, X), PIECE_COLS)] = made.astype(BF16)
        return carry

    lax.fori_loop(0, 4, l_facet, 0, unroll=2)
    def a_wait(i, carry):
        a_arrival(far_first(i)).wait_recv()
        return carry

    lax.fori_loop(0, K - 1, a_wait, 0)
    made = jnp.dot(l_tab[...], part_in[...].reshape(K * ROWS, X), preferred_element_type=F32)
    asm[0, 0] = jnp.concatenate([made[:S], made[S:]], axis=1).astype(BF16)

    def c_copy(src, dst, half, send, there):
        return pltpu.make_async_remote_copy(
            src_ref=asm.at[src, 0],
            dst_ref=asm.at[dst, half],
            send_sem=c_send.at[send],
            recv_sem=c_recv.at[dst, half],
            device_id=(me, there),
            device_id_type=MESH,
        )

    def chip(step):
        return 2 * ((z + step) & 3)

    c_copies = [
        c_copy(0, 3, 0, 6, chip(2) + core),
        c_copy(0, 3, 1, 7, chip(2) + sibling),
        c_copy(0, 0, 1, 0, chip(0) + sibling),
        c_copy(0, 2, 0, 2, chip(1) + core),
        c_copy(0, 1, 0, 3, chip(3) + core),
    ]
    for copy in c_copies:
        copy.start()

    for load in loads[4:8]:
        load.wait()
    frequency = sub_u[col]

    def w_block(b, carry):
        for h in range(2):
            x = iota((X // 2, X), 0) + h * (X // 2)
            u = iota((X // 2, X), 1) + b * X
            real, imag = unit(0 - 64 * x * (frequency + u))
            top = slice(h * (X // 2), (h + 1) * (X // 2))
            low = slice(X + h * (X // 2), X + (h + 1) * (X // 2))
            w_tab[b, top, :X] = real.astype(BF16)
            w_tab[b, top, X:] = imag.astype(BF16)
            w_tab[b, low, :X] = (-imag).astype(BF16)
            w_tab[b, low, X:] = real.astype(BF16)
        return carry

    lax.fori_loop(0, UB, w_block, 0)

    strip = jnp.zeros((C, X), jnp.int32)
    for at, step in enumerate(PLACES):
        for c in range(2):
            strip = jnp.where(
                iota((C, X), 0) == 2 * at + c, strip_off[2 * ((z + step) & 3) + (core ^ c)], strip
            )

    def d_block(b, carry):
        real, imag = unit(0 - strip * (frequency + iota((C, X), 1) + b * X))
        d_tab[b, :, :X] = real
        d_tab[b, :, X:] = imag
        return carry

    lax.fori_loop(0, UB, d_block, 0)

    pair_lane = iota((8, 2 * X), 1) >> 1

    def weight_lane(i, total):
        return jnp.where(pair_lane == i, row_weight[i & 7, i >> 3], total)

    weight_row = lax.fori_loop(0, BLOCKS * 8, weight_lane, jnp.zeros((8, 2 * X), F32))
    band_row = jnp.zeros((8, 2 * X), jnp.int32)
    for b in range(BLOCKS):
        band_row = jnp.where((pair_lane >> 3) == b, band[0, b], band_row)
    row = iota((2 * S, 2 * X), 0)
    lane = iota((2 * S, 2 * X), 1)
    covers = (
        (band_row[0:1] == ((row & (S - 1)) >> 3))
        & (((lane >> 1) & 7) == (row & 7))
        & ((lane & 1) == (row >> 6))
    )
    spread = jnp.where(covers, jnp.broadcast_to(weight_row[0:1], (2 * S, 2 * X)), 0.0)
    weight[...] = jnp.broadcast_to(jnp.sum(spread[:S], axis=1, keepdims=True), (S, X)) * (
        1.0 / 32.0
    )
    high = spread.astype(BF16)
    both = jnp.concatenate([high, (spread - high.astype(F32)).astype(BF16)], axis=0)

    def base_block(b, carry):
        vis_load(b).wait()
        made = jnp.dot(both, vis.at[b].reshape(2 * X, X)[...], preferred_element_type=F32)
        real = made[:S] + made[2 * S : 3 * S]
        imag = made[S : 2 * S] + made[3 * S :]
        cos, sin = cos_sin(screen[:, pl.ds(pl.multiple_of(b * X, X), X)])
        base[b, :, :X] = real * cos + imag * sin
        base[b, :, X:] = imag * cos - real * sin
        return carry

    lax.fori_loop(0, UB, base_block, 0, unroll=2)

    def turn_table(f, carry):
        lt_tab[f] = l_tab[:, pl.ds(pl.multiple_of(f * PIECE_COLS, X), PIECE_COLS)].T
        return carry

    lax.fori_loop(0, 4, turn_table, 0)

    def c_wait(at, half):
        c_copy(at, at, half, 0, chip(0) + sibling).wait_recv()

    def grid_part(low, count):
        def grid_block(b, carry):
            made = jnp.dot(
                asm[low : low + count].reshape(count * 2 * S, 2 * X),
                w_tab[b],
                preferred_element_type=F32,
            )
            real = jnp.zeros((S, X), F32)
            imag = jnp.zeros((S, X), F32)
            for c in range(2 * count):
                dr = d_tab[b, 2 * low + c : 2 * low + c + 1, :X]
                di = d_tab[b, 2 * low + c : 2 * low + c + 1, X:]
                pr = made[c * S : (c + 1) * S, :X]
                pi = made[c * S : (c + 1) * S, X:]
                real = real + (pr * dr - pi * di)
                imag = imag + (pr * di + pi * dr)
            base[b, :, :X] -= weight[...] * real
            base[b, :, X:] -= weight[...] * imag
            return carry

        lax.fori_loop(0, UB, grid_block, 0, unroll=4)

    c_wait(0, 1)
    grid_part(0, 1)
    for at in (1, 2):
        c_wait(at, 0)
        forward = c_copy(at, at, 1, 3 + at, chip(0) + sibling)
        forward.start()
        c_copies.append(forward)
    c_wait(1, 1)
    c_wait(2, 1)
    grid_part(1, 2)
    c_wait(3, 0)
    c_wait(3, 1)
    grid_part(3, 1)

    def share_part(low, high):
        rows = slice(low * S, high * S)
        share_acc[rows, :] = jnp.zeros(((high - low) * S, 2 * X), F32)

        def share_block(b, carry):
            real = base[b, :, :X]
            imag = base[b, :, X:]
            turned = []
            for c in range(low, high):
                dr = d_tab[b, c : c + 1, :X]
                di = d_tab[b, c : c + 1, X:]
                turned.append(
                    jnp.concatenate(
                        [
                            (real * dr + imag * di).astype(BF16),
                            (imag * dr - real * di).astype(BF16),
                        ],
                        axis=1,
                    )
                )
            share_acc[rows, :] += lax.dot_general(
                jnp.concatenate(turned, axis=0),
                w_tab[b],
                (((1,), (1,)), ((), ())),
                preferred_element_type=F32,
            )
            return carry

        lax.fori_loop(0, UB, share_block, 0, unroll=8 if high - low < 3 else 4)

    def pair_copy(at):
        return pltpu.make_async_remote_copy(
            src_ref=pair_out.at[at],
            dst_ref=pair_in.at[at],
            send_sem=pair_send.at[at],
            recv_sem=pair_recv.at[at],
            device_id=(me, 2 * z + sibling),
            device_id_type=MESH,
        )

    def pair_start(at):
        pair_out[at] = share_acc[(2 * at + 1) * S : (2 * at + 2) * S, :].astype(BF16)
        pair_copy(at).start()

    def strip_total(at):
        pair_copy(at).wait_recv()
        return share_acc[2 * at * S : (2 * at + 1) * S, :] + pair_in[at].astype(F32)

    def e_copy(at):
        return pltpu.make_async_remote_copy(
            src_ref=share_out.at[at],
            dst_ref=share_in.at[PLACES.index((4 - PLACES[at]) % 4)],
            send_sem=e_send.at[at],
            recv_sem=e_recv.at[PLACES.index((4 - PLACES[at]) % 4)],
            device_id=(me, chip(PLACES[at]) + core),
            device_id_type=MESH,
        )

    def e_arrival(at):
        return pltpu.make_async_remote_copy(
            src_ref=share_out.at[at],
            dst_ref=share_in.at[at],
            send_sem=e_send.at[at],
            recv_sem=e_recv.at[at],
            device_id=(me, chip(PLACES[at]) + core),
            device_id_type=MESH,
        )

    def e_start(at):
        share_out[at] = strip_total(at).astype(BF16)
        e_copy(at).start()

    share_part(7, 8)
    pair_start(3)
    share_part(2, 7)
    pair_start(1)
    pair_start(2)
    e_start(3)
    share_part(0, 2)
    pair_start(0)
    e_start(1)
    e_start(2)
    total = strip_total(0)

    row = iota((2 * S, 2 * S), 0)
    lane = iota((2 * S, 2 * S), 1)
    weave = ((row >> 1) == (lane & (S - 1))) & ((row & 1) == (lane >> 6))
    weave = jnp.where(weave, 1.0, 0.0).astype(BF16)

    def rest_store(b):
        lanes = pl.ds(pl.multiple_of(b * X, X), X)
        return pltpu.make_async_copy(rest_out.at[b], residual.at[:, :, lanes], rest_sem.at[b])

    def rest_block(b, carry):
        woven = jnp.dot(
            weave,
            jnp.concatenate([base[b, :, :X], base[b, :, X:]], axis=0).astype(BF16),
            preferred_element_type=F32,
        )
        rest_out.at[b].reshape(2 * S, X)[...] = woven.astype(BF16)
        rest_store(b).start()
        return carry

    lax.fori_loop(0, UB, rest_block, 0, unroll=4)

    for at in (1, 2, 3):
        e_arrival(at).wait_recv()
        total = total + share_in[at].astype(F32)
    share = jnp.concatenate([total[:, :X], total[:, X:]], axis=0).astype(BF16)

    def f_copy(p):
        there = facet_step(me, p)
        return pltpu.make_async_remote_copy(
            src_ref=back_out.at[there, :SENT],
            dst_ref=back.at[me, :SENT],
            send_sem=f_send.at[p],
            recv_sem=f_recv.at[me],
            device_id=(there, col),
            device_id_type=MESH,
        )

    def f_arrival(p):
        source = facet_step(me, back_step(p))
        return pltpu.make_async_remote_copy(
            src_ref=back_out.at[source, :SENT],
            dst_ref=back.at[source, :SENT],
            send_sem=f_send.at[p],
            recv_sem=f_recv.at[source],
            device_id=(source, col),
            device_id_type=MESH,
        )

    def back_group(a, carry):
        facet = ((me >> 3) + (far_first(a * 8) >> 3)) & 3
        made = jnp.dot(lt_tab[facet], share, preferred_element_type=F32)
        back_out[pl.ds(facet * 8, 8)] = made.astype(BF16).reshape(8, ROWS, X)

        def f_start(i, inner):
            f_copy(far_first(a * 8 + i)).start()
            return inner

        lax.fori_loop(0, 7 if a == 3 else 8, f_start, 0)
        return carry

    for a in range(4):
        back_group(a, 0)
    back[me] = back_out[me]

    def image_group(i, carry):
        start = (((me >> 3) - (far_first(i * 8) >> 3)) & 3) * 8

        def f_wait(j, inner):
            f_arrival(far_first(i * 8 + j)).wait_recv()
            return inner

        lax.fori_loop(0, 7 if i == 3 else 8, f_wait, 0)
        made = lax.dot_general(
            back[pl.ds(start, 8)].reshape(8 * ROWS, X),
            n_tab[pl.ds(start, 8)].reshape(8 * ROWS, 2 * Y),
            (((0,), (0,)), ((), ())),
            preferred_element_type=F32,
        )
        back_acc[...] = made if i == 0 else back_acc[...] + made
        return carry

    for i in range(4):
        image_group(i, 0)
    image[...] = (back_acc[...].T * (1.0 / 32.0)).astype(BF16)

    def sent(p, carry):
        a_copy(p).wait_send()
        f_copy(p).wait_send()
        return carry

    lax.fori_loop(1, K, sent, 0)
    for copy in c_copies:
        copy.wait_send()
    for at in range(4):
        pair_copy(at).wait_send()
    for at in (1, 2, 3):
        e_copy(at).wait_send()

    def stored(b, carry):
        rest_store(b).wait()
        return carry

    lax.fori_loop(0, UB, stored, 0)


def store(residual, image, residual_out, image_out, sem):
    copies = [
        pltpu.make_async_copy(residual, residual_out, sem.at[0]),
        pltpu.make_async_copy(image, image_out, sem.at[1]),
    ]
    for copy in copies:
        copy.start()
    for copy in copies:
        copy.wait()


def shards(
    facet_strips,
    facet_off,
    strip_off,
    sub_v,
    sub_u,
    screen_phase,
    visibilities,
    block_band,
    vis_weight,
):
    vmem = pl.BlockSpec(memory_space=pltpu.VMEM)
    anywhere = pl.BlockSpec(memory_space=pl.ANY)
    dma = pltpu.SemaphoreType.DMA
    q, b = piece_factors()
    residual, image = pl.pallas_call(
        kernel,
        name="imaging_round",
        out_shape=(
            jax.ShapeDtypeStruct((S, 2, U), BF16),
            jax.ShapeDtypeStruct((2 * Y, X), BF16),
        ),
        in_specs=[pl.BlockSpec(memory_space=pltpu.HBM)] * 11,
        out_specs=(anywhere, vmem),
        scratch_shapes=[
            pltpu.SMEM((4,), jnp.int32),
            pltpu.SMEM((C,), jnp.int32),
            pltpu.SMEM((K,), jnp.int32),
            pltpu.SMEM((C,), jnp.int32),
            pltpu.SMEM((1, BLOCKS), jnp.int32),
            pltpu.SMEM((8, BLOCKS), F32),
            pltpu.VMEM((2 * Y, X), BF16),
            pltpu.VMEM((SENT, 2 * Y), F32),
            pltpu.VMEM((S, PIECE_COLS), F32),
            pltpu.VMEM((S, U), F32),
            pltpu.VMEM((UB, BLOCKS * 8, 2, X), BF16),
            pltpu.VMEM((K // 4, 4, 4 * Y), F32),
            pltpu.VMEM((K, ROWS, 2 * Y), BF16),
            pltpu.VMEM((K, ROWS, X), BF16),
            pltpu.VMEM((K, ROWS, X), BF16),
            pltpu.VMEM((2 * S, K * ROWS), BF16),
            pltpu.VMEM((4, PIECE_COLS, 2 * S), BF16),
            pltpu.VMEM((4, 2, S, 2 * X), BF16),
            pltpu.VMEM((UB, 2 * X, 2 * X), BF16),
            pltpu.VMEM((UB, C, 2 * X), F32),
            pltpu.VMEM((UB, S, 2 * X), F32),
            pltpu.VMEM((S, X), F32),
            pltpu.VMEM((UB, S, 2, X), BF16),
            pltpu.VMEM((C * S, 2 * X), F32),
            pltpu.VMEM((4, S, 2 * X), BF16),
            pltpu.VMEM((4, S, 2 * X), BF16),
            pltpu.VMEM((4, S, 2 * X), BF16),
            pltpu.VMEM((4, S, 2 * X), BF16),
            pltpu.VMEM((K, ROWS, X), BF16),
            pltpu.VMEM((K, ROWS, X), BF16),
            pltpu.VMEM((X, 2 * Y), F32),
            dma((10,)),
            dma((UB,)),
            dma((UB,)),
            dma((K,)),
            dma((K,)),
            dma((8,)),
            dma((4, 2)),
            dma((4,)),
            dma((4,)),
            dma((4,)),
            dma((4,)),
            dma((K,)),
            dma((K,)),
        ],
        compiler_params=pltpu.CompilerParams(
            collective_id=0, has_side_effects=True, vmem_limit_bytes=48 * 1024 * 1024
        ),
    )(
        *(
            pltpu.with_memory_space_constraint(array, pltpu.HBM)
            for array in (
                facet_off,
                strip_off,
                sub_v,
                sub_u,
                facet_strips.reshape(2 * Y, X),
                jnp.asarray(b),
                jnp.asarray(q),
                block_band.T,
                vis_weight.T,
                screen_phase,
                visibilities.reshape(BLOCKS * 8, 2, U),
            )
        )
    )
    hbm = pl.BlockSpec(memory_space=pltpu.HBM)
    residual, image = pl.pallas_call(
        store,
        name="store",
        out_shape=(
            jax.ShapeDtypeStruct((S, 2, U), BF16),
            jax.ShapeDtypeStruct((2 * Y, X), BF16),
        ),
        in_specs=[anywhere, anywhere],
        out_specs=(hbm, hbm),
        scratch_shapes=[dma((2,))],
    )(
        pltpu.with_memory_space_constraint(residual, pltpu.VMEM),
        pltpu.with_memory_space_constraint(image, pltpu.VMEM),
    )
    return residual, image.reshape(Y, 2, X)


def solution(mesh):
    return jax.shard_map(
        shards,
        mesh=mesh,
        in_specs=(
            P("facet", None, "col"),
            P(),
            P(),
            P(),
            P(),
            P("facet", "col"),
            P("facet", None, None, "col"),
            P("facet", "col"),
            P("facet", "col"),
        ),
        out_specs=(P("facet", None, "col"), P("facet", None, "col")),
        check_vma=False,
    )
```
